32 devices in a mesh: dp: 8 (over z, y), tensor: 4 (over x, core).
Axes of the slice: x: 2, y: 2, z: 4, core: 2. Of those that a mesh axis runs over, the one named last changes fastest.
Arguments:
- hidden_in: bfloat16 [8192, 1024], P(('dp', 'tensor')), may hold values from -6 to 6
- attn_gain: float32 [1024], replicated, may hold values from 0.1 to 1.9
- qkv_weight: bfloat16 [3, 1024, 1024], P(None, 'dp', 'tensor'), may hold values from -0.1875 to 0.1875
- out_weight: bfloat16 [1024, 1024], P('tensor', 'dp'), may hold values from -2 to 2
- mlp_gain: float32 [1024], replicated, may hold values from 0.1 to 1.9
- in_weight: bfloat16 [2, 1024, 2624], P(None, 'dp', 'tensor'), may hold values from -0.1875 to 0.1875
- down_weight: bfloat16 [2624, 1024], P('tensor', 'dp'), may hold values from -0.125 to 0.125
- cotangent: bfloat16 [8192, 1024], P(('dp', 'tensor')), may hold values from -6 to 6
Outputs:
- layer_out: bfloat16 [8192, 1024], P(('dp', 'tensor'))
- input_grad: float32 [8192, 1024], P(('dp', 'tensor'))
- attn_gain_grad: float32 [1024], replicated
- qkv_weight_grad: float32 [3, 1024, 1024], P(None, 'dp', 'tensor')
- out_weight_grad: float32 [1024, 1024], P('tensor', 'dp')
- mlp_gain_grad: float32 [1024], replicated
- in_weight_grad: float32 [2, 1024, 2624], P(None, 'dp', 'tensor')
- down_weight_grad: float32 [2624, 1024], P('tensor', 'dp')
The draws below stay inside these ranges and needn't reach their ends.
All inputs are finite; a program needn't handle non-finite values.
Results may differ from the reference program's by a relative error of at most 0.015.
Values may be sent and summed in bfloat16 or wider, within the bound.
No kernel may reach another device: no remote copies, remote signals or barrier semaphores. Data moves between devices by JAX's collectives and lax.ppermute only.
A program may use at most 128 MiB of HBM per device.

```python
import math
import jax
import jax.numpy as jnp
from jax import lax

D = 1024
HD = 64
FF = 2624
SEQ_LEN = 1024
SEQS = 8
TOKENS = 8192


def with_spikes(drawn, rng, source, target, blocks, factor):
    def block_of(position):
        return (jnp.arange(drawn.shape[position]) // (drawn.shape[position] // blocks)).reshape((-1,) + (1,) * (drawn.ndim - 1 - position))

    near = jax.random.permutation(rng, blocks)[block_of(target)]
    far = (block_of(target) + blocks // 2) % blocks
    return jnp.where((block_of(source) == near) | (block_of(source) == far), factor * drawn, drawn)


def shard_levels(stream_key, shape, split, smallest, largest):
    factor_of, own = 1.0, jax.random.fold_in(stream_key, 6)
    for axis_at, parts in split:
        draws = jnp.exp(jax.random.uniform(jax.random.fold_in(own, axis_at), (parts,), jnp.float32, smallest / len(split), largest / len(split)))
        factor_of = factor_of * jnp.repeat(draws, shape[axis_at] // parts).reshape([-1 if axis == axis_at else 1 for axis in range(len(shape))])
    return factor_of


def noise(stream_key, extent, deviation, reach, split=(), dtype=jnp.bfloat16):
    entries = deviation * jax.random.normal(stream_key, extent, jnp.float32)
    if split:
        entries = entries * shard_levels(stream_key, extent, split, -0.22, 0.18)
    return jnp.clip(entries, -reach, reach).astype(dtype)


def gaussian_with(key, extent, scale, most, cuts, heavy, held_as=jnp.bfloat16):
    drawn = scale * jax.random.normal(key, extent, jnp.float32)
    if cuts:
        drawn = drawn * shard_levels(key, extent, cuts, -0.22, 0.18)
    return jnp.clip(with_spikes(drawn, jax.random.fold_in(key, 3), *heavy), -most, most).astype(held_as)


def setup_inputs(seed: int = 0) -> dict:
    seeds = jax.random.split(jax.random.key(seed), 9)
    hidden_in = gaussian_with(seeds[0], (TOKENS, D), 1.0, 6.0, ((0, 32),), (0, 1, 32, 2.75))
    attn_gain = jnp.clip(1.0 + 0.18 * jax.random.normal(seeds[1], (D,), jnp.float32), 0.1, 1.9)
    qkv_weight = noise(seeds[2], (3, D, D), D ** -0.5, 0.1875, ((1, 8), (2, 4)))
    out_weight = noise(seeds[3], (D, D), (max(1, D * 8 // SEQ_LEN)) ** -0.5, 2.0, ((0, 4), (1, 8)))
    mlp_gain = jnp.clip(1.0 + 0.18 * jax.random.normal(seeds[4], (D,), jnp.float32), 0.1, 1.9)
    in_weight = noise(seeds[5], (2, D, FF), D ** -0.5, 0.1875, ((1, 8), (2, 4)))
    down_weight = noise(seeds[6], (FF, D), FF ** -0.5, 0.125, ((0, 4), (1, 8)))
    cotangent = gaussian_with(seeds[7], (TOKENS, D), 1.0, 6.0, ((0, 32),), (0, 1, 32, 2.75))
    return {"hidden_in": hidden_in, "attn_gain": attn_gain, "qkv_weight": qkv_weight, "out_weight": out_weight, "mlp_gain": mlp_gain, "in_weight": in_weight, "down_weight": down_weight, "cotangent": cotangent}


norm_eps = 1e-05
rope_base = 160000.0
highest = lax.Precision.HIGHEST

@jax.custom_vjp
def low(v):
    return lax.optimization_barrier(v.astype(jnp.bfloat16)).astype(jnp.float32)

@jax.custom_vjp
def low_back(v):
    return v

def low_keep(v):
    return (low(v), None)

def low_pass(kept, grad):
    return (grad,)

def back_keep(v):
    return (v, None)

def back_low(kept, grad):
    return (low(grad),)
low.defvjp(low_keep, low_pass)
low_back.defvjp(back_keep, back_low)

def layer_norm(features, scales):
    centred = features - lax.optimization_barrier(jnp.mean(features, axis=-1, keepdims=True))
    spread = lax.optimization_barrier(jnp.mean(centred * centred, axis=-1, keepdims=True))
    return centred * lax.rsqrt(spread + norm_eps) * scales

def angle_table(length, head_size):
    exponents = jnp.arange(0, head_size, 2).astype(jnp.float32) / head_size
    inverse = rope_base ** (-exponents)
    places = jnp.arange(length).astype(jnp.float32)
    angles = places[:, None] * inverse[None, :]
    angles = jnp.concatenate([angles, angles], axis=-1)
    return (jnp.cos(angles), jnp.sin(angles))

def rotate(tensor, cosine, sine_table):
    half_size = tensor.shape[-1] // 2
    turned = jnp.concatenate([-tensor[..., half_size:], tensor[..., :half_size]], axis=-1)
    return tensor * cosine + turned * sine_table

def layer_forward(inputs, attn_gain, qkv_weight, out_weight, mlp_gain, in_weight, down_weight):
    groups, length, model_width = inputs.shape
    heads_all = model_width // HD
    cosine, sine_table = angle_table(length, HD)
    cos_heads = cosine[:, None, :]
    sin_heads = sine_table[:, None, :]
    normed = low(layer_norm(inputs, attn_gain))
    projected = low_back(jnp.einsum('bld,cde->cble', normed, qkv_weight, precision=highest))
    split_heads = projected.reshape(3, groups, length, heads_all, HD)
    query_rows = low(rotate(split_heads[0], cos_heads, sin_heads))
    key_rows = low(rotate(split_heads[1], cos_heads, sin_heads))
    value_rows = low(split_heads[2])
    scores = low_back(jnp.einsum('blhe,bmhe->bhlm', query_rows, key_rows, precision=highest) * HD ** (-0.5))
    probs = low(jax.nn.softmax(scores, axis=-1))
    mixed_rows = low_back(low(jnp.einsum('bhlm,bmhe->blhe', probs, value_rows, precision=highest)))
    mixed_rows = mixed_rows.reshape(groups, length, model_width)
    attn_out = low_back(jnp.einsum('bld,de->ble', mixed_rows, out_weight, precision=highest))
    middle = inputs + attn_out
    normed_two = low(layer_norm(middle, mlp_gain))
    gate_up = low_back(jnp.einsum('bld,cdf->cblf', normed_two, in_weight, precision=highest))
    hidden = low(jax.nn.gelu(gate_up[0], approximate=False) * gate_up[1])
    mlp_out = low_back(jnp.einsum('blf,fd->bld', hidden, down_weight, precision=highest))
    return middle + mlp_out

def reference(hidden_in, attn_gain, qkv_weight, out_weight, mlp_gain, in_weight, down_weight, cotangent):
    params = (attn_gain.astype(jnp.float32), qkv_weight.astype(jnp.float32), out_weight.astype(jnp.float32), mlp_gain.astype(jnp.float32), in_weight.astype(jnp.float32), down_weight.astype(jnp.float32))
    group_size = math.gcd(SEQS, max(1, 4096 // SEQ_LEN))
    group_count = SEQS // group_size
    inputs = hidden_in.astype(jnp.float32).reshape(group_count, group_size, SEQ_LEN, D)
    grads_in = cotangent.astype(jnp.float32).reshape(group_count, group_size, SEQ_LEN, D)

    def one_group(totals, paired):
        group_in, group_grad = paired
        outputs, pull = jax.vjp(layer_forward, group_in, *params)
        pulled = pull(group_grad)
        totals = tuple((left + right for left, right in zip(totals, pulled[1:])))
        return (totals, (outputs, pulled[0]))
    initial = tuple((jnp.zeros_like(weight) for weight in params))
    totals, (outputs, input_grads) = lax.scan(one_group, initial, (inputs, grads_in))
    layer_out = outputs.reshape(TOKENS, D).astype(jnp.bfloat16)
    input_grad = input_grads.reshape(TOKENS, D)
    return (layer_out, input_grad, totals[0], totals[1], totals[2], totals[3], totals[4], totals[5])
```

```python
import functools
import math

import jax
import jax.numpy as jnp
from jax import lax
from jax.experimental import pallas as pl
from jax.experimental.pallas import tpu as pltpu
from jax.sharding import PartitionSpec as P

HD = 64
NORM_EPS = 1e-05
ROPE_BASE = 160000.0
BF = jnp.bfloat16
F32 = jnp.float32
LOG2E = math.log2(math.e)
VMEM_LIMIT = 56 * 1024 * 1024

NN = (((1,), (0,)), ((), ()))
NT = (((1,), (1,)), ((), ()))
TN = (((0,), (0,)), ((), ()))


def mm(a, b, dims=NN):
    return lax.dot_general(a, b, dims, preferred_element_type=F32)


def vmem():
    return pl.BlockSpec(memory_space=pltpu.VMEM)


def smem():
    return pl.BlockSpec(memory_space=pltpu.SMEM)


def hbm():
    return pl.BlockSpec(memory_space=pl.ANY)


def params():
    return pltpu.CompilerParams(vmem_limit_bytes=VMEM_LIMIT)


def call(body, ins, outs, scratch=(), flops=0, name=None):
    nbytes = sum(a.size * a.dtype.itemsize for a, _ in ins)
    nbytes += sum(math.prod(s) * jnp.dtype(d).itemsize for s, d in outs)
    return pl.pallas_call(
        body,
        out_shape=[jax.ShapeDtypeStruct(s, d) for s, d in outs],
        in_specs=[s for _, s in ins],
        out_specs=[vmem() for _ in outs],
        scratch_shapes=list(scratch),
        compiler_params=params(),
        cost_estimate=pl.CostEstimate(flops=flops, transcendentals=0, bytes_accessed=nbytes),
        name=name,
    )(*[a for a, _ in ins])


def swap(value, axis, size, distance):
    return lax.ppermute(value, axis, [(i, i ^ distance) for i in range(size)])


def after(value, *others):
    return lax.optimization_barrier((value, *others))[0]


def start_pieces(pieces, offs, rows, first, count, target, at, sem):
    copies = []
    for i, piece in enumerate(pieces):
        where = pl.ds(pl.multiple_of(offs[i] * rows, rows), rows)
        copy = pltpu.make_async_copy(
            piece.at[pl.ds(first, count)], target.at[pl.ds(at, count), where], sem.at[i]
        )
        copy.start()
        copies.append(copy)
    return copies


def turn(u, cos, sin):
    lane = lax.broadcasted_iota(jnp.int32, u.shape, 1)
    low = (lane & 63) < 32
    turned = jnp.where(low, pltpu.roll(u, 96, 1), pltpu.roll(u, 32, 1))
    return u * cos + turned * sin


def head_mask(shape, head):
    lane = lax.broadcasted_iota(jnp.int32, shape, 1)
    return (lane >> 6) == head


def attend_forward(n_pieces, piece_rows, scale, refs):
    offs, n0, n1, n2, n3, cos, sin = refs[:7]
    qk = refs[7 : 7 + n_pieces]
    vo = refs[7 + n_pieces : 7 + 2 * n_pieces]
    outs = refs[7 + 2 * n_pieces :]
    m0, m1, m2, m3, q_ref, k_ref, v_ref, lse_ref, w, sem_a, sem_b = outs
    copies_a = start_pieces(qk, offs, piece_rows, 0, 2, w, 0, sem_a)
    copies_b = start_pieces(vo, offs, piece_rows, 0, 1, w, 2, sem_b)
    for c in copies_a:
        c.wait()
    norms = (n0, n1, n2, n3)
    rows = n0.shape[0]
    width = w.shape[2]
    for i in range(4):
        at = pl.ds(i * rows, rows)
        for j, ref in ((0, q_ref), (1, k_ref)):
            u = mm(norms[i][...], w[j])
            for g in range(width // 128):
                col = slice(g * 128, g * 128 + 128)
                ref[at, col] = turn(u[:, col], cos[at, :], sin[at, :]).astype(BF)
    for c in copies_b:
        c.wait()
    for i in range(4):
        v_ref[pl.ds(i * rows, rows), :] = mm(norms[i][...], w[2]).astype(BF)
    mixed = (m0, m1, m2, m3)
    factor = scale * LOG2E
    for i in range(4):
        at = pl.ds(i * rows, rows)

        def one_head(h, acc, at=at):
            mask = head_mask((rows, width), h)
            qm = jnp.where(mask, q_ref[at, :], jnp.zeros((), BF))
            s = mm(qm, k_ref[...], NT)
            top = jnp.max(s, axis=1, keepdims=True)
            e = jnp.exp2((s - top) * factor)
            total = jnp.sum(e, axis=1, keepdims=True)
            o = mm(e.astype(BF), v_ref[...]) / total
            lse2 = top * factor + jnp.log2(total)
            row = jnp.transpose(jnp.broadcast_to(lse2, (rows, 128)))
            lse_ref[pl.ds(h, 1), at] = row[0:1, :]
            return jnp.where(mask, o, acc)

        acc = lax.fori_loop(0, width // HD, one_head, jnp.zeros((rows, width), F32))
        mixed[i][...] = acc.astype(BF)


def norm_stats(v):
    mean = jnp.mean(v, axis=-1, keepdims=True)
    centred = v - mean
    spread = jnp.mean(centred * centred, axis=-1, keepdims=True)
    r = lax.rsqrt(spread + NORM_EPS)
    return centred * r, r


def norm_body(h_ref, gain_ref, o_ref):
    xhat, _ = norm_stats(h_ref[...].astype(F32))
    o_ref[...] = (xhat * gain_ref[...]).astype(BF)


def load_out_weights(offs, outs_w, ow, sem, piece_rows, n_pieces):
    copies = []
    for b in range(4):
        for i in range(n_pieces):
            where = pl.ds(pl.multiple_of(offs[i] * piece_rows, piece_rows), piece_rows)
            c = pltpu.make_async_copy(
                outs_w[b].at[pl.ds(i * piece_rows, piece_rows)], ow.at[b, where], sem.at[b, i]
            )
            c.start()
            copies.append(c)
    return copies


def project_out(n_pieces, piece_rows, refs):
    offs, h_ref, gain, x0, x1, x2, x3, w0, w1, w2, w3, mid_ref, norm_ref, ow, sem = refs
    copies = load_out_weights(offs, (w0, w1, w2, w3), ow, sem, piece_rows, n_pieces)
    for c in copies:
        c.wait()
    total = h_ref[...].astype(F32)
    for b, x in enumerate((x0, x1, x2, x3)):
        total = total + mm(x[...], ow[b], NT)
    mid_ref[...] = total
    xhat, _ = norm_stats(total)
    norm_ref[...] = (xhat * gain[...]).astype(BF)


INV_SQRT2 = 1.0 / math.sqrt(2.0)
INV_SQRT2PI = 1.0 / math.sqrt(2.0 * math.pi)


def feed_forward(n_pieces, piece_rows, refs):
    offs, n0, n1, c0, c1 = refs[:5]
    pieces = refs[5 : 5 + n_pieces]
    p0, p1, y0, y1, hid, gug, w, sem = refs[5 + n_pieces :]
    copies = start_pieces(pieces, offs, piece_rows, 0, 3, w, 0, sem)
    for c in copies:
        c.wait()
    rows = n0.shape[0]
    for n, c, p, y, i in ((n0, c0, p0, y0, 0), (n1, c1, p1, y1, 1)):
        at = pl.ds(i * rows, rows)
        gate = mm(n[...], w[0])
        up = mm(n[...], w[1])
        back = mm(c[...], w[2])
        cdf = 0.5 * (1.0 + lax.erf(gate * INV_SQRT2))
        pdf = jnp.exp(-0.5 * gate * gate) * INV_SQRT2PI
        act = gate * cdf
        hidden = (act * up).astype(BF)
        g0 = (back * up * (cdf + gate * pdf)).astype(BF)
        g1 = (back * act).astype(BF)
        hid[at, :] = hidden
        gug[0, at, :] = g0
        gug[1, at, :] = g1
        p[...] = (mm(g0, w[0], NT) + mm(g1, w[1], NT)).astype(BF)
        y[...] = mm(hidden, w[2], NT).astype(BF)


def pick_columns(ref, first, second, size):
    a = ref[:, pl.ds(pl.multiple_of(first * size, size), size)]
    b = ref[:, pl.ds(pl.multiple_of(second * size, size), size)]
    return jnp.concatenate([a, b], axis=1)


def mlp_grads(refs):
    cols = refs[0]
    n, c = refs[1:5], refs[5:9]
    hid, gug = refs[9:11], refs[11:13]
    outs = refs[13:21]
    half = hid[0].shape[0]
    rows = n[0].shape[0]
    for k in range(4):
        first, second = cols[2 * k], cols[2 * k + 1]
        for j in range(3):
            total = None
            for i in range(4):
                source = c[i] if j == 2 else n[i]
                left = pick_columns(source, first, second, 128)
                at = pl.ds((i % 2) * rows, rows)
                right = hid[i // 2][at, :] if j == 2 else gug[i // 2][j, at, :]
                part = mm(left, right, TN)
                total = part if total is None else total + part
            outs[2 * k][j] = total[:128].astype(BF)
            outs[2 * k + 1][j] = total[128:].astype(BF)


def norm_back(v, g):
    xhat, r = norm_stats(v)
    mean_g = jnp.mean(g, axis=-1, keepdims=True)
    mean_gx = jnp.mean(g * xhat, axis=-1, keepdims=True)
    return r * (g - mean_g - xhat * mean_gx), xhat


def middle_back(n_pieces, piece_rows, refs):
    offs, mid, cot, gain, sa, sb, sc, w0, w1, w2, w3 = refs[:11]
    mg_ref, low_ref, x0, x1, x2, x3, gain_ref, ow, sem = refs[11:]
    copies = load_out_weights(offs, (w0, w1, w2, w3), ow, sem, piece_rows, n_pieces)
    got = sa[...].astype(F32) + sb[...].astype(F32) + sc[...].astype(F32)
    back, xhat = norm_back(mid[...], gain[...] * got)
    gain_ref[...] = jnp.sum(got * xhat, axis=0, keepdims=True)
    mg = cot[...].astype(F32) + back
    mg_ref[...] = mg
    low = mg.astype(BF)
    low_ref[...] = low
    for c in copies:
        c.wait()
    for b, x in enumerate((x0, x1, x2, x3)):
        x[...] = mm(low, ow[b]).astype(BF)


def attend_backward(scale, refs):
    g0, g1, g2, g3, m0, m1, m2, m3, q, k, v, lse, cos, sin = refs[:14]
    pg, do, dot_rows, dq = refs[14:]
    rows = g0.shape[0]
    length, width = q.shape
    heads = width // HD
    lane = lax.broadcasted_iota(jnp.int32, (8, width), 1) >> 6
    head = lax.broadcasted_iota(jnp.int32, (8, width), 0)
    ones = jnp.where(lane == head, 1.0, 0.0).astype(BF)
    for i, (g, m) in enumerate(((g0, m0), (g1, m1), (g2, m2), (g3, m3))):
        at = pl.ds(i * rows, rows)
        do[at, :] = g[...]
        t = g[...].astype(F32) * m[...].astype(F32)
        hi = t.astype(BF)
        lo = (t - hi.astype(F32)).astype(BF)
        dot_rows[:, at] = mm(ones, hi, NT) + mm(ones, lo, NT)
    dq[...] = jnp.zeros_like(dq)
    factor = scale * LOG2E
    for i in range(4):
        at = pl.ds(i * rows, rows)
        zero = jnp.zeros((rows, width), F32)

        def one_head(h, carry, at=at):
            dk_acc, dv_acc = carry
            mask = head_mask((length, width), h)
            here = head_mask((rows, width), h)
            nil = jnp.zeros((), BF)
            qm = jnp.where(mask, q[...], nil)
            dom = jnp.where(mask, do[...], nil)
            km = jnp.where(here, k[at, :], nil)
            s = mm(k[at, :], qm, NT)
            p = jnp.exp2(s * factor - lse[pl.ds(h, 1), :])
            dv_acc = dv_acc + mm(p.astype(BF), dom)
            dp = mm(v[at, :], dom, NT)
            ds = (p * (dp - dot_rows[pl.ds(h, 1), :])).astype(BF)
            dk_acc = dk_acc + mm(ds, qm)
            dq[...] += mm(ds, km, TN)
            return dk_acc, dv_acc

        dk_acc, dv_acc = lax.fori_loop(0, heads, one_head, (zero, zero))
        for g in range(width // 128):
            col = slice(g * 128, g * 128 + 128)
            part = dk_acc[:, col] * scale
            pg[1, at, col] = turn(part, cos[at, :], -sin[at, :]).astype(BF)
        pg[2, at, :] = dv_acc.astype(BF)
    for i in range(4):
        at = pl.ds(i * rows, rows)
        for g in range(width // 128):
            col = slice(g * 128, g * 128 + 128)
            part = dq[at, col] * scale
            pg[0, at, col] = turn(part, cos[at, :], -sin[at, :]).astype(BF)


def attn_grads(refs):
    cols = refs[0]
    n, a, m, pg = refs[1:5], refs[5:9], refs[9:13], refs[13]
    outs = refs[14:22]
    rows = n[0].shape[0]
    for k in range(4):
        first, second = cols[2 * k], cols[2 * k + 1]
        for j in range(4):
            total = None
            for i in range(4):
                source = a[i] if j == 3 else n[i]
                left = pick_columns(source, first, second, 128)
                right = m[i][...] if j == 3 else pg[j, pl.ds(i * rows, rows), :]
                part = mm(left, right, TN)
                total = part if total is None else total + part
            outs[2 * k][j] = total[:128].astype(BF)
            outs[2 * k + 1][j] = total[128:].astype(BF)


def normed_back(n_pieces, piece_rows, refs):
    offs, gain, n0, n1, n2, n3, pg = refs[:7]
    qk = refs[7 : 7 + n_pieces]
    vo = refs[7 + n_pieces : 7 + 2 * n_pieces]
    p0, p1, p2, p3, gain_ref, w, sem_a, sem_b = refs[7 + 2 * n_pieces :]
    copies = start_pieces(qk, offs, piece_rows, 0, 2, w, 0, sem_a)
    copies += start_pieces(vo, offs, piece_rows, 0, 1, w, 2, sem_b)
    for c in copies:
        c.wait()
    rows = n0.shape[0]
    sums = None
    for i, (n, p) in enumerate(((n0, p0), (n1, p1), (n2, p2), (n3, p3))):
        at = pl.ds(i * rows, rows)
        total = mm(pg[0, at, :], w[0], NT) + mm(pg[1, at, :], w[1], NT) + mm(pg[2, at, :], w[2], NT)
        p[...] = total.astype(BF)
        part = jnp.sum(total * n[...].astype(F32), axis=0, keepdims=True)
        sums = part if sums is None else sums + part
    gain_ref[...] = sums / gain[...]


def input_back(h, mg, gain, sa, sb, sc, o_ref):
    got = sa[...].astype(F32) + sb[...].astype(F32) + sc[...].astype(F32)
    back, _ = norm_back(h[...].astype(F32), gain[...] * got)
    o_ref[...] = mg[...] + back


def body(function, *static):
    return lambda *refs: function(*static, refs)


def angle_tables(mine, rows):
    exponents = jnp.arange(0, HD, 2).astype(F32) / HD
    inverse = ROPE_BASE ** (-exponents)
    block = jnp.arange(4, dtype=jnp.int32)[:, None] ^ mine
    places = (block * rows + jnp.arange(rows, dtype=jnp.int32)[None, :]).reshape(-1)
    angles = places.astype(F32)[:, None] * inverse[None, :]
    cos, sin = jnp.cos(angles), jnp.sin(angles)
    return (
        jnp.concatenate([cos, cos, cos, cos], axis=1),
        jnp.concatenate([-sin, sin, -sin, sin], axis=1),
    )


def shards(sizes, *args):
    hidden_in, attn_gain, qkv_weight, out_weight, mlp_gain, in_weight, down_weight, cotangent = args
    dp, tp = sizes
    rows, model = hidden_in.shape
    length = rows * tp
    piece_rows = qkv_weight.shape[1]
    width = qkv_weight.shape[2]
    units = in_weight.shape[2]
    scale = HD ** (-0.5)
    direct = dp == 8
    mine = lax.axis_index("tensor")
    place = lax.axis_index("dp")
    gain_one, gain_two = attn_gain.reshape(1, model), mlp_gain.reshape(1, model)

    tensor = lambda v, k: swap(v, "tensor", tp, k)
    depth = lambda v, k: swap(v, "dp", dp, k)

    def gather(shard):
        if direct:
            along = [shard] + [depth(shard, 2 * k) for k in (1, 2, 3)]
            across = [depth(v, 1) for v in along]
            return [v for pair in zip(along, across) for v in pair]
        return [lax.all_gather(shard, "dp", axis=1, tiled=True)]

    if direct:
        offs = place ^ jnp.arange(8, dtype=jnp.int32)
        n_pieces, long_rows = 8, piece_rows
    else:
        offs = jnp.zeros((1,), jnp.int32)
        n_pieces, long_rows = 1, model
    sems = lambda *s: pltpu.SemaphoreType.DMA(s)

    def spread(own):
        far = tensor(own, 2)
        return [own, tensor(own, 1), far, tensor(far, 1)]

    def exchange(blocks):
        return [blocks[0]] + [tensor(blocks[k], k) for k in (1, 2, 3)]

    qk_shard = qkv_weight[0:2]
    qk = gather(qk_shard)
    (normed,) = call(
        norm_body, [(hidden_in, vmem()), (gain_one, vmem())], [((rows, model), BF)], name="norm"
    )
    normed_attn = spread(normed)
    vo_shard = jnp.concatenate([qkv_weight[2:3], out_weight.T[None]], axis=0)
    vo = gather(vo_shard)
    cos, sin = angle_tables(mine, rows)
    *mixed, q, k, v, lse = call(
        body(attend_forward, n_pieces, long_rows, scale),
        [(offs, smem())]
        + [(x, vmem()) for x in normed_attn]
        + [(cos, vmem()), (sin, vmem())]
        + [(x, hbm()) for x in qk + vo],
        [((rows, width), BF)] * 4 + [((length, width), BF)] * 3 + [((8, length), F32)],
        [pltpu.VMEM((3, model, width), BF), sems(n_pieces), sems(n_pieces)],
        flops=2 * length * model * width * 3 + 4 * length * length * width * 4,
        name="attend_forward",
    )
    mixed_own = exchange(mixed)
    out_own = jnp.concatenate([x[1] for x in vo], axis=0)
    out_all = spread(out_own)
    middle, normed_two = call(
        body(project_out, n_pieces, long_rows),
        [(offs, smem()), (hidden_in, vmem()), (gain_two, vmem())]
        + [(x, vmem()) for x in mixed_own]
        + [(x, hbm()) for x in out_all],
        [((rows, model), F32), ((rows, model), BF)],
        [pltpu.VMEM((4, model, width), BF), sems(4, n_pieces)],
        flops=2 * rows * model * model,
        name="project_out",
    )

    mlp_shard = jnp.concatenate([in_weight, down_weight.T[None]], axis=0)
    mlp = gather(mlp_shard)
    cot = spread(cotangent)
    normed_mlp = spread(normed_two)

    def feed(first):
        return call(
            body(feed_forward, n_pieces, long_rows),
            [(offs, smem())]
            + [(x, vmem()) for x in normed_mlp[first : first + 2] + cot[first : first + 2]]
            + [(x, hbm()) for x in mlp],
            [((rows, model), BF)] * 4 + [((2 * rows, units), BF), ((2, 2 * rows, units), BF)],
            [pltpu.VMEM((3, model, units), BF), sems(n_pieces)],
            flops=2 * 2 * rows * model * units * 6,
            name="feed_forward",
        )

    near_back, near_send, near_out, near_out_send, near_hidden, near_grad = feed(0)
    far_back, far_send, far_out, far_out_send, far_hidden, far_grad = feed(2)
    add = lambda a, b: (a.astype(F32) + b.astype(F32)).astype(BF)
    near_got = tensor(near_send, 1)
    from_far = tensor(add(far_back, tensor(far_send, 1)), 2)
    out_far = tensor(add(far_out, tensor(far_out_send, 1)), 2)
    mlp_out = near_out.astype(F32) + tensor(near_out_send, 1).astype(F32) + out_far.astype(F32)
    layer_out = (middle + mlp_out).astype(BF)

    if direct:
        z, y = place // 2, place % 2
        order = [1, 2, 3, 0]
        cols = jnp.stack([c for b in order for c in ((z ^ b) * 2 + (1 - y), (z ^ b) * 2 + y)])
    else:
        cols = jnp.arange(8, dtype=jnp.int32)
    cols = cols.astype(jnp.int32)

    def reduce(blocks, parts, columns):
        if not direct:
            whole = jnp.concatenate(blocks, axis=1)
            return lax.psum_scatter(whole, "dp", scatter_dimension=1, tiled=True).astype(F32)
        got = [depth(blocks[2 * i], 1) for i in range(4)]
        total = [add(blocks[2 * i + 1], got[i]) for i in range(3)]
        back = [depth(total[i], 2 * order[i]) for i in range(3)]
        own = blocks[7].astype(F32) + got[3].astype(F32)
        return own + back[0].astype(F32) + back[1].astype(F32) + back[2].astype(F32)

    middle_grad, low_grad, x0, x1, x2, x3, gain_two_part = call(
        body(middle_back, n_pieces, long_rows),
        [(offs, smem()), (middle, vmem()), (cotangent, vmem()), (gain_two, vmem())]
        + [(x, vmem()) for x in (near_back, near_got, from_far)]
        + [(x, hbm()) for x in out_all],
        [((rows, model), F32), ((rows, model), BF)]
        + [((rows, width), BF)] * 4
        + [((1, model), F32)],
        [pltpu.VMEM((4, model, width), BF), sems(4, n_pieces)],
        flops=2 * rows * model * model,
        name="middle_back",
    )
    mixed_grad = exchange([x0, x1, x2, x3])
    attn_out_grad = spread(low_grad)

    grads = call(
        body(mlp_grads),
        [(cols, smem())]
        + [(x, vmem()) for x in normed_mlp + cot]
        + [(x, vmem()) for x in (near_hidden, far_hidden, near_grad, far_grad)],
        [((3, 128, units), BF)] * 8,
        flops=2 * length * model * units * 3,
        name="mlp_grads",
    )
    mlp_total = reduce(grads, 3, units)
    in_shard, down_shard = mlp_total[0:2], mlp_total[2].T

    (pg,) = call(
        body(attend_backward, scale),
        [(x, vmem()) for x in mixed_grad + mixed + [q, k, v, lse, cos, sin]],
        [((3, length, width), BF)],
        [pltpu.VMEM((length, width), BF), pltpu.VMEM((8, length), F32), pltpu.VMEM((length, width), F32)],
        flops=10 * length * length * width * 4,
        name="attend_backward",
    )
    attn = call(
        body(attn_grads),
        [(cols, smem())]
        + [(x, vmem()) for x in normed_attn + attn_out_grad + mixed]
        + [(pg, vmem())],
        [((4, 128, width), BF)] * 8,
        flops=2 * length * model * width * 4,
        name="attn_grads",
    )
    attn_total = reduce(attn, 4, width)
    qkv_shard, out_shard = attn_total[0:3], attn_total[3].T
    b0, b1, b2, b3, gain_one_part = call(
        body(normed_back, n_pieces, long_rows),
        [(offs, smem()), (gain_one, vmem())]
        + [(x, vmem()) for x in normed_attn + [pg]]
        + [(x, hbm()) for x in qk + vo],
        [((rows, model), BF)] * 4 + [((1, model), F32)],
        [pltpu.VMEM((3, model, width), BF), sems(n_pieces), sems(n_pieces)],
        flops=2 * length * model * width * 3,
        name="normed_back",
    )
    far_sum = add(b2, tensor(b3, 1))
    near_sum = tensor(b1, 1)
    (input_grad,) = call(
        input_back,
        [(x, vmem()) for x in (hidden_in, middle_grad, gain_one, b0, near_sum, tensor(far_sum, 2))],
        [((rows, model), F32)],
        name="input_back",
    )

    gains = jnp.concatenate([gain_one_part, gain_two_part], axis=0).reshape(16, 128)
    if direct:
        gains = gains + tensor(gains, 1)
        gains = gains + tensor(gains, 2)
        gains = gains + depth(gains, 1)
        gains = (gains + depth(gains, 2)) + (depth(gains, 4) + depth(gains, 6))
    else:
        gains = lax.psum(gains, ("dp", "tensor"))
    gains = gains.reshape(2, model)
    return (layer_out, input_grad, gains[0], qkv_shard, out_shard, gains[1], in_shard, down_shard)


def solution(mesh):
    sizes = (mesh.shape["dp"], mesh.shape["tensor"])
    return jax.shard_map(
        functools.partial(shards, sizes),
        mesh=mesh,
        in_specs=(
            P(("dp", "tensor"), None),
            P(),
            P(None, "dp", "tensor"),
            P("tensor", "dp"),
            P(),
            P(None, "dp", "tensor"),
            P("tensor", "dp"),
            P(("dp", "tensor"), None),
        ),
        out_specs=(
            P(("dp", "tensor"), None),
            P(("dp", "tensor"), None),
            P(),
            P(None, "dp", "tensor"),
            P("tensor", "dp"),
            P(),
            P(None, "dp", "tensor"),
            P("tensor", "dp"),
        ),
        check_vma=False,
    )
```

```python
import functools
import math

import jax
import jax.numpy as jnp
import numpy as np
from jax import lax
from jax.experimental import pallas as pl
from jax.experimental.pallas import tpu as pltpu
from jax.sharding import PartitionSpec as P

HD = 64
NORM_EPS = 1e-05
ROPE_BASE = 160000.0
BF = jnp.bfloat16
F32 = jnp.float32
LOG2E = math.log2(math.e)
COST = 1000
VMEM_MIB = 56

NN = (((1,), (0,)), ((), ()))
NT = (((1,), (1,)), ((), ()))
TN = (((0,), (0,)), ((), ()))


def mm(a, b, dims=NN):
    return lax.dot_general(a, b, dims, preferred_element_type=F32)


def vmem():
    return pl.BlockSpec(memory_space=pltpu.VMEM)


def smem():
    return pl.BlockSpec(memory_space=pltpu.SMEM)


def hbm():
    return pl.BlockSpec(memory_space=pltpu.HBM)


def call(body, ins, outs, scratch=(), name=None):
    return pl.pallas_call(
        body,
        out_shape=[jax.ShapeDtypeStruct(o[0], o[1]) for o in outs],
        in_specs=[i[1] for i in ins],
        out_specs=[o[2] for o in outs],
        scratch_shapes=list(scratch),
        compiler_params=pltpu.CompilerParams(vmem_limit_bytes=VMEM_MIB * 1024 * 1024),
        cost_estimate=pl.CostEstimate(flops=COST, transcendentals=0, bytes_accessed=COST),
        name=name,
    )(*[i[0] for i in ins])


def swap(value, axis, size, distance, label):
    with jax.named_scope(label):
        return lax.ppermute(value, axis, [(i, i ^ distance) for i in range(size)])


def gate(values, others):
    return list(lax.optimization_barrier((tuple(values), tuple(others)))[0])


def start(source, target, sem):
    copy = pltpu.make_async_copy(source, target, sem)
    copy.start()
    return copy


def start_pieces(pieces, offs, size, target, sem, axis):
    copies = []
    for i, piece in enumerate(pieces):
        where = pl.ds(pl.multiple_of(offs[i] * size, size), size)
        copies.append(start(piece, target.at[(slice(None),) * axis + (where,)], sem.at[i]))
    return copies


def wait(copies):
    for c in copies:
        c.wait()


def angles_at(table, block, rows):
    both = table[pl.ds(pl.multiple_of(block * rows, rows), rows), :]
    other = pltpu.roll(both, 64, 1)
    lane = lax.broadcasted_iota(jnp.int32, both.shape, 1)
    cos = jnp.where(lane < 64, both, other)
    sin = jnp.where(lane < 64, other, both)
    return cos, jnp.where((lane & 63) < 32, -sin, sin)


def turn(u, cos, sin):
    lane = lax.broadcasted_iota(jnp.int32, u.shape, 1)
    low = (lane & 63) < 32
    turned = jnp.where(low, pltpu.roll(u, 96, 1), pltpu.roll(u, 32, 1))
    return u * cos + turned * sin


def head_mask(shape, head):
    lane = lax.broadcasted_iota(jnp.int32, shape, 1)
    return (lane >> 6) == head


def attend_forward(n_pieces, piece_rows, scale, refs):
    offs, mine = refs[:2]
    norms, table = refs[2:6], refs[6]
    pieces = refs[7 : 7 + n_pieces]
    refs = refs[7 + n_pieces :]
    mixed, (q_out, k_out, v_out, lse_ref) = refs[0:4], refs[4:8]
    n, tab, w, q, k, v, sem_w, sem = refs[8:]
    rows, width = n.shape[1], w.shape[2]
    loads = start_pieces([x.at[pl.ds(0, 3)] for x in pieces], offs, piece_rows, w, sem_w, 1)
    norm_loads = [start(norms[i], n.at[i], sem.at[i]) for i in range(4)]
    table_load = start(table, tab, sem.at[4])
    wait(loads)
    table_load.wait()
    for i in range(4):
        at = pl.ds(i * rows, rows)
        cos, sin = angles_at(tab, mine[0] ^ i, rows)
        norm_loads[i].wait()
        for j, ref in ((0, q), (1, k)):
            u = mm(n[i], w[j])
            for g in range(width // 128):
                col = slice(g * 128, g * 128 + 128)
                ref[at, col] = turn(u[:, col], cos, sin).astype(BF)
        v[at, :] = mm(n[i], w[2]).astype(BF)
    stores = [start(x, y, sem.at[5 + i]) for i, (x, y) in enumerate(((q, q_out), (k, k_out), (v, v_out)))]
    factor = scale * LOG2E
    heads = width // HD
    for i in range(4):
        at = pl.ds(i * rows, rows)

        def one_head(h, acc, at=at):
            mask = head_mask((rows, width), h)
            qm = jnp.where(mask, q[at, :], jnp.zeros((), BF))
            s = mm(qm, k[...], NT)
            top = jnp.max(s, axis=1, keepdims=True)
            e = jnp.exp2((s - top) * factor)
            total = jnp.sum(e, axis=1, keepdims=True)
            o = mm(e.astype(BF), v[...]) / total
            lse2 = top * factor + jnp.log2(total)
            row = jnp.transpose(jnp.broadcast_to(lse2, (rows, 128)))
            lse_ref[pl.ds(h, 1), at] = row[0:1, :]
            return jnp.where(mask, o, acc)

        acc = lax.fori_loop(0, heads, one_head, jnp.zeros((rows, width), F32))
        mixed[i][...] = acc.astype(BF)
    wait(stores)


def norm_stats(v):
    mean = jnp.mean(v, axis=-1, keepdims=True)
    centred = v - mean
    spread = jnp.mean(centred * centred, axis=-1, keepdims=True)
    r = lax.rsqrt(spread + NORM_EPS)
    return centred * r, r


def norm_body(h_ref, gain_ref, o_ref):
    xhat, _ = norm_stats(h_ref[...].astype(F32))
    o_ref[...] = (xhat * gain_ref[...]).astype(BF)


def pack_body(qkv, out, inner, down, first, second):
    first[0:3] = qkv[...]
    first[3] = out[...].T
    second[0:2] = inner[...]
    second[2] = down[...]


def assemble_out(n_pieces, piece_rows, refs):
    offs, pieces, o_ref, sem = refs[0], refs[1 : 1 + n_pieces], refs[1 + n_pieces], refs[2 + n_pieces]
    wait(start_pieces([x.at[3] for x in pieces], offs, piece_rows, o_ref, sem, 0))


def project_out(h_ref, gain, x0, x1, x2, x3, w0, w1, w2, w3, mid_ref, norm_ref):
    total = h_ref[...].astype(F32)
    for x, w in ((x0, w0), (x1, w1), (x2, w2), (x3, w3)):
        total = total + mm(x[...], w[...], NT)
    mid_ref[...] = total
    xhat, _ = norm_stats(total)
    norm_ref[...] = (xhat * gain[...]).astype(BF)


INV_SQRT2 = 1.0 / math.sqrt(2.0)
INV_SQRT2PI = 1.0 / math.sqrt(2.0 * math.pi)


def feed_rows(n, c, w):
    gate = mm(n, w[0], NT)
    up = mm(n, w[1], NT)
    back = mm(c, w[2], NT)
    cdf = 0.5 * (1.0 + lax.erf(gate * INV_SQRT2))
    pdf = jnp.exp(-0.5 * gate * gate) * INV_SQRT2PI
    act = gate * cdf
    hidden = (act * up).astype(BF)
    g0 = (back * up * (cdf + gate * pdf)).astype(BF)
    g1 = (back * act).astype(BF)
    grad = (mm(g0, w[0]) + mm(g1, w[1])).astype(BF)
    return grad, mm(hidden, w[2]).astype(BF), hidden, g0, g1


def load_mlp(pieces, offs, size, w, sem):
    return [
        start_pieces([x.at[j] for x in pieces], offs, size, w.at[j], sem.at[j], 1) for j in range(3)
    ]


def feed_far(n_pieces, size, refs):
    offs, n_in, c_in, pieces = refs[0], refs[1:3], refs[3:5], refs[5 : 5 + n_pieces]
    grads, outs, (hid, gug), (n, c, w, sem_w, sem) = (
        refs[5 + n_pieces : 7 + n_pieces],
        refs[7 + n_pieces : 9 + n_pieces],
        refs[9 + n_pieces : 11 + n_pieces],
        refs[11 + n_pieces :],
    )
    loads = [start(n_in[i], n.at[i], sem.at[i]) for i in range(2)]
    loads += [start(c_in[i], c.at[i], sem.at[2 + i]) for i in range(2)]
    for group in load_mlp(pieces, offs, size, w, sem_w):
        wait(group)
    wait(loads)
    rows = n.shape[1]
    for i in range(2):
        at = pl.ds(i * rows, rows)
        grads[i][...], outs[i][...], hid[at, :], gug[0, at, :], gug[1, at, :] = feed_rows(n[i], c[i], w)


def pick_columns(ref, first, second, size):
    a = ref[:, pl.ds(pl.multiple_of(first * size, size), size)]
    b = ref[:, pl.ds(pl.multiple_of(second * size, size), size)]
    return jnp.concatenate([a, b], axis=1)


def mlp_grads(cols, blocks, n, c, hidden, grads, outs):
    for k, block in enumerate(blocks):
        first, second = cols[2 * block], cols[2 * block + 1]
        for j in range(3):
            total = None
            for i in range(4):
                right = pick_columns((c if j == 2 else n).at[i], first, second, 128)
                part = mm(hidden(i) if j == 2 else grads(i, j), right, TN)
                total = part if total is None else total + part
            outs[2 * k][j] = total[:, :128].astype(BF)
            outs[2 * k + 1][j] = total[:, 128:].astype(BF)


def feed_near(n_pieces, size, refs):
    offs, cols, n_in, c_in, hid_far, gug_far = refs[0], refs[1], refs[2:6], refs[6:10], refs[10], refs[11]
    pieces = refs[12 : 12 + n_pieces]
    refs = refs[12 + n_pieces :]
    grads, outs, (hid, gug), blocks = refs[0:2], refs[2:4], refs[4:6], refs[6:10]
    n, c, hf, gf, w, sem_w, sem = refs[10:]
    loads = [start(n_in[i], n.at[i], sem.at[i]) for i in range(4)]
    loads += [start(c_in[i], c.at[i], sem.at[4 + i]) for i in range(4)]
    groups = load_mlp(pieces, offs, size, w, sem_w)
    late = [start(hid_far, hf, sem.at[8]), start(gug_far, gf, sem.at[9])]
    for group in groups:
        wait(group)
    wait(loads)
    rows = n.shape[1]
    for i in range(2):
        at = pl.ds(i * rows, rows)
        grads[i][...], outs[i][...], hid[at, :], gug[0, at, :], gug[1, at, :] = feed_rows(n[i], c[i], w)
    wait(late)
    hidden = lambda i: (hf if i > 1 else hid)[pl.ds(i % 2 * rows, rows), :]
    both = lambda i, j: (gf if i > 1 else gug)[j, pl.ds(i % 2 * rows, rows), :]
    mlp_grads(cols, (0, 1), n, c, hidden, both, blocks)


def feed_late(refs):
    cols, n_in, c_in = refs[0], refs[1:5], refs[5:9]
    sources, blocks = refs[9:13], refs[13:17]
    n, c, hn, hf, gn, gf, sem = refs[17:]
    loads = [start(n_in[i], n.at[i], sem.at[i]) for i in range(4)]
    loads += [start(c_in[i], c.at[i], sem.at[4 + i]) for i in range(4)]
    loads += [start(x, y, sem.at[8 + i]) for i, (x, y) in enumerate(zip(sources, (hn, hf, gn, gf)))]
    wait(loads)
    rows = n.shape[1]
    hidden = lambda i: (hf if i > 1 else hn)[pl.ds(i % 2 * rows, rows), :]
    both = lambda i, j: (gf if i > 1 else gn)[j, pl.ds(i % 2 * rows, rows), :]
    mlp_grads(cols, (2, 3), n, c, hidden, both, blocks)


def norm_back(v, g):
    xhat, r = norm_stats(v)
    mean_g = jnp.mean(g, axis=-1, keepdims=True)
    mean_gx = jnp.mean(g * xhat, axis=-1, keepdims=True)
    return r * (g - mean_g - xhat * mean_gx), xhat


def middle_back(mid, cot, gain, sa, sb, sc, w0, w1, w2, w3, mg_ref, low_ref, x0, x1, x2, x3, gain_ref):
    got = sa[...].astype(F32) + sb[...].astype(F32) + sc[...].astype(F32)
    back, xhat = norm_back(mid[...], gain[...] * got)
    sums = jnp.sum(got * xhat, axis=0, keepdims=True)
    for i in range(8):
        gain_ref[pl.ds(i, 1), :] = sums[:, 128 * i : 128 * i + 128]
    mg = cot[...].astype(F32) + back
    mg_ref[...] = mg
    low = mg.astype(BF)
    low_ref[...] = low
    for x, w in ((x0, w0), (x1, w1), (x2, w2), (x3, w3)):
        x[...] = mm(low, w[...]).astype(BF)


def attend_backward(scale, refs):
    cols, mine = refs[:2]
    grads_in, mixed_in, q_in, k_in, v_in, lse_in, table, norms = (
        refs[2:6], refs[6:10], refs[10], refs[11], refs[12], refs[13], refs[14], refs[15:19]
    )
    outs, pg_out = refs[19:27], refs[27]
    pg, do, o, q, k, v, lse, tab, n, dot_rows, dq, sem = refs[28:]
    rows = n.shape[1]
    length, width = q.shape
    heads = width // HD
    near = [start(grads_in[i], do.at[pl.ds(i * rows, rows)], sem.at[i]) for i in range(4)]
    near += [start(mixed_in[i], o.at[pl.ds(i * rows, rows)], sem.at[4 + i]) for i in range(4)]
    pairs = ((q_in, q), (k_in, k), (v_in, v), (lse_in, lse))
    near += [start(x, y, sem.at[8 + i]) for i, (x, y) in enumerate(pairs)]
    late = [start(table, tab, sem.at[12])]
    late += [start(norms[i], n.at[i], sem.at[13 + i]) for i in range(4)]
    wait(near)
    lane = lax.broadcasted_iota(jnp.int32, (8, width), 1) >> 6
    head = lax.broadcasted_iota(jnp.int32, (8, width), 0)
    ones = jnp.where(lane == head, 1.0, 0.0).astype(BF)
    for i in range(4):
        at = pl.ds(i * rows, rows)
        t = do[at, :].astype(F32) * o[at, :].astype(F32)
        hi = t.astype(BF)
        lo = (t - hi.astype(F32)).astype(BF)
        dot_rows[:, at] = mm(ones, hi, NT) + mm(ones, lo, NT)
    dq[...] = jnp.zeros_like(dq)
    factor = scale * LOG2E
    for i in range(4):
        at = pl.ds(i * rows, rows)
        zero = jnp.zeros((rows, width), F32)

        def one_head(h, carry, at=at):
            dk_acc, dv_acc = carry
            mask = head_mask((length, width), h)
            here = head_mask((rows, width), h)
            nil = jnp.zeros((), BF)
            qm = jnp.where(mask, q[...], nil)
            dom = jnp.where(mask, do[...], nil)
            km = jnp.where(here, k[at, :], nil)
            s = mm(k[at, :], qm, NT)
            p = jnp.exp2(s * factor - lse[pl.ds(h, 1), :])
            dv_acc = dv_acc + mm(p.astype(BF), dom)
            dp = mm(v[at, :], dom, NT)
            ds = (p * (dp - dot_rows[pl.ds(h, 1), :])).astype(BF)
            dk_acc = dk_acc + mm(ds, qm)
            dq[...] += mm(ds, km, TN)
            return dk_acc, dv_acc

        dk_acc, dv_acc = lax.fori_loop(0, heads, one_head, (zero, zero))
        if i == 0:
            wait(late)
        cos, sin = angles_at(tab, mine[0] ^ i, rows)
        for g in range(width // 128):
            col = slice(g * 128, g * 128 + 128)
            part = dk_acc[:, col] * scale
            pg[1, at, col] = turn(part, cos, -sin).astype(BF)
        pg[2, at, :] = dv_acc.astype(BF)
    for i in range(4):
        at = pl.ds(i * rows, rows)
        cos, sin = angles_at(tab, mine[0] ^ i, rows)
        for g in range(width // 128):
            col = slice(g * 128, g * 128 + 128)
            part = dq[at, col] * scale
            pg[0, at, col] = turn(part, cos, -sin).astype(BF)
    store = start(pg, pg_out, sem.at[17])
    for block in range(4):
        first, second = cols[2 * block], cols[2 * block + 1]
        for j in range(3):
            total = None
            for i in range(4):
                left = pick_columns(n.at[i], first, second, 128)
                part = mm(left, pg[j, pl.ds(i * rows, rows), :], TN)
                total = part if total is None else total + part
            outs[2 * block][j] = total[:128].astype(BF)
            outs[2 * block + 1][j] = total[128:].astype(BF)
    store.wait()


def out_grads(refs):
    cols = refs[0]
    a, m = refs[1:5], refs[5:9]
    sent, kept = refs[9:11]
    for block in range(4):
        first, second = cols[2 * block], cols[2 * block + 1]
        total = None
        for i in range(4):
            part = mm(m[i][...], pick_columns(a[i], first, second, 128), TN)
            total = part if total is None else total + part
        sent[block] = total[:, :128].astype(BF)
        kept[block] = total[:, 128:].astype(BF)


def halves_of(x):
    high = x.astype(BF)
    return high, (x - high.astype(F32)).astype(BF)


def write_gains(ref, rows, gains):
    high, low = halves_of(gains)
    tail = pl.ds(rows, 16)
    ref[tail, :] = jnp.zeros((16, ref.shape[1]), BF)
    ref[tail, 0:128] = high
    ref[tail, 128:256] = low
    return high.astype(F32) + low.astype(F32)


def read_gains(ref, rows):
    tail = pl.ds(rows, 16)
    return ref[tail, 0:128].astype(F32) + ref[tail, 128:256].astype(F32)


def add_far(part, got, gains, o_ref, gains_ref):
    rows = part.shape[0]
    o_ref[pl.ds(0, rows), :] = (part[...].astype(F32) + got[pl.ds(0, rows), :].astype(F32)).astype(BF)
    gains_ref[...] = write_gains(o_ref, rows, gains[...] + read_gains(got, rows))


def add_out(kept, got, gains, s0, s1, s2, own, gains_ref):
    rows = own.shape[0]
    high, low = halves_of(gains[...])
    for i, ref in enumerate((s0, s1, s2)):
        ref[pl.ds(0, rows), :] = (kept[i].astype(F32) + got[i].astype(F32)).astype(BF)
        ref[pl.ds(rows, 16), :] = high
        ref[pl.ds(rows + 16, 16), :] = low
    own[...] = kept[3].astype(F32) + got[3].astype(F32)
    gains_ref[...] = high.astype(F32) + low.astype(F32)


def end_out(own, r0, r1, r2, gains, o_ref, gains_ref):
    rows = own.shape[0]
    total = own[...]
    parts = []
    for r in (r0, r1, r2):
        total = total + r[pl.ds(0, rows), :].astype(F32)
        parts.append(r[pl.ds(rows, 16), :].astype(F32) + r[pl.ds(rows + 16, 16), :].astype(F32))
    o_ref[...] = total
    gains_ref[...] = (gains[...] + parts[2]) + (parts[0] + parts[1])


def normed_back(n_pieces, piece_rows, refs):
    offs, gain, gain_two, norms, pg_in = refs[0], refs[1], refs[2], refs[3:7], refs[7]
    pieces = refs[8 : 8 + n_pieces]
    refs = refs[8 + n_pieces :]
    parts, gain_ref = refs[0:4], refs[4]
    n, pg, w, sem_w, sem = refs[5:]
    loads = start_pieces([x.at[pl.ds(0, 3)] for x in pieces], offs, piece_rows, w, sem_w, 1)
    loads.append(start(pg_in, pg, sem.at[4]))
    late = [start(norms[i], n.at[i], sem.at[i]) for i in range(4)]
    wait(loads)
    wait(late)
    rows = n.shape[1]
    sums = None
    for i in (3, 2, 1, 0):
        at = pl.ds(i * rows, rows)
        total = mm(pg[0, at, :], w[0], NT) + mm(pg[1, at, :], w[1], NT) + mm(pg[2, at, :], w[2], NT)
        parts[i][pl.ds(0, rows), :] = total.astype(BF)
        part = jnp.sum(total * n[i].astype(F32), axis=0, keepdims=True)
        sums = part if sums is None else sums + part
    sums = sums / gain[...]
    both = [sums[:, 128 * i : 128 * i + 128] for i in range(8)] + [gain_two[...]]
    gain_ref[...] = write_gains(parts[3], rows, jnp.concatenate(both, axis=0))


def input_back(h, mg, gain, sa, sb, sc, o_ref):
    got = sa[...].astype(F32) + sb[...].astype(F32) + sc[pl.ds(0, sa.shape[0]), :].astype(F32)
    back, _ = norm_back(h[...].astype(F32), gain[...] * got)
    o_ref[...] = mg[...] + back


def body(function, *static):
    return lambda *refs: function(*static, refs)


def angle_table(length):
    exponents = np.arange(0, HD, 2).astype(np.float32) / np.float32(HD)
    inverse = np.float32(ROPE_BASE) ** (-exponents)
    angles = np.arange(length).astype(np.float32)[:, None] * inverse[None, :]
    cos, sin = np.cos(angles), np.sin(angles)
    return np.concatenate([cos, cos, sin, sin], axis=1).astype(np.float32)


def shards(sizes, *args):
    hidden_in, attn_gain, qkv_weight, out_weight, mlp_gain, in_weight, down_weight, cotangent = args
    dp, tp = sizes
    rows, model = hidden_in.shape
    length = rows * tp
    piece_rows = qkv_weight.shape[1]
    width = qkv_weight.shape[2]
    units = in_weight.shape[2]
    scale = HD ** (-0.5)
    direct = dp == 8
    mine_one = lax.axis_index("tensor").astype(jnp.int32).reshape(1)
    place = lax.axis_index("dp")
    gain_one, gain_two = attn_gain.reshape(1, model), mlp_gain.reshape(1, model)

    def tensor(value, k, label):
        return swap(value, "tensor", tp, k, f"{label}_t{k}")

    def depth(value, k, label):
        return swap(value, "dp", dp, k, f"{label}_d{k}")

    def gather(shard, axis, label):
        if direct:
            along = [shard] + [depth(shard, 2 * k, label) for k in (1, 2, 3)]
            across = [depth(v, 1, f"{label}{i}") for i, v in enumerate(along)]
            return [v for pair in zip(along, across) for v in pair]
        return [lax.all_gather(shard, "dp", axis=axis, tiled=True)]

    def only_direct(values):
        return values if direct else []

    if direct:
        offs = place ^ jnp.arange(8, dtype=jnp.int32)
        n_pieces, piece = 8, piece_rows
        z, y = place // 2, place % 2
        order = [2, 3, 1, 0]
        cols = jnp.stack([c for b in order for c in ((z ^ b) * 2 + (1 - y), (z ^ b) * 2 + y)])
    else:
        offs = jnp.zeros((1,), jnp.int32)
        n_pieces, piece = 1, model
        cols = jnp.arange(8, dtype=jnp.int32)
    cols = cols.astype(jnp.int32)
    sems = lambda *s: pltpu.SemaphoreType.DMA(s)
    add = lambda a, b: (a.astype(F32) + b.astype(F32)).astype(BF)

    def spread(own, label):
        far = tensor(own, 2, label)
        return [own, tensor(own, 1, label), far, tensor(far, 1, label + "far")]

    def exchange(blocks, label):
        return [blocks[0]] + [tensor(blocks[k], k, label) for k in (1, 2, 3)]

    def reduce(blocks, axis, label):
        if not direct:
            whole = jnp.concatenate(blocks, axis=axis)
            return lax.psum_scatter(whole, "dp", scatter_dimension=axis, tiled=True).astype(F32)
        got = [depth(blocks[2 * i], 1, f"{label}{i}") for i in range(4)]
        total = [add(blocks[2 * i + 1], got[i]) for i in range(3)]
        back = [depth(total[i], 2 * order[i], label) for i in range(3)]
        own = blocks[7].astype(F32) + got[3].astype(F32)
        return own + back[0].astype(F32) + back[1].astype(F32) + back[2].astype(F32)

    near = lambda *xs: [(x, vmem()) for x in xs]
    away = lambda xs: [(x, hbm()) for x in xs]
    scalar = lambda *xs: [(x, smem()) for x in xs]
    vm = lambda shape, dtype=BF: (shape, dtype, vmem())
    hb = lambda shape, dtype=BF: (shape, dtype, hbm())
    buf = lambda *shape, dtype=BF: pltpu.VMEM(shape, dtype)

    shard, mlp_shard = call(
        pack_body,
        near(qkv_weight, out_weight, in_weight.transpose(0, 2, 1), down_weight),
        [vm((4, piece_rows, width)), vm((3, units, piece_rows))],
        name="pack",
    )
    qkvo = gather(shard, 1, "qkvo")
    (normed,) = call(norm_body, near(hidden_in, gain_one), [vm((rows, model))], name="norm")
    normed_attn = spread(normed, "norm")
    table = jnp.asarray(angle_table(length))
    if direct:
        (mlp_along,) = gate([mlp_shard], [qkvo[4], qkvo[6]])
        (mlp_across,) = gate([mlp_shard], [qkvo[5], qkvo[7]])
        z1, z2 = [depth(mlp_along, 2 * k, "mlp") for k in (1, 2)]
        (cotangent_there,) = gate([cotangent], [normed_attn[2]])
    else:
        cotangent_there = cotangent
    cot = spread(cotangent_there, "cot")
    (out_own,) = call(
        body(assemble_out, n_pieces, piece),
        scalar(offs) + away(gate(qkvo[:1], [z1] if direct else []) + qkvo[1:]),
        [vm((model, width))],
        [sems(n_pieces)],
        name="assemble_out",
    )
    out_all = spread(out_own, "outw")
    if direct:
        z3 = depth(gate([mlp_along], [z1])[0], 6, "mlp")
        y0, y1, y2 = [depth(x, 1, f"mlp{i}") for i, x in enumerate((mlp_across, z1, z2))]
        before = [z2, y0]
    else:
        mlp, before = gather(mlp_shard, 2, "mlp"), []
    *mixed, q, k, v, lse = call(
        body(attend_forward, n_pieces, piece, scale),
        scalar(offs, mine_one)
        + away(gate(normed_attn, before + out_all[1:2]))
        + away([table] + qkvo),
        [vm((rows, width))] * 4 + [hb((length, width))] * 3 + [vm((8, length), F32)],
        [buf(4, rows, model), buf(length, 128, dtype=F32), buf(3, model, width)]
        + [buf(length, width)] * 3
        + [sems(n_pieces), sems(8)],
        name="attend_forward",
    )
    mixed_own = exchange(mixed, "mixed")
    if direct:
        y3 = depth(gate([z3], [lse])[0], 1, "mlp3")
        before = [y1, y2, z3]
        mlp = [mlp_shard, y0, z1, y1, z2, y2, z3, y3]
    middle, normed_two = call(
        project_out,
        near(hidden_in, gain_two, *gate(mixed_own, before), *out_all),
        [vm((rows, model), F32), vm((rows, model))],
        name="project_out",
    )

    normed_far = tensor(normed_two, 2, "norm2")
    (normed_relay,) = gate([normed_far], only_direct(mlp[7:]))
    normed_mlp = [normed_two, tensor(normed_two, 1, "norm2"), normed_far, tensor(normed_relay, 1, "norm2far")]
    far_back, far_send, far_out, far_out_send, far_hidden, far_grad = call(
        body(feed_far, n_pieces, piece),
        scalar(offs) + away(normed_mlp[2:] + cot[2:] + mlp),
        [vm((rows, model))] * 4 + [vm((2 * rows, units)), vm((2, 2 * rows, units))],
        [buf(2, rows, model)] * 2 + [buf(3, units, model), sems(3, n_pieces), sems(4)],
        name="feed_far",
    )
    far_sum = add(far_back, tensor(far_send, 1, "far"))
    from_far = tensor(far_sum, 2, "far")
    near_back, near_send, near_out, near_out_send, near_hidden, near_grad, *grads = call(
        body(feed_near, n_pieces, piece),
        scalar(offs, cols)
        + away(gate(normed_mlp, [far_sum]) + cot + [far_hidden, far_grad] + mlp),
        [vm((rows, model))] * 4
        + [vm((2 * rows, units)), vm((2, 2 * rows, units))]
        + [vm((3, units, 128))] * 4,
        [buf(4, rows, model)] * 2
        + [buf(2 * rows, units), buf(2, 2 * rows, units)]
        + [buf(3, units, model), sems(3, n_pieces), sems(10)],
        name="feed_near",
    )
    near_got = tensor(near_send, 1, "near")
    out_sum = add(far_out, tensor(far_out_send, 1, "lofar"))
    out_near = tensor(near_out_send, 1, "lonear")

    middle_grad, low_grad, x0, x1, x2, x3, gain_two_part = call(
        middle_back,
        near(middle, cotangent, gain_two, near_back, near_got, from_far, *out_all),
        [vm((rows, model), F32), vm((rows, model))] + [vm((rows, width))] * 4 + [vm((8, 128), F32)],
        name="middle_back",
    )
    mixed_grad = exchange([x0, x1, x2, x3], "mgrad")
    attn_out_grad = spread(low_grad, "aog")
    grads += call(
        body(feed_late),
        scalar(cols)
        + away(gate(normed_mlp, [low_grad, out_sum, out_near]) + cot + [near_hidden, far_hidden, near_grad, far_grad]),
        [vm((3, units, 128))] * 4,
        [buf(4, rows, model)] * 2
        + [buf(2 * rows, units)] * 2
        + [buf(2, 2 * rows, units)] * 2
        + [sems(12)],
        name="feed_late",
    )
    early = list(grads[7:])
    if direct:
        grads[0], grads[2] = gate([grads[0], grads[2]], [from_far])
        grads[4], grads[6] = gate([grads[4], grads[6]], mixed_grad)
        got = [depth(grads[2 * i], 1, f"gmlp{i}") for i in range(4)]
        early += [add(grads[2 * i + 1], got[i]) for i in range(2)]
        back = [depth(early[1 + i], 2 * order[i], "gmlp") for i in range(2)]

    *attn, pg = call(
        body(attend_backward, scale),
        scalar(cols, mine_one)
        + away(gate(mixed_grad, early) + mixed + [q, k, v, lse, table] + normed_attn),
        [vm((3, 128, width))] * 8 + [hb((3, length, width))],
        [buf(3, length, width)]
        + [buf(length, width)] * 5
        + [buf(8, length, dtype=F32), buf(length, 128, dtype=F32), buf(4, rows, model)]
        + [buf(8, length, dtype=F32), buf(length, width, dtype=F32), sems(18)],
        name="attend_backward",
    )
    qkv_shard = reduce(attn, 1, "gqkv")
    if direct:
        (pg,) = gate([pg], [back[0], back[1], got[2], got[3]])
    b0, b1, b2, b3, gains = call(
        body(normed_back, n_pieces, piece),
        scalar(offs) + near(gain_one, gain_two_part) + away(normed_attn + [pg] + qkvo),
        [vm((rows, model))] * 3 + [vm((rows + 16, model)), vm((16, 128), F32)],
        [buf(4, rows, model), buf(3, length, width), buf(3, model, width), sems(n_pieces), sems(5)],
        name="normed_back",
    )
    near_sum = tensor(b1, 1, "nnear")
    sent_far, gains = call(
        add_far,
        near(b2, tensor(b3, 1, "nfar"), gains),
        [vm((rows + 16, model)), vm((16, 128), F32)],
        name="add_far",
    )
    got_far = tensor(sent_far, 2, "nfar")
    gains = gains + (got_far[rows:, 0:128].astype(F32) + got_far[rows:, 128:256].astype(F32))
    (input_grad,) = call(
        input_back,
        near(hidden_in, middle_grad, gain_one, b0, near_sum, got_far),
        [vm((rows, model), F32)],
        name="input_back",
    )

    out_sent, out_kept = call(
        body(out_grads),
        scalar(cols) + near(*attn_out_grad, *gate(mixed, [sent_far])),
        [vm((4, width, 128))] * 2,
        name="out_grads",
    )
    if direct:
        out_got = depth(out_sent, 1, "gout")
        gains = gains + depth(gains, 1, "gain")
        *sent, own, gains = call(
            add_out,
            near(out_kept, out_got, gains),
            [vm((width + 32, 128))] * 3 + [vm((width, 128), F32), vm((16, 128), F32)],
            name="add_out",
        )
        out_back = [depth(sent[i], 2 * order[i], "gout") for i in range(3)]
        out_shard, gains = call(
            end_out,
            near(own, *out_back, gains),
            [vm((width, 128), F32), vm((16, 128), F32)],
            name="end_out",
        )
    else:
        halves = [x[i] for i in range(4) for x in (out_sent, out_kept)]
        out_shard = reduce(halves, 1, "gout")
        gains = lax.psum(gains, "dp")
    gains = gains.reshape(2, model)

    if direct:
        late = add(gate([grads[5]], [b3])[0], got[2])
        back.append(depth(late, 2 * order[2], "gmlp"))
        mlp_total = grads[7].astype(F32) + got[3].astype(F32)
        mlp_total += back[0].astype(F32) + back[1].astype(F32) + back[2].astype(F32)
    else:
        mlp_total = reduce(grads, 2, "gmlp")
    in_shard, down_shard = mlp_total[0:2].transpose(0, 2, 1), mlp_total[2]

    out_far = tensor(gate([out_sum], [got_far])[0], 2, "lofar")
    out_near = near_out.astype(F32) + out_near.astype(F32)
    layer_out = (middle + (out_near + out_far.astype(F32))).astype(BF)
    return (layer_out, input_grad, gains[0], qkv_shard, out_shard, gains[1], in_shard, down_shard)


def solution(mesh):
    sizes = (mesh.shape["dp"], mesh.shape["tensor"])
    return jax.shard_map(
        functools.partial(shards, sizes),
        mesh=mesh,
        in_specs=(
            P(("dp", "tensor"), None),
            P(),
            P(None, "dp", "tensor"),
            P("tensor", "dp"),
            P(),
            P(None, "dp", "tensor"),
            P("tensor", "dp"),
            P(("dp", "tensor"), None),
        ),
        out_specs=(
            P(("dp", "tensor"), None),
            P(("dp", "tensor"), None),
            P(),
            P(None, "dp", "tensor"),
            P("tensor", "dp"),
            P(),
            P(None, "dp", "tensor"),
            P("tensor", "dp"),
        ),
        check_vma=False,
    )
```

```python
import functools
import math

import jax
import jax.numpy as jnp
import numpy as np
from jax import lax
from jax.experimental import pallas as pl
from jax.experimental.pallas import tpu as pltpu
from jax.sharding import PartitionSpec as P

HD = 64
NORM_EPS = 1e-05
ROPE_BASE = 160000.0
BF = jnp.bfloat16
F32 = jnp.float32
LOG2E = math.log2(math.e)
COST = 1000
VMEM_MIB = 56

NN = (((1,), (0,)), ((), ()))
NT = (((1,), (1,)), ((), ()))
TN = (((0,), (0,)), ((), ()))


def mm(a, b, dims=NN):
    return lax.dot_general(a, b, dims, preferred_element_type=F32)


def vmem():
    return pl.BlockSpec(memory_space=pltpu.VMEM)


def smem():
    return pl.BlockSpec(memory_space=pltpu.SMEM)


def hbm():
    return pl.BlockSpec(memory_space=pltpu.HBM)


def call(body, ins, outs, scratch=(), name=None):
    return pl.pallas_call(
        body,
        out_shape=[jax.ShapeDtypeStruct(o[0], o[1]) for o in outs],
        in_specs=[i[1] for i in ins],
        out_specs=[o[2] for o in outs],
        scratch_shapes=list(scratch),
        compiler_params=pltpu.CompilerParams(vmem_limit_bytes=VMEM_MIB * 1024 * 1024),
        cost_estimate=pl.CostEstimate(flops=COST, transcendentals=0, bytes_accessed=COST),
        name=name,
    )(*[i[0] for i in ins])


def swap(value, axis, size, distance, label):
    with jax.named_scope(label):
        return lax.ppermute(value, axis, [(i, i ^ distance) for i in range(size)])


def gate(values, others):
    return list(lax.optimization_barrier((tuple(values), tuple(others)))[0])


def start(source, target, sem):
    copy = pltpu.make_async_copy(source, target, sem)
    copy.start()
    return copy


def start_pieces(pieces, offs, size, target, sem, axis):
    copies = []
    for i, piece in enumerate(pieces):
        where = pl.ds(pl.multiple_of(offs[i] * size, size), size)
        copies.append(start(piece, target.at[(slice(None),) * axis + (where,)], sem.at[i]))
    return copies


def wait(copies):
    for c in copies:
        c.wait()


def angles_at(table, block, rows):
    both = table[pl.ds(pl.multiple_of(block * rows, rows), rows), :]
    other = pltpu.roll(both, 64, 1)
    lane = lax.broadcasted_iota(jnp.int32, both.shape, 1)
    cos = jnp.where(lane < 64, both, other)
    sin = jnp.where(lane < 64, other, both)
    return cos, jnp.where((lane & 63) < 32, -sin, sin)


def turn(u, cos, sin):
    lane = lax.broadcasted_iota(jnp.int32, u.shape, 1)
    low = (lane & 63) < 32
    turned = jnp.where(low, pltpu.roll(u, 96, 1), pltpu.roll(u, 32, 1))
    return u * cos + turned * sin


def head_mask(shape, head):
    lane = lax.broadcasted_iota(jnp.int32, shape, 1)
    return (lane >> 6) == head


def attend_forward(n_pieces, piece_rows, scale, refs):
    offs, mine = refs[:2]
    norms, table = refs[2:6], refs[6]
    pieces = refs[7 : 7 + n_pieces]
    refs = refs[7 + n_pieces :]
    parts, (mixed_out, q_out, k_out, v_out, lse_ref) = refs[0:4], refs[4:9]
    n, tab, w, q, k, v, mixed, sem_w, sem = refs[9:]
    rows, width = n.shape[1], w.shape[2]
    loads = start_pieces(pieces, offs, piece_rows, w, sem_w, 1)
    norm_loads = [start(norms[i], n.at[i], sem.at[i]) for i in range(4)]
    table_load = start(table, tab, sem.at[4])
    wait(loads)
    table_load.wait()
    for i in range(4):
        at = pl.ds(i * rows, rows)
        cos, sin = angles_at(tab, mine[0] ^ i, rows)
        norm_loads[i].wait()
        for j, ref in ((0, q), (1, k)):
            u = mm(n[i], w[j])
            for g in range(width // 128):
                col = slice(g * 128, g * 128 + 128)
                ref[at, col] = turn(u[:, col], cos, sin).astype(BF)
        v[at, :] = mm(n[i], w[2]).astype(BF)
    stores = [start(x, y, sem.at[5 + i]) for i, (x, y) in enumerate(((q, q_out), (k, k_out), (v, v_out)))]
    factor = scale * LOG2E
    heads = width // HD
    group = 2 * rows
    for half in range(2):
        at = pl.ds(half * group, group)
        masks = [head_mask((group, width), h) for h in range(heads)]

        def scores(h):
            return mm(jnp.where(masks[h], q[at, :], jnp.zeros((), BF)), k[...], NT)

        acc = jnp.zeros((group, width), F32)
        s = scores(0)
        for h in range(heads):
            ahead = scores(h + 1) if h + 1 < heads else None
            top = jnp.max(s, axis=1, keepdims=True)
            e = jnp.exp2((s - top) * factor)
            total = jnp.sum(e, axis=1, keepdims=True)
            o = mm(e.astype(BF), v[...]) * (1.0 / total)
            lse2 = top * factor + jnp.log2(total)
            row = jnp.transpose(jnp.broadcast_to(lse2, (group, 128)))
            lse_ref[pl.ds(h, 1), at] = row[0:1, :]
            acc = jnp.where(masks[h], o, acc)
            s = ahead
        low = acc.astype(BF)
        mixed[at, :] = low
        part = mm(low, w[3], NT).astype(BF)
        parts[2 * half][...] = part[:rows]
        parts[2 * half + 1][...] = part[rows:]
    stores.append(start(mixed, mixed_out, sem.at[8]))
    wait(stores)


def norm_stats(v):
    mean = jnp.mean(v, axis=-1, keepdims=True)
    centred = v - mean
    spread = jnp.mean(centred * centred, axis=-1, keepdims=True)
    r = lax.rsqrt(spread + NORM_EPS)
    return centred * r, r


def norm_body(h_ref, gain_ref, o_ref):
    xhat, _ = norm_stats(h_ref[...].astype(F32))
    o_ref[...] = (xhat * gain_ref[...]).astype(BF)


def pack_body(qkv, out, inner, down, first, second):
    first[0:3] = qkv[...]
    first[3] = out[...].T
    second[0:2] = inner[...]
    second[2] = down[...]


def middle_rows(h_ref, gain, a, b, c, mid_ref, norm_ref):
    total = h_ref[...].astype(F32) + (a[...].astype(F32) + b[...].astype(F32) + c[...].astype(F32))
    mid_ref[...] = total
    xhat, _ = norm_stats(total)
    norm_ref[...] = (xhat * gain[...]).astype(BF)


INV_SQRT2 = 1.0 / math.sqrt(2.0)
INV_SQRT2PI = 1.0 / math.sqrt(2.0 * math.pi)


def feed_rows(n, c, w, grads, outs, hid, gug):
    rows = n.shape[1]
    products = [(mm(n[i], w[0], NT), mm(n[i], w[1], NT), mm(c[i], w[2], NT)) for i in range(2)]
    for i, (gate, up, back) in enumerate(products):
        at = pl.ds(i * rows, rows)
        cdf = 0.5 * (1.0 + lax.erf(gate * INV_SQRT2))
        pdf = jnp.exp(-0.5 * gate * gate) * INV_SQRT2PI
        act = gate * cdf
        hidden = (act * up).astype(BF)
        g0 = (back * up * (cdf + gate * pdf)).astype(BF)
        g1 = (back * act).astype(BF)
        grads[i][...] = (mm(g0, w[0]) + mm(g1, w[1])).astype(BF)
        outs[i][...] = mm(hidden, w[2]).astype(BF)
        hid[:, at] = hidden.T
        gug[0, :, at] = g0.T
        gug[1, :, at] = g1.T


def load_mlp(pieces, offs, size, w, sem):
    return [
        start_pieces([x.at[j] for x in pieces], offs, size, w.at[j], sem.at[j], 1) for j in range(3)
    ]


def feed_far(n_pieces, size, refs):
    offs, n_in, c_in, pieces = refs[0], refs[1:3], refs[3:5], refs[5 : 5 + n_pieces]
    grads, outs, (hid, gug), (n, c, w, sem_w, sem) = (
        refs[5 + n_pieces : 7 + n_pieces],
        refs[7 + n_pieces : 9 + n_pieces],
        refs[9 + n_pieces : 11 + n_pieces],
        refs[11 + n_pieces :],
    )
    loads = [start(n_in[i], n.at[i], sem.at[i]) for i in range(2)]
    loads += [start(c_in[i], c.at[i], sem.at[2 + i]) for i in range(2)]
    for group in load_mlp(pieces, offs, size, w, sem_w):
        wait(group)
    wait(loads)
    feed_rows(n, c, w, grads, outs, hid, gug)


def pick_columns(ref, first, second, size):
    a = ref[:, pl.ds(pl.multiple_of(first * size, size), size)]
    b = ref[:, pl.ds(pl.multiple_of(second * size, size), size)]
    return jnp.concatenate([a, b], axis=1)


def mlp_grads(cols, blocks, n, c, hidden, grads, outs):
    group = hidden[0].shape[1]
    for k, block in enumerate(blocks):
        first, second = cols[2 * block], cols[2 * block + 1]
        rights = [pick_columns(x, first, second, 128) for x in (n, c)]
        for j in range(3):
            left = hidden if j == 2 else [x.at[j] for x in grads]
            right = rights[1] if j == 2 else rights[0]
            total = mm(left[0][...], right[:group]) + mm(left[1][...], right[group:])
            outs[2 * k][j] = total[:, :128].astype(BF)
            outs[2 * k + 1][j] = total[:, 128:].astype(BF)


def start_rows(sources, target, sem, at):
    rows = sources[0].shape[0]
    return [start(x, target.at[pl.ds(i * rows, rows)], sem.at[at + i]) for i, x in enumerate(sources)]


class Halves:
    def __init__(self, ref, rows):
        self.ref, self.shape = ref, (2, rows, ref.shape[1])

    def __getitem__(self, i):
        return self.ref[pl.ds(i * self.shape[1], self.shape[1]), :]


def feed_near(n_pieces, size, refs):
    offs, cols, n_in, c_in, hid_far, gug_far = refs[0], refs[1], refs[2:6], refs[6:10], refs[10], refs[11]
    pieces = refs[12 : 12 + n_pieces]
    refs = refs[12 + n_pieces :]
    grads, outs, (hid, gug), blocks = refs[0:2], refs[2:4], refs[4:6], refs[6:10]
    n, c, hf, gf, w, sem_w, sem = refs[10:]
    loads = start_rows(n_in, n, sem, 0)[:2]
    groups = load_mlp(pieces, offs, size, w, sem_w)
    rows = n_in[0].shape[0]
    more = start_rows(c_in, c, sem, 4)
    late = [start(hid_far, hf, sem.at[8]), start(gug_far, gf, sem.at[9])]
    for group in groups:
        wait(group)
    wait(loads)
    wait(more)
    feed_rows(Halves(n, rows), Halves(c, rows), w, grads, outs, hid, gug)
    for i in (2, 3):
        pltpu.make_async_copy(n_in[i], n.at[pl.ds(i * rows, rows)], sem.at[i]).wait()
    wait(late)
    mlp_grads(cols, (0, 1), n, c, (hid, hf), (gug, gf), blocks)


def feed_late(refs):
    cols, n_in, c_in = refs[0], refs[1:5], refs[5:9]
    sources, blocks = refs[9:13], refs[13:17]
    n, c, hn, hf, gn, gf, sem = refs[17:]
    loads = start_rows(n_in, n, sem, 0)
    loads += [start(x, y, sem.at[8 + i]) for i, (x, y) in enumerate(zip(sources, (hn, hf, gn, gf)))]
    loads += start_rows(c_in, c, sem, 4)
    wait(loads)
    mlp_grads(cols, (2, 3), n, c, (hn, hf), (gn, gf), blocks)


def norm_back(v, g):
    xhat, r = norm_stats(v)
    mean_g = jnp.mean(g, axis=-1, keepdims=True)
    mean_gx = jnp.mean(g * xhat, axis=-1, keepdims=True)
    return r * (g - mean_g - xhat * mean_gx), xhat


def middle_back(mid, cot, gain, sa, sb, sc, mg_ref, low_ref, gain_ref):
    got = sa[...].astype(F32) + sb[...].astype(F32) + sc[...].astype(F32)
    back, xhat = norm_back(mid[...], gain[...] * got)
    sums = jnp.sum(got * xhat, axis=0, keepdims=True)
    for i in range(8):
        gain_ref[pl.ds(i, 1), :] = sums[:, 128 * i : 128 * i + 128]
    mg = cot[...].astype(F32) + back
    mg_ref[...] = mg
    low_ref[...] = mg.astype(BF)


def attend_backward(n_pieces, piece_rows, scale, refs):
    cols, mine, offs, gain, gain_two = refs[:5]
    refs = refs[5:]
    grads_in, mixed_in, q_in, k_in, v_in, lse_in, table, norms = (
        refs[0:4], refs[4], refs[5], refs[6], refs[7], refs[8], refs[9], refs[10:14]
    )
    pieces = refs[14 : 14 + n_pieces]
    refs = refs[14 + n_pieces :]
    outs, parts, gain_ref = refs[0:8], refs[8:12], refs[12]
    pg, do, o, q, k, v, lse, tab, n, a, dot_rows, dq, w, sem_w, sem = refs[13:]
    rows = grads_in[0].shape[0]
    length, width = q.shape
    heads = width // HD
    weights = start_pieces(pieces, offs, piece_rows, w, sem_w, 1)
    grads = start_rows(grads_in, a, sem, 0)
    pairs = ((mixed_in, o), (q_in, q), (k_in, k), (v_in, v), (lse_in, lse))
    near = [start(x, y, sem.at[4 + i]) for i, (x, y) in enumerate(pairs)]
    late = [start(table, tab, sem.at[12])]
    late += start_rows(norms, n, sem, 13)
    wait(weights)
    for i in range(4):
        grads[i].wait()
        at = pl.ds(i * rows, rows)
        do[at, :] = mm(a[at, :], w[3]).astype(BF)
    wait(near)
    lane = lax.broadcasted_iota(jnp.int32, (8, width), 1) >> 6
    head = lax.broadcasted_iota(jnp.int32, (8, width), 0)
    ones = jnp.where(lane == head, 1.0, 0.0).astype(BF)
    for i in range(4):
        at = pl.ds(i * rows, rows)
        t = do[at, :].astype(F32) * o[at, :].astype(F32)
        hi = t.astype(BF)
        lo = (t - hi.astype(F32)).astype(BF)
        dot_rows[:, at] = mm(ones, hi, NT) + mm(ones, lo, NT)
    dq[...] = jnp.zeros_like(dq)
    factor = scale * LOG2E
    nil = jnp.zeros((), BF)

    def one_block(i, carry):
        at = pl.ds(pl.multiple_of(i * rows, rows), rows)
        dk_acc = jnp.zeros((rows, width), F32)
        dv_acc = jnp.zeros((rows, width), F32)
        dq_acc = None
        for h in range(heads):
            mask = head_mask((length, width), h)
            qm = jnp.where(mask, q[...], nil)
            dom = jnp.where(mask, do[...], nil)
            km = jnp.where(head_mask((rows, width), h), k[at, :], nil)
            s = mm(k[at, :], qm, NT)
            dp = mm(v[at, :], dom, NT)
            p = jnp.exp2(s * factor - lse[pl.ds(h, 1), :])
            ds = (p * (dp - dot_rows[pl.ds(h, 1), :])).astype(BF)
            dv_acc = dv_acc + mm(p.astype(BF), dom)
            dk_acc = dk_acc + mm(ds, qm)
            part = mm(ds, km, TN)
            dq_acc = part if dq_acc is None else dq_acc + part
        dq[...] += dq_acc
        cos, sin = angles_at(tab, mine[0] ^ i, rows)
        for g in range(width // 128):
            col = slice(g * 128, g * 128 + 128)
            to = slice(width + g * 128, width + g * 128 + 128)
            pg[at, to] = turn(dk_acc[:, col] * scale, cos, -sin).astype(BF)
        pg[at, 2 * width :] = dv_acc.astype(BF)
        return carry

    wait(late[:1])
    lax.fori_loop(0, 4, one_block, 0)
    for i in range(4):
        at = pl.ds(i * rows, rows)
        cos, sin = angles_at(tab, mine[0] ^ i, rows)
        for g in range(width // 128):
            col = slice(g * 128, g * 128 + 128)
            pg[at, col] = turn(dq[at, col] * scale, cos, -sin).astype(BF)
    wait(late[1:])
    for block in range(4):
        first, second = cols[2 * block], cols[2 * block + 1]
        total = mm(pick_columns(n, first, second, 128), pg[...], TN)
        for j in range(3):
            part = total[:, j * width : (j + 1) * width].astype(BF)
            outs[2 * block][j] = part[:128]
            outs[2 * block + 1][j] = part[128:]
        part = mm(pick_columns(a, first, second, 128), o[...], TN).astype(BF)
        outs[2 * block][3] = part[:128]
        outs[2 * block + 1][3] = part[128:]
    sums = None
    for i in range(4):
        at = pl.ds(i * rows, rows)
        total = sum(mm(pg[at, j * width : (j + 1) * width], w[j], NT) for j in range(3))
        parts[i][pl.ds(0, rows), :] = total.astype(BF)
        part = jnp.sum(total * n[at, :].astype(F32), axis=0, keepdims=True)
        sums = part if sums is None else sums + part
    sums = sums / gain[...]
    both = [sums[:, 128 * i : 128 * i + 128] for i in range(8)] + [gain_two[...]]
    gain_ref[...] = write_gains(parts[3], rows, jnp.concatenate(both, axis=0))


def write_gains(ref, rows, gains):
    high = gains.astype(BF)
    low = (gains - high.astype(F32)).astype(BF)
    tail = pl.ds(rows, 16)
    ref[tail, :] = jnp.zeros((16, ref.shape[1]), BF)
    ref[tail, 0:128] = high
    ref[tail, 128:256] = low
    return high.astype(F32) + low.astype(F32)


def read_gains(ref, rows):
    tail = pl.ds(rows, 16)
    return ref[tail, 0:128].astype(F32) + ref[tail, 128:256].astype(F32)


def add_far(part, got, gains, o_ref, gains_ref):
    rows = part.shape[0]
    o_ref[pl.ds(0, rows), :] = (part[...].astype(F32) + got[pl.ds(0, rows), :].astype(F32)).astype(BF)
    gains_ref[...] = write_gains(o_ref, rows, gains[...] + read_gains(got, rows))


def input_back(h, mg, gain, sa, sb, sc, gains, o_ref, gains_ref):
    rows = sa.shape[0]
    gains_ref[...] = gains[...] + read_gains(sc, rows)
    got = sa[...].astype(F32) + sb[...].astype(F32) + sc[pl.ds(0, rows), :].astype(F32)
    back, _ = norm_back(h[...].astype(F32), gain[...] * got)
    o_ref[...] = mg[...] + back


def body(function, *static):
    return lambda *refs: function(*static, refs)


def angle_table(length):
    exponents = np.arange(0, HD, 2).astype(np.float32) / np.float32(HD)
    inverse = np.float32(ROPE_BASE) ** (-exponents)
    angles = np.arange(length).astype(np.float32)[:, None] * inverse[None, :]
    cos, sin = np.cos(angles), np.sin(angles)
    return np.concatenate([cos, cos, sin, sin], axis=1).astype(np.float32)


def shards(sizes, *args):
    hidden_in, attn_gain, qkv_weight, out_weight, mlp_gain, in_weight, down_weight, cotangent = args
    dp, tp = sizes
    rows, model = hidden_in.shape
    length = rows * tp
    piece_rows = qkv_weight.shape[1]
    width = qkv_weight.shape[2]
    units = in_weight.shape[2]
    scale = HD ** (-0.5)
    direct = dp == 8
    mine_one = lax.axis_index("tensor").astype(jnp.int32).reshape(1)
    place = lax.axis_index("dp")
    gain_one, gain_two = attn_gain.reshape(1, model), mlp_gain.reshape(1, model)

    def tensor(value, k, label):
        return swap(value, "tensor", tp, k, f"{label}_t{k}")

    def depth(value, k, label):
        return swap(value, "dp", dp, k, f"{label}_d{k}")

    def gather(shard, axis, label):
        if direct:
            far = depth(shard, 4, label)
            along = [shard, depth(shard, 2, label), far, depth(far, 2, label + "far")]
            across = [depth(v, 1, f"{label}{i}") for i, v in enumerate(along)]
            return [v for pair in zip(along, across) for v in pair]
        return [lax.all_gather(shard, "dp", axis=axis, tiled=True)]

    def only_direct(values):
        return values if direct else []

    if direct:
        offs = place ^ jnp.arange(8, dtype=jnp.int32)
        n_pieces, piece = 8, piece_rows
        z, y = place // 2, place % 2
        order = [1, 3, 2, 0]
        cols = jnp.stack([c for b in order for c in ((z ^ b) * 2 + (1 - y), (z ^ b) * 2 + y)])
    else:
        offs = jnp.zeros((1,), jnp.int32)
        n_pieces, piece = 1, model
        cols = jnp.arange(8, dtype=jnp.int32)
    cols = cols.astype(jnp.int32)
    sems = lambda *s: pltpu.SemaphoreType.DMA(s)
    add = lambda a, b: (a.astype(F32) + b.astype(F32)).astype(BF)

    def spread(own, label):
        far = tensor(own, 2, label)
        return [own, tensor(own, 1, label), far, tensor(far, 1, label + "far")]

    def exchange(blocks, label):
        return [blocks[0]] + [tensor(blocks[k], k, label) for k in (1, 2, 3)]

    def reduce(blocks, axis, label):
        whole = jnp.concatenate(blocks, axis=axis)
        return lax.psum_scatter(whole, "dp", scatter_dimension=axis, tiled=True).astype(F32)

    def sum_of(*values):
        return sum(v.astype(F32) for v in values)

    near = lambda *xs: [(x, vmem()) for x in xs]
    away = lambda xs: [(x, hbm()) for x in xs]
    scalar = lambda *xs: [(x, smem()) for x in xs]
    vm = lambda shape, dtype=BF: (shape, dtype, vmem())
    hb = lambda shape, dtype=BF: (shape, dtype, hbm())
    buf = lambda *shape, dtype=BF: pltpu.VMEM(shape, dtype)

    shard, mlp_shard = call(
        pack_body,
        near(qkv_weight, out_weight, in_weight.transpose(0, 2, 1), down_weight),
        [vm((4, piece_rows, width)), vm((3, units, piece_rows))],
        name="pack",
    )
    qkvo = gather(shard, 1, "qkvo")
    (normed,) = call(norm_body, near(hidden_in, gain_one), [vm((rows, model))], name="norm")
    if direct:
        (normed,) = gate([normed], [qkvo[1], qkvo[2], qkvo[4]])
    normed_attn = spread(normed, "norm")
    table = jnp.asarray(angle_table(length))
    if direct:
        (mlp_along,) = gate([mlp_shard], [qkvo[6]])
        (mlp_across,) = gate([mlp_shard], [qkvo[7]])
        z2, z1 = [depth(mlp_along, 2 * k, "mlp") for k in (2, 1)]
        (cotangent_there,) = gate([cotangent], [normed_attn[2]])
    else:
        cotangent_there = cotangent
    cot = spread(cotangent_there, "cot")
    if direct:
        before = []
    else:
        mlp, before = gather(mlp_shard, 2, "mlp"), []
    *parts, mixed, q, k, v, lse = call(
        body(attend_forward, n_pieces, piece, scale),
        scalar(offs, mine_one)
        + away(normed_attn)
        + away([table] + qkvo),
        [vm((rows, model))] * 4 + [hb((length, width))] * 4 + [vm((8, length), F32)],
        [buf(4, rows, model), buf(length, 128, dtype=F32), buf(4, model, width)]
        + [buf(length, width)] * 4
        + [sems(n_pieces), sems(9)],
        name="attend_forward",
    )
    if direct:
        y0 = depth(mlp_across, 1, "mlp0")
        *parts, lse = gate(parts + [lse], [z1, z2, y0])
    attn_far = add(parts[2], tensor(parts[3], 1, "afar"))
    attn_near = tensor(parts[1], 1, "anear")
    attn_got = tensor(attn_far, 2, "afar")
    if direct:
        z3 = depth(gate([z2], [lse])[0], 2, "mlpfar")
        y1, y2, y3 = [depth(gate([x], [lse])[0], 1, f"mlp{i}") for i, x in ((1, z1), (2, z2), (3, z3))]
        before = [y1, z3]
        mlp = [mlp_shard, y0, z1, y1, z2, y2, z3, y3]
    middle, normed_two = call(
        middle_rows,
        near(hidden_in, gain_two, *gate([parts[0]], before), attn_near, attn_got),
        [vm((rows, model), F32), vm((rows, model))],
        name="middle_rows",
    )

    normed_far = tensor(normed_two, 2, "norm2")
    (normed_relay,) = gate([normed_far], only_direct(mlp[5:]))
    normed_mlp = [normed_two, tensor(normed_two, 1, "norm2"), normed_far, tensor(normed_relay, 1, "norm2far")]
    far_back, far_send, far_out, far_out_send, far_hidden, far_grad = call(
        body(feed_far, n_pieces, piece),
        scalar(offs) + away(normed_mlp[2:] + cot[2:] + mlp),
        [vm((rows, model))] * 4 + [vm((units, 2 * rows)), vm((2, units, 2 * rows))],
        [buf(2, rows, model)] * 2 + [buf(3, units, model), sems(3, n_pieces), sems(4)],
        name="feed_far",
    )
    far_sum = add(far_back, tensor(far_send, 1, "far"))
    from_far = tensor(far_sum, 2, "far")
    near_back, near_send, near_out, near_out_send, near_hidden, near_grad, *grads = call(
        body(feed_near, n_pieces, piece),
        scalar(offs, cols)
        + away(gate(normed_mlp, [far_sum]) + cot + [far_hidden, far_grad] + mlp),
        [vm((rows, model))] * 4
        + [vm((units, 2 * rows)), vm((2, units, 2 * rows))]
        + [vm((3, units, 128))] * 4,
        [buf(length, model)] * 2
        + [buf(units, 2 * rows), buf(2, units, 2 * rows)]
        + [buf(3, units, model), sems(3, n_pieces), sems(10)],
        name="feed_near",
    )
    near_got = tensor(near_send, 1, "near")
    out_sum = add(far_out, tensor(far_out_send, 1, "lofar"))
    out_near = tensor(near_out_send, 1, "lonear")

    middle_grad, low_grad, gain_two_part = call(
        middle_back,
        near(middle, cotangent, gain_two, near_back, near_got, from_far),
        [vm((rows, model), F32), vm((rows, model)), vm((8, 128), F32)],
        name="middle_back",
    )
    attn_out_grad = spread(low_grad, "aog")
    grads += call(
        body(feed_late),
        scalar(cols)
        + away(gate(normed_mlp, [low_grad, out_sum, out_near]) + cot + [near_hidden, far_hidden, near_grad, far_grad]),
        [vm((3, units, 128))] * 4,
        [buf(length, model)] * 2
        + [buf(units, 2 * rows)] * 2
        + [buf(2, units, 2 * rows)] * 2
        + [sems(12)],
        name="feed_late",
    )
    early = [grads[7]]
    if direct:
        grads[0], grads[2] = gate([grads[0], grads[2]], [from_far])
        grads[4], grads[6] = gate([grads[4], grads[6]], [attn_out_grad[2]])
        got = [depth(grads[2 * i], 1, f"gmlp{i}") for i in range(4)]
        sums = [add(grads[2 * i + 1], got[i]) for i in range(2)]
        early.append(sums[0])
        back = [depth(sums[i], 2, f"gmlpz{i}") for i in range(2)]

    *attn, b0, b1, b2, b3, gains = call(
        body(attend_backward, n_pieces, piece, scale),
        scalar(cols, mine_one, offs)
        + near(gain_one, gain_two_part)
        + away(gate(attn_out_grad, early) + [mixed, q, k, v, lse, table] + normed_attn + qkvo),
        [vm((4, 128, width))] * 8
        + [vm((rows, model))] * 3
        + [vm((rows + 16, model)), vm((16, 128), F32)],
        [buf(length, 3 * width)]
        + [buf(length, width)] * 5
        + [buf(8, length, dtype=F32), buf(length, 128, dtype=F32), buf(length, model), buf(length, model)]
        + [buf(8, length, dtype=F32), buf(length, width, dtype=F32)]
        + [buf(4, model, width), sems(n_pieces), sems(17)],
        name="attend_backward",
    )
    if direct:
        late = sum_of(gate([grads[5]], [b0])[0], got[2], back[1]).astype(BF)
        last = depth(late, 4, "gmlp")
        *attn, b3 = gate(attn + [b3], [late, back[0], got[3]])
        gqkv = [depth(attn[2 * i], 1, f"gqkv{i}") for i in range(3)]
        qkv_sums = [add(attn[2 * i + 1], gqkv[i]) for i in range(2)]
        qkv_back = [depth(qkv_sums[i], 2, f"gqkvz{i}") for i in range(2)]
    sent_far, gains = call(
        add_far,
        near(b2, tensor(b3, 1, "nfar"), gains),
        [vm((rows + 16, model)), vm((16, 128), F32)],
        name="add_far",
    )
    got_far = tensor(sent_far, 2, "nfar")
    (b1,) = gate([b1], [sent_far])
    near_sum = tensor(b1, 1, "nnear")
    if direct:
        (b0,) = gate([b0], [last])
    input_grad, gains = call(
        input_back,
        near(hidden_in, middle_grad, gain_one, b0, near_sum, got_far, gains),
        [vm((rows, model), F32), vm((16, 128), F32)],
        name="input_back",
    )
    out_far = tensor(gate([out_sum], [got_far])[0], 2, "lofar")
    out_near = near_out.astype(F32) + out_near.astype(F32)
    layer_out = (middle + (out_near + out_far.astype(F32))).astype(BF)

    if direct:
        (attn[6],) = gate(attn[6:7], [input_grad])
        gains = gains + depth(gains, 1, "gain")
        gains = gains + depth(gains, 2, "gain")
        gains = gains + depth(gains, 4, "gain")
        gqkv.append(depth(attn[6], 1, "gqkv3"))
        qkv_late = sum_of(attn[5], gqkv[2], qkv_back[1]).astype(BF)
        qkv_last = depth(qkv_late, 4, "gqkv")
        attn_total = sum_of(attn[7], gqkv[3], qkv_back[0], gate([qkv_last], [out_far, gains])[0])
    else:
        gains = lax.psum(gains, "dp")
        attn_total = reduce(attn, 1, "gqkv")
    qkv_shard, out_shard = attn_total[0:3], attn_total[3].T
    gains = gains.reshape(2, model)

    if direct:
        mlp_total = sum_of(grads[7], got[3], back[0], gate([last], [input_grad])[0])
    else:
        mlp_total = reduce(grads, 2, "gmlp")
    in_shard, down_shard = mlp_total[0:2].transpose(0, 2, 1), mlp_total[2]

    return (layer_out, input_grad, gains[0], qkv_shard, out_shard, gains[1], in_shard, down_shard)


def solution(mesh):
    sizes = (mesh.shape["dp"], mesh.shape["tensor"])
    return jax.shard_map(
        functools.partial(shards, sizes),
        mesh=mesh,
        in_specs=(
            P(("dp", "tensor"), None),
            P(),
            P(None, "dp", "tensor"),
            P("tensor", "dp"),
            P(),
            P(None, "dp", "tensor"),
            P("tensor", "dp"),
            P(("dp", "tensor"), None),
        ),
        out_specs=(
            P(("dp", "tensor"), None),
            P(("dp", "tensor"), None),
            P(),
            P(None, "dp", "tensor"),
            P("tensor", "dp"),
            P(),
            P(None, "dp", "tensor"),
            P("tensor", "dp"),
        ),
        check_vma=False,
    )
```

```python
import functools
import math

import jax
import jax.numpy as jnp
import numpy as np
from jax import lax
from jax.experimental import pallas as pl
from jax.experimental.pallas import tpu as pltpu
from jax.sharding import PartitionSpec as P

HD = 64
NORM_EPS = 1e-05
ROPE_BASE = 160000.0
BF = jnp.bfloat16
F32 = jnp.float32
LOG2E = math.log2(math.e)
COST = 1000
VMEM_MIB = 56

NN = (((1,), (0,)), ((), ()))
NT = (((1,), (1,)), ((), ()))
TN = (((0,), (0,)), ((), ()))


def mm(a, b, dims=NN):
    return lax.dot_general(a, b, dims, preferred_element_type=F32)


def vmem():
    return pl.BlockSpec(memory_space=pltpu.VMEM)


def smem():
    return pl.BlockSpec(memory_space=pltpu.SMEM)


def hbm():
    return pl.BlockSpec(memory_space=pltpu.HBM)


def call(body, ins, outs, scratch=(), name=None):
    return pl.pallas_call(
        body,
        out_shape=[jax.ShapeDtypeStruct(o[0], o[1]) for o in outs],
        in_specs=[i[1] for i in ins],
        out_specs=[o[2] for o in outs],
        scratch_shapes=list(scratch),
        compiler_params=pltpu.CompilerParams(vmem_limit_bytes=VMEM_MIB * 1024 * 1024),
        cost_estimate=pl.CostEstimate(flops=COST, transcendentals=0, bytes_accessed=COST),
        name=name,
    )(*[i[0] for i in ins])


def swap(value, axis, size, distance, label):
    with jax.named_scope(label):
        return lax.ppermute(value, axis, [(i, i ^ distance) for i in range(size)])


def gate(values, others):
    return list(lax.optimization_barrier((tuple(values), tuple(others)))[0])


def start(source, target, sem):
    copy = pltpu.make_async_copy(source, target, sem)
    copy.start()
    return copy


def start_pieces(pieces, offs, size, target, sem, axis):
    copies = []
    for i, piece in enumerate(pieces):
        where = pl.ds(pl.multiple_of(offs[i] * size, size), size)
        copies.append(start(piece, target.at[(slice(None),) * axis + (where,)], sem.at[i]))
    return copies


def stop_rows(source, targets, sem, at):
    rows = targets[0].shape[0]
    return [
        start(source.at[pl.ds(i * rows, rows)], x, sem.at[at + i]) for i, x in enumerate(targets)
    ]


def wait(copies):
    for c in copies:
        c.wait()


def angles_at(table, block, rows):
    both = table[pl.ds(pl.multiple_of(block * rows, rows), rows), :]
    other = pltpu.roll(both, 64, 1)
    lane = lax.broadcasted_iota(jnp.int32, both.shape, 1)
    cos = jnp.where(lane < 64, both, other)
    sin = jnp.where(lane < 64, other, both)
    return cos, jnp.where((lane & 63) < 32, -sin, sin)


def turn(u, cos, sin):
    lane = lax.broadcasted_iota(jnp.int32, u.shape, 1)
    low = (lane & 63) < 32
    turned = jnp.where(low, pltpu.roll(u, 96, 1), pltpu.roll(u, 32, 1))
    return u * cos + turned * sin


def head_mask(shape, head):
    lane = lax.broadcasted_iota(jnp.int32, shape, 1)
    return (lane >> 6) == head


def attend_forward(n_pieces, piece_rows, scale, refs):
    offs, mine = refs[:2]
    norms, table = refs[2:6], refs[6]
    pieces = refs[7 : 7 + n_pieces]
    refs = refs[7 + n_pieces :]
    parts, (mixed_out, q_out, k_out, v_out, lse_ref) = refs[0:4], refs[4:9]
    n, tab, w, q, k, v, mixed, part, sem_w, sem = refs[9:]
    rows, width = n.shape[1], w.shape[2]
    loads = start_pieces(pieces, offs, piece_rows, w, sem_w, 1)
    norm_loads = [start(norms[i], n.at[i], sem.at[i]) for i in range(4)]
    table_load = start(table, tab, sem.at[4])
    wait(loads)
    table_load.wait()
    wait(norm_loads)

    def project(i, carry):
        at = pl.ds(pl.multiple_of(i * rows, rows), rows)
        cos, sin = angles_at(tab, mine[0] ^ i, rows)
        for j, ref in ((0, q), (1, k)):
            u = mm(n[i], w[j])
            for g in range(width // 128):
                col = slice(g * 128, g * 128 + 128)
                ref[at, col] = turn(u[:, col], cos, sin).astype(BF)
        v[at, :] = mm(n[i], w[2]).astype(BF)
        return carry

    lax.fori_loop(0, 4, project, 0)
    stores = [start(x, y, sem.at[5 + i]) for i, (x, y) in enumerate(((q, q_out), (k, k_out), (v, v_out)))]
    factor = scale * LOG2E
    heads = width // HD
    group = 2 * rows

    def attend(half, carry):
        at = pl.ds(pl.multiple_of(half * group, group), group)
        masks = [head_mask((group, width), h) for h in range(heads)]

        def scores(h):
            return mm(jnp.where(masks[h], q[at, :], jnp.zeros((), BF)), k[...], NT)

        acc = jnp.zeros((group, width), F32)
        s = scores(0)
        for h in range(heads):
            ahead = scores(h + 1) if h + 1 < heads else None
            top = jnp.max(s, axis=1, keepdims=True)
            e = jnp.exp2((s - top) * factor)
            total = jnp.sum(e, axis=1, keepdims=True)
            o = mm(e.astype(BF), v[...]) * (1.0 / total)
            lse2 = top * factor + jnp.log2(total)
            row = jnp.transpose(jnp.broadcast_to(lse2, (group, 128)))
            lse_ref[pl.ds(h, 1), at] = row[0:1, :]
            acc = jnp.where(masks[h], o, acc)
            s = ahead
        low = acc.astype(BF)
        mixed[at, :] = low
        part[at, :] = mm(low, w[3], NT).astype(BF)
        return carry

    lax.fori_loop(0, 2, attend, 0)
    stores.append(start(mixed, mixed_out, sem.at[8]))
    stores += stop_rows(part, parts, sem, 9)
    wait(stores)


def norm_stats(v):
    mean = jnp.mean(v, axis=-1, keepdims=True)
    centred = v - mean
    spread = jnp.mean(centred * centred, axis=-1, keepdims=True)
    r = lax.rsqrt(spread + NORM_EPS)
    return centred * r, r


def norm_body(h_ref, gain_ref, o_ref):
    xhat, _ = norm_stats(h_ref[...].astype(F32))
    o_ref[...] = (xhat * gain_ref[...]).astype(BF)


def pack_body(qkv, out, inner, down, first, second):
    first[0:3] = qkv[...]
    first[3] = out[...].T
    second[0:2] = inner[...]
    second[2] = down[...]


def middle_rows(h_ref, gain, a, b, c, mid_ref, norm_ref):
    total = h_ref[...].astype(F32) + (a[...].astype(F32) + b[...].astype(F32) + c[...].astype(F32))
    mid_ref[...] = total
    xhat, _ = norm_stats(total)
    norm_ref[...] = (xhat * gain[...]).astype(BF)


INV_SQRT2 = 1.0 / math.sqrt(2.0)
INV_SQRT2PI = 1.0 / math.sqrt(2.0 * math.pi)


def feed_rows(n, c, w, grad, out, hid, gug, count, rows):
    def one_block(i, carry):
        at = pl.ds(pl.multiple_of(i * rows, rows), rows)
        gate = mm(n[at, :], w[0], NT)
        up = mm(n[at, :], w[1], NT)
        back = mm(c[at, :], w[2], NT)
        cdf = 0.5 * (1.0 + lax.erf(gate * INV_SQRT2))
        pdf = jnp.exp(-0.5 * gate * gate) * INV_SQRT2PI
        act = gate * cdf
        hidden = (act * up).astype(BF)
        g0 = (back * up * (cdf + gate * pdf)).astype(BF)
        g1 = (back * act).astype(BF)
        grad[at, :] = (mm(g0, w[0]) + mm(g1, w[1])).astype(BF)
        out[at, :] = mm(hidden, w[2]).astype(BF)
        hid[:, at] = hidden.T
        gug[0, :, at] = g0.T
        gug[1, :, at] = g1.T
        return carry

    lax.fori_loop(0, count, one_block, 0)


def load_mlp(pieces, offs, size, w, sem):
    return [
        start_pieces([x.at[j] for x in pieces], offs, size, w.at[j], sem.at[j], 1) for j in range(3)
    ]


def feed_far(n_pieces, size, refs):
    offs, n_in, c_in, pieces = refs[0], refs[1:3], refs[3:5], refs[5 : 5 + n_pieces]
    refs = refs[5 + n_pieces :]
    grads, outs, (hid, gug) = refs[0:2], refs[2:4], refs[4:6]
    n, c, grad, out, w, sem_w, sem = refs[6:]
    loads = start_rows(n_in, n, sem, 0) + start_rows(c_in, c, sem, 2)
    for group in load_mlp(pieces, offs, size, w, sem_w):
        wait(group)
    wait(loads)
    feed_rows(n, c, w, grad, out, hid, gug, 2, n_in[0].shape[0])
    wait(stop_rows(grad, grads, sem, 0) + stop_rows(out, outs, sem, 2))


def pick_columns(ref, first, second, size):
    a = ref[:, pl.ds(pl.multiple_of(first * size, size), size)]
    b = ref[:, pl.ds(pl.multiple_of(second * size, size), size)]
    return jnp.concatenate([a, b], axis=1)


def mlp_grads(cols, first_block, n, c, hidden, grads, block_sums):
    group = hidden[0].shape[1]

    def one_block(k, carry):
        at = 2 * (first_block + k)
        rights = [pick_columns(x, cols[at], cols[at + 1], 128) for x in (n, c)]
        for j in range(3):
            left = hidden if j == 2 else [x.at[j] for x in grads]
            right = rights[1] if j == 2 else rights[0]
            total = mm(left[0][...], right[:group]) + mm(left[1][...], right[group:])
            block_sums[k, 0, j] = total[:, :128].astype(BF)
            block_sums[k, 1, j] = total[:, 128:].astype(BF)
        return carry

    lax.fori_loop(0, 2, one_block, 0)


def stop_blocks(block_sums, blocks, sem, at):
    return [start(block_sums.at[i // 2, i % 2], x, sem.at[at + i]) for i, x in enumerate(blocks)]


def start_rows(sources, target, sem, at):
    rows = sources[0].shape[0]
    return [start(x, target.at[pl.ds(i * rows, rows)], sem.at[at + i]) for i, x in enumerate(sources)]


def feed_near(n_pieces, size, refs):
    offs, cols, n_in, c_in, hid_far, gug_far = refs[0], refs[1], refs[2:6], refs[6:10], refs[10], refs[11]
    pieces = refs[12 : 12 + n_pieces]
    refs = refs[12 + n_pieces :]
    grads, outs, (hid, gug), blocks = refs[0:2], refs[2:4], refs[4:6], refs[6:10]
    n, c, hf, gf, grad, out, block_sums, w, sem_w, sem = refs[10:]
    loads = start_rows(n_in, n, sem, 0)
    groups = load_mlp(pieces, offs, size, w, sem_w)
    loads += start_rows(c_in, c, sem, 4)
    late = [start(hid_far, hf, sem.at[8]), start(gug_far, gf, sem.at[9])]
    for group in groups:
        wait(group)
    wait(loads)
    feed_rows(n, c, w, grad, out, hid, gug, 2, n_in[0].shape[0])
    wait(late)
    stores = stop_rows(grad, grads, sem, 0) + stop_rows(out, outs, sem, 2)
    mlp_grads(cols, 0, n, c, (hid, hf), (gug, gf), block_sums)
    wait(stores + stop_blocks(block_sums, blocks, sem, 4))


def feed_late(refs):
    cols, n_in, c_in = refs[0], refs[1:5], refs[5:9]
    sources, blocks = refs[9:13], refs[13:17]
    n, c, hn, hf, gn, gf, block_sums, sem = refs[17:]
    loads = start_rows(n_in, n, sem, 0)
    loads += [start(x, y, sem.at[8 + i]) for i, (x, y) in enumerate(zip(sources, (hn, hf, gn, gf)))]
    loads += start_rows(c_in, c, sem, 4)
    wait(loads)
    mlp_grads(cols, 2, n, c, (hn, hf), (gn, gf), block_sums)
    wait(stop_blocks(block_sums, blocks, sem, 0))


def norm_back(v, g):
    xhat, r = norm_stats(v)
    mean_g = jnp.mean(g, axis=-1, keepdims=True)
    mean_gx = jnp.mean(g * xhat, axis=-1, keepdims=True)
    return r * (g - mean_g - xhat * mean_gx), xhat


def middle_back(mid, cot, gain, sa, sb, sc, mg_ref, low_ref, gain_ref):
    got = sa[...].astype(F32) + sb[...].astype(F32) + sc[...].astype(F32)
    back, xhat = norm_back(mid[...], gain[...] * got)
    sums = jnp.sum(got * xhat, axis=0, keepdims=True)
    for i in range(8):
        gain_ref[pl.ds(i, 1), :] = sums[:, 128 * i : 128 * i + 128]
    mg = cot[...].astype(F32) + back
    mg_ref[...] = mg
    low_ref[...] = mg.astype(BF)


def attend_backward(n_pieces, piece_rows, scale, refs):
    cols, mine, offs, gain, gain_two = refs[:5]
    refs = refs[5:]
    grads_in, mixed_in, q_in, k_in, v_in, lse_in, table, norms = (
        refs[0:4], refs[4], refs[5], refs[6], refs[7], refs[8], refs[9], refs[10:14]
    )
    pieces = refs[14 : 14 + n_pieces]
    refs = refs[14 + n_pieces :]
    outs, parts, gain_ref = refs[0:8], refs[8:12], refs[12]
    pg, do, o, q, k, v, lse, tab, n, a, dot_rows, dq, w, block_sums, sent, sem_w, sem = refs[13:]
    rows = grads_in[0].shape[0]
    length, width = q.shape
    heads = width // HD
    weights = start_pieces(pieces, offs, piece_rows, w, sem_w, 1)
    grads = start_rows(grads_in, a, sem, 0)
    pairs = ((mixed_in, o), (q_in, q), (k_in, k), (v_in, v), (lse_in, lse))
    near = [start(x, y, sem.at[4 + i]) for i, (x, y) in enumerate(pairs)]
    late = [start(table, tab, sem.at[12])]
    late += start_rows(norms, n, sem, 13)
    wait(weights)
    wait(grads)
    wait(near)
    lane = lax.broadcasted_iota(jnp.int32, (8, width), 1) >> 6
    head = lax.broadcasted_iota(jnp.int32, (8, width), 0)
    ones = jnp.where(lane == head, 1.0, 0.0).astype(BF)

    def output_grads(i, carry):
        at = pl.ds(pl.multiple_of(i * rows, rows), rows)
        d = mm(a[at, :], w[3]).astype(BF)
        do[at, :] = d
        t = d.astype(F32) * o[at, :].astype(F32)
        hi = t.astype(BF)
        lo = (t - hi.astype(F32)).astype(BF)
        dot_rows[:, at] = mm(ones, hi, NT) + mm(ones, lo, NT)
        return carry

    lax.fori_loop(0, 4, output_grads, 0)
    dq[...] = jnp.zeros_like(dq)
    factor = scale * LOG2E
    nil = jnp.zeros((), BF)

    def one_block(i, carry):
        at = pl.ds(pl.multiple_of(i * rows, rows), rows)
        dk_acc = jnp.zeros((rows, width), F32)
        dv_acc = jnp.zeros((rows, width), F32)
        dq_acc = None
        for h in range(heads):
            mask = head_mask((length, width), h)
            qm = jnp.where(mask, q[...], nil)
            dom = jnp.where(mask, do[...], nil)
            km = jnp.where(head_mask((rows, width), h), k[at, :], nil)
            s = mm(k[at, :], qm, NT)
            dp = mm(v[at, :], dom, NT)
            p = jnp.exp2(s * factor - lse[pl.ds(h, 1), :])
            ds = (p * (dp - dot_rows[pl.ds(h, 1), :])).astype(BF)
            dv_acc = dv_acc + mm(p.astype(BF), dom)
            dk_acc = dk_acc + mm(ds, qm)
            part = mm(ds, km, TN)
            dq_acc = part if dq_acc is None else dq_acc + part
        dq[...] += dq_acc
        cos, sin = angles_at(tab, mine[0] ^ i, rows)
        for g in range(width // 128):
            col = slice(g * 128, g * 128 + 128)
            to = slice(width + g * 128, width + g * 128 + 128)
            pg[at, to] = turn(dk_acc[:, col] * scale, cos, -sin).astype(BF)
        pg[at, 2 * width :] = dv_acc.astype(BF)
        return carry

    wait(late[:1])
    lax.fori_loop(0, 4, one_block, 0)

    def query_grads(i, carry):
        at = pl.ds(pl.multiple_of(i * rows, rows), rows)
        cos, sin = angles_at(tab, mine[0] ^ i, rows)
        for g in range(width // 128):
            col = slice(g * 128, g * 128 + 128)
            pg[at, col] = turn(dq[at, col] * scale, cos, -sin).astype(BF)
        return carry

    lax.fori_loop(0, 4, query_grads, 0)
    wait(late[1:])

    def weight_grads(block, carry):
        first, second = cols[2 * block], cols[2 * block + 1]
        total = mm(pick_columns(n, first, second, 128), pg[...], TN)
        last = mm(pick_columns(a, first, second, 128), o[...], TN)
        for j in range(4):
            part = last if j == 3 else total[:, j * width : (j + 1) * width]
            part = part.astype(BF)
            block_sums[block, 0, j] = part[:128]
            block_sums[block, 1, j] = part[128:]
        return carry

    lax.fori_loop(0, 4, weight_grads, 0)
    stores = stop_blocks(block_sums, outs, sem, 0)

    def row_grads(i, sums):
        at = pl.ds(pl.multiple_of(i * rows, rows), rows)
        total = sum(mm(pg[at, j * width : (j + 1) * width], w[j], NT) for j in range(3))
        sent[at, :] = total.astype(BF)
        return sums + jnp.sum(total * n[at, :].astype(F32), axis=0, keepdims=True)

    sums = lax.fori_loop(0, 4, row_grads, jnp.zeros((1, n.shape[1]), F32))
    sums = sums / gain[...]
    both = [sums[:, 128 * i : 128 * i + 128] for i in range(8)] + [gain_two[...]]
    gain_ref[...] = write_gains(sent, length, jnp.concatenate(both, axis=0))
    ends = [rows] * 3 + [rows + 16]
    for i in range(4):
        stores.append(start(sent.at[pl.ds(i * rows, ends[i])], parts[i], sem.at[8 + i]))
    wait(stores)


def write_gains(ref, rows, gains):
    high = gains.astype(BF)
    low = (gains - high.astype(F32)).astype(BF)
    tail = pl.ds(rows, 16)
    ref[tail, :] = jnp.zeros((16, ref.shape[1]), BF)
    ref[tail, 0:128] = high
    ref[tail, 128:256] = low
    return high.astype(F32) + low.astype(F32)


def read_gains(ref, rows):
    tail = pl.ds(rows, 16)
    return ref[tail, 0:128].astype(F32) + ref[tail, 128:256].astype(F32)


def add_far(part, got, gains, o_ref, gains_ref):
    rows = part.shape[0]
    o_ref[pl.ds(0, rows), :] = (part[...].astype(F32) + got[pl.ds(0, rows), :].astype(F32)).astype(BF)
    gains_ref[...] = write_gains(o_ref, rows, gains[...] + read_gains(got, rows))


def input_back(h, mg, gain, sa, sb, sc, gains, o_ref, gains_ref):
    rows = sa.shape[0]
    gains_ref[...] = gains[...] + read_gains(sc, rows)
    got = sa[...].astype(F32) + sb[...].astype(F32) + sc[pl.ds(0, rows), :].astype(F32)
    back, _ = norm_back(h[...].astype(F32), gain[...] * got)
    o_ref[...] = mg[...] + back


def body(function, *static):
    return lambda *refs: function(*static, refs)


def angle_table(length):
    exponents = np.arange(0, HD, 2).astype(np.float32) / np.float32(HD)
    inverse = np.float32(ROPE_BASE) ** (-exponents)
    angles = np.arange(length).astype(np.float32)[:, None] * inverse[None, :]
    cos, sin = np.cos(angles), np.sin(angles)
    return np.concatenate([cos, cos, sin, sin], axis=1).astype(np.float32)


def shards(sizes, *args):
    hidden_in, attn_gain, qkv_weight, out_weight, mlp_gain, in_weight, down_weight, cotangent = args
    dp, tp = sizes
    rows, model = hidden_in.shape
    length = rows * tp
    piece_rows = qkv_weight.shape[1]
    width = qkv_weight.shape[2]
    units = in_weight.shape[2]
    scale = HD ** (-0.5)
    direct = dp == 8
    mine_one = lax.axis_index("tensor").astype(jnp.int32).reshape(1)
    place = lax.axis_index("dp")
    gain_one, gain_two = attn_gain.reshape(1, model), mlp_gain.reshape(1, model)

    def tensor(value, k, label):
        return swap(value, "tensor", tp, k, f"{label}_t{k}")

    def depth(value, k, label):
        return swap(value, "dp", dp, k, f"{label}_d{k}")

    def gather(shard, axis, label):
        if direct:
            far = depth(shard, 4, label)
            along = [shard, depth(shard, 2, label), far, depth(far, 2, label + "far")]
            across = [depth(v, 1, f"{label}{i}") for i, v in enumerate(along)]
            return [v for pair in zip(along, across) for v in pair]
        return [lax.all_gather(shard, "dp", axis=axis, tiled=True)]

    def only_direct(values):
        return values if direct else []

    if direct:
        offs = place ^ jnp.arange(8, dtype=jnp.int32)
        n_pieces, piece = 8, piece_rows
        z, y = place // 2, place % 2
        order = [1, 3, 2, 0]
        cols = jnp.stack([c for b in order for c in ((z ^ b) * 2 + (1 - y), (z ^ b) * 2 + y)])
    else:
        offs = jnp.zeros((1,), jnp.int32)
        n_pieces, piece = 1, model
        cols = jnp.arange(8, dtype=jnp.int32)
    cols = cols.astype(jnp.int32)
    sems = lambda *s: pltpu.SemaphoreType.DMA(s)
    add = lambda a, b: (a.astype(F32) + b.astype(F32)).astype(BF)

    def spread(own, label):
        far = tensor(own, 2, label)
        return [own, tensor(own, 1, label), far, tensor(far, 1, label + "far")]

    def exchange(blocks, label):
        return [blocks[0]] + [tensor(blocks[k], k, label) for k in (1, 2, 3)]

    def reduce(blocks, axis, label):
        whole = jnp.concatenate(blocks, axis=axis)
        return lax.psum_scatter(whole, "dp", scatter_dimension=axis, tiled=True).astype(F32)

    def sum_of(*values):
        return sum(v.astype(F32) for v in values)

    near = lambda *xs: [(x, vmem()) for x in xs]
    away = lambda xs: [(x, hbm()) for x in xs]
    scalar = lambda *xs: [(x, smem()) for x in xs]
    vm = lambda shape, dtype=BF: (shape, dtype, vmem())
    hb = lambda shape, dtype=BF: (shape, dtype, hbm())
    buf = lambda *shape, dtype=BF: pltpu.VMEM(shape, dtype)

    shard, mlp_shard = call(
        pack_body,
        near(qkv_weight, out_weight, in_weight.transpose(0, 2, 1), down_weight),
        [vm((4, piece_rows, width)), vm((3, units, piece_rows))],
        name="pack",
    )
    qkvo = gather(shard, 1, "qkvo")
    (normed,) = call(norm_body, near(hidden_in, gain_one), [vm((rows, model))], name="norm")
    if direct:
        (normed,) = gate([normed], [qkvo[1], qkvo[2], qkvo[4]])
    normed_attn = spread(normed, "norm")
    table = jnp.asarray(angle_table(length))
    if direct:
        (mlp_along,) = gate([mlp_shard], [qkvo[6]])
        (mlp_across,) = gate([mlp_shard], [qkvo[7]])
        z2, z1 = [depth(mlp_along, 2 * k, "mlp") for k in (2, 1)]
        (cotangent_there,) = gate([cotangent], [normed_attn[2]])
    else:
        cotangent_there = cotangent
    cot = spread(cotangent_there, "cot")
    if direct:
        before = []
    else:
        mlp, before = gather(mlp_shard, 2, "mlp"), []
    *parts, mixed, q, k, v, lse = call(
        body(attend_forward, n_pieces, piece, scale),
        scalar(offs, mine_one)
        + away(normed_attn)
        + away([table] + qkvo),
        [hb((rows, model))] * 4 + [hb((length, width))] * 4 + [vm((8, length), F32)],
        [buf(4, rows, model), buf(length, 128, dtype=F32), buf(4, model, width)]
        + [buf(length, width)] * 4
        + [buf(length, model), sems(n_pieces), sems(13)],
        name="attend_forward",
    )
    if direct:
        y0 = depth(mlp_across, 1, "mlp0")
        *parts, lse = gate(parts + [lse], [z1, z2, y0])
    attn_far = add(parts[2], tensor(parts[3], 1, "afar"))
    attn_near = tensor(parts[1], 1, "anear")
    attn_got = tensor(attn_far, 2, "afar")
    if direct:
        z3 = depth(gate([z2], [lse])[0], 2, "mlpfar")
        y1, y2, y3 = [depth(gate([x], [lse])[0], 1, f"mlp{i}") for i, x in ((1, z1), (2, z2), (3, z3))]
        before = [y1, z3]
        mlp = [mlp_shard, y0, z1, y1, z2, y2, z3, y3]
    middle, normed_two = call(
        middle_rows,
        near(hidden_in, gain_two, *gate([parts[0]], before), attn_near, attn_got),
        [vm((rows, model), F32), vm((rows, model))],
        name="middle_rows",
    )

    normed_far = tensor(normed_two, 2, "norm2")
    (normed_relay,) = gate([normed_far], only_direct(mlp[5:]))
    normed_mlp = [normed_two, tensor(normed_two, 1, "norm2"), normed_far, tensor(normed_relay, 1, "norm2far")]
    far_back, far_send, far_out, far_out_send, far_hidden, far_grad = call(
        body(feed_far, n_pieces, piece),
        scalar(offs) + away(normed_mlp[2:] + cot[2:] + mlp),
        [hb((rows, model))] * 4 + [vm((units, 2 * rows)), vm((2, units, 2 * rows))],
        [buf(2 * rows, model)] * 4 + [buf(3, units, model), sems(3, n_pieces), sems(4)],
        name="feed_far",
    )
    far_sum = add(far_back, tensor(far_send, 1, "far"))
    from_far = tensor(far_sum, 2, "far")
    near_back, near_send, near_out, near_out_send, near_hidden, near_grad, *grads = call(
        body(feed_near, n_pieces, piece),
        scalar(offs, cols)
        + away(gate(normed_mlp, [far_sum]) + cot + [far_hidden, far_grad] + mlp),
        [hb((rows, model))] * 4
        + [vm((units, 2 * rows)), vm((2, units, 2 * rows))]
        + [hb((3, units, 128))] * 4,
        [buf(length, model)] * 2
        + [buf(units, 2 * rows), buf(2, units, 2 * rows)]
        + [buf(2 * rows, model)] * 2
        + [buf(2, 2, 3, units, 128), buf(3, units, model), sems(3, n_pieces), sems(10)],
        name="feed_near",
    )
    near_got = tensor(near_send, 1, "near")
    out_sum = add(far_out, tensor(far_out_send, 1, "lofar"))
    out_near = tensor(near_out_send, 1, "lonear")

    middle_grad, low_grad, gain_two_part = call(
        middle_back,
        near(middle, cotangent, gain_two, near_back, near_got, from_far),
        [vm((rows, model), F32), vm((rows, model)), vm((8, 128), F32)],
        name="middle_back",
    )
    attn_out_grad = spread(low_grad, "aog")
    if direct:
        (grads[0],) = gate(grads[:1], [from_far])
        got = [depth(grads[0], 1, "gmlp0")]
        sums = [add(grads[1], got[0])]
        (grads[2],) = gate(grads[2:3], sums)
        before = [low_grad, sums[0], out_sum, out_near]
    else:
        before = [low_grad]
    grads += call(
        body(feed_late),
        scalar(cols)
        + away(gate(normed_mlp, before) + cot + [near_hidden, far_hidden, near_grad, far_grad]),
        [hb((3, units, 128))] * 4,
        [buf(length, model)] * 2
        + [buf(units, 2 * rows)] * 2
        + [buf(2, units, 2 * rows)] * 2
        + [buf(2, 2, 3, units, 128), sems(12)],
        name="feed_late",
    )
    early = [grads[7]]
    if direct:
        grads[4], grads[6] = gate([grads[4], grads[6]], [attn_out_grad[2]])
        got += [depth(grads[2 * i], 1, f"gmlp{i}") for i in (1, 2, 3)]
        sums.append(add(grads[3], got[1]))
        back = [depth(sums[i], 2, f"gmlpz{i}") for i in range(2)]
        early.append(sums[1])

    *attn, b0, b1, b2, b3, gains = call(
        body(attend_backward, n_pieces, piece, scale),
        scalar(cols, mine_one, offs)
        + near(gain_one, gain_two_part)
        + away(gate(attn_out_grad, early) + [mixed, q, k, v, lse, table] + normed_attn + qkvo),
        [hb((4, 128, width))] * 8
        + [hb((rows, model))] * 3
        + [hb((rows + 16, model)), vm((16, 128), F32)],
        [buf(length, 3 * width)]
        + [buf(length, width)] * 5
        + [buf(8, length, dtype=F32), buf(length, 128, dtype=F32), buf(length, model), buf(length, model)]
        + [buf(8, length, dtype=F32), buf(length, width, dtype=F32)]
        + [buf(4, model, width), buf(4, 2, 4, 128, width), buf(length + 16, model)]
        + [sems(n_pieces), sems(17)],
        name="attend_backward",
    )
    if direct:
        late = sum_of(gate([grads[5]], [b0])[0], got[2], back[1]).astype(BF)
        last = depth(late, 4, "gmlp")
        *attn, b3 = gate(attn + [b3], [late, back[0], got[3]])
        gqkv = [depth(attn[2 * i], 1, f"gqkv{i}") for i in range(3)]
        qkv_sums = [add(attn[2 * i + 1], gqkv[i]) for i in range(2)]
        qkv_back = [depth(qkv_sums[i], 2, f"gqkvz{i}") for i in range(2)]
    sent_far, gains = call(
        add_far,
        near(b2, tensor(b3, 1, "nfar"), gains),
        [vm((rows + 16, model)), vm((16, 128), F32)],
        name="add_far",
    )
    got_far = tensor(sent_far, 2, "nfar")
    (b1,) = gate([b1], [sent_far])
    near_sum = tensor(b1, 1, "nnear")
    if direct:
        (b0,) = gate([b0], [last])
    input_grad, gains = call(
        input_back,
        near(hidden_in, middle_grad, gain_one, b0, near_sum, got_far, gains),
        [vm((rows, model), F32), vm((16, 128), F32)],
        name="input_back",
    )
    out_far = tensor(gate([out_sum], [got_far])[0], 2, "lofar")
    out_near = near_out.astype(F32) + out_near.astype(F32)
    layer_out = (middle + (out_near + out_far.astype(F32))).astype(BF)

    if direct:
        (attn[6],) = gate(attn[6:7], [input_grad])
        gains = gains + depth(gains, 1, "gain")
        gains = gains + depth(gains, 2, "gain")
        gains = gains + depth(gains, 4, "gain")
        gqkv.append(depth(attn[6], 1, "gqkv3"))
        qkv_late = sum_of(attn[5], gqkv[2], qkv_back[1]).astype(BF)
        qkv_last = depth(qkv_late, 4, "gqkv")
        attn_total = sum_of(attn[7], gqkv[3], qkv_back[0], gate([qkv_last], [out_far, gains])[0])
    else:
        gains = lax.psum(gains, "dp")
        attn_total = reduce(attn, 1, "gqkv")
    qkv_shard, out_shard = attn_total[0:3], attn_total[3].T
    gains = gains.reshape(2, model)

    if direct:
        mlp_total = sum_of(grads[7], got[3], back[0], gate([last], [input_grad])[0])
    else:
        mlp_total = reduce(grads, 2, "gmlp")
    in_shard, down_shard = mlp_total[0:2].transpose(0, 2, 1), mlp_total[2]

    return (layer_out, input_grad, gains[0], qkv_shard, out_shard, gains[1], in_shard, down_shard)


def solution(mesh):
    sizes = (mesh.shape["dp"], mesh.shape["tensor"])
    return jax.shard_map(
        functools.partial(shards, sizes),
        mesh=mesh,
        in_specs=(
            P(("dp", "tensor"), None),
            P(),
            P(None, "dp", "tensor"),
            P("tensor", "dp"),
            P(),
            P(None, "dp", "tensor"),
            P("tensor", "dp"),
            P(("dp", "tensor"), None),
        ),
        out_specs=(
            P(("dp", "tensor"), None),
            P(("dp", "tensor"), None),
            P(),
            P(None, "dp", "tensor"),
            P("tensor", "dp"),
            P(),
            P(None, "dp", "tensor"),
            P("tensor", "dp"),
        ),
        check_vma=False,
    )
```

```python
import functools
import math

import jax
import jax.numpy as jnp
import numpy as np
from jax import lax
from jax.experimental import pallas as pl
from jax.experimental.pallas import tpu as pltpu
from jax.sharding import PartitionSpec as P

HD = 64
NORM_EPS = 1e-05
ROPE_BASE = 160000.0
BF = jnp.bfloat16
F32 = jnp.float32
LOG2E = math.log2(math.e)
COST = 1000
VMEM_MIB = 56

NN = (((1,), (0,)), ((), ()))
NT = (((1,), (1,)), ((), ()))
TN = (((0,), (0,)), ((), ()))


def mm(a, b, dims=NN):
    return lax.dot_general(a, b, dims, preferred_element_type=F32)


def vmem():
    return pl.BlockSpec(memory_space=pltpu.VMEM)


def smem():
    return pl.BlockSpec(memory_space=pltpu.SMEM)


def hbm():
    return pl.BlockSpec(memory_space=pltpu.HBM)


def call(body, ins, outs, scratch=(), name=None):
    return pl.pallas_call(
        body,
        out_shape=[jax.ShapeDtypeStruct(o[0], o[1]) for o in outs],
        in_specs=[i[1] for i in ins],
        out_specs=[o[2] for o in outs],
        scratch_shapes=list(scratch),
        compiler_params=pltpu.CompilerParams(vmem_limit_bytes=VMEM_MIB * 1024 * 1024),
        cost_estimate=pl.CostEstimate(flops=COST, transcendentals=0, bytes_accessed=COST),
        name=name,
    )(*[i[0] for i in ins])


def swap(value, axis, size, distance, label):
    with jax.named_scope(label):
        return lax.ppermute(value, axis, [(i, i ^ distance) for i in range(size)])


def gate(values, others):
    return list(lax.optimization_barrier((tuple(values), tuple(others)))[0])


def start(source, target, sem):
    copy = pltpu.make_async_copy(source, target, sem)
    copy.start()
    return copy


def start_pieces(pieces, offs, size, target, sem, axis):
    copies = []
    for i, piece in enumerate(pieces):
        where = pl.ds(pl.multiple_of(offs[i] * size, size), size)
        copies.append(start(piece, target.at[(slice(None),) * axis + (where,)], sem.at[i]))
    return copies


def stop_rows(source, targets, sem, at):
    rows = targets[0].shape[0]
    return [
        start(source.at[pl.ds(i * rows, rows)], x, sem.at[at + i]) for i, x in enumerate(targets)
    ]


def wait(copies):
    for c in copies:
        c.wait()


def angles_at(table, block, rows):
    both = table[pl.ds(pl.multiple_of((block & 1) * rows, rows), rows), :]
    here = jnp.where(block < 2, both, pltpu.roll(both, 64, 1))
    a, b, c = [pltpu.roll(here, shift, 1) for shift in (32, 64, 96)]
    lane = lax.broadcasted_iota(jnp.int32, both.shape, 1)
    even = (lane & 63) < 32
    cos = jnp.where(lane < 64, jnp.where(even, here, a), jnp.where(even, b, c))
    sin = jnp.where(lane < 64, jnp.where(even, -c, here), jnp.where(even, -a, b))
    return cos, sin


def turn(u, cos, sin):
    lane = lax.broadcasted_iota(jnp.int32, u.shape, 1)
    low = (lane & 63) < 32
    turned = jnp.where(low, pltpu.roll(u, 96, 1), pltpu.roll(u, 32, 1))
    return u * cos + turned * sin


def head_mask(shape, head):
    lane = lax.broadcasted_iota(jnp.int32, shape, 1)
    return (lane >> 6) == head


def attend_forward(n_pieces, piece_rows, scale, refs):
    offs, mine = refs[:2]
    norms, table = refs[2:6], refs[6]
    pieces = refs[7 : 7 + n_pieces]
    refs = refs[7 + n_pieces :]
    parts, (mixed_out, q_out, k_out, v_out, lse_ref) = refs[0:4], refs[4:9]
    n, tab, w, q, k, v, mixed, part, sem_w, sem = refs[9:]
    rows, width = n.shape[1], w.shape[2]
    loads = start_pieces(pieces, offs, piece_rows, w, sem_w, 1)
    norm_loads = [start(norms[i], n.at[i], sem.at[i]) for i in range(4)]
    table_load = start(table, tab, sem.at[4])
    wait(loads)
    table_load.wait()
    wait(norm_loads)

    def project(i, carry):
        at = pl.ds(pl.multiple_of(i * rows, rows), rows)
        cos, sin = angles_at(tab, mine[0] ^ i, rows)
        for j, ref in ((0, q), (1, k)):
            u = mm(n[i], w[j])
            for g in range(width // 128):
                col = slice(g * 128, g * 128 + 128)
                ref[at, col] = turn(u[:, col], cos, sin).astype(BF)
        v[at, :] = mm(n[i], w[2]).astype(BF)
        return carry

    lax.fori_loop(0, 4, project, 0)
    stores = [start(x, y, sem.at[5 + i]) for i, (x, y) in enumerate(((q, q_out), (k, k_out), (v, v_out)))]
    factor = scale * LOG2E
    heads = width // HD
    group = 2 * rows

    def attend(half, carry):
        at = pl.ds(pl.multiple_of(half * group, group), group)
        masks = [head_mask((group, width), h) for h in range(heads)]

        def scores(h):
            return mm(jnp.where(masks[h], q[at, :], jnp.zeros((), BF)), k[...], NT)

        acc = jnp.zeros((group, width), F32)
        s = scores(0)
        for h in range(heads):
            ahead = scores(h + 1) if h + 1 < heads else None
            top = jnp.max(s, axis=1, keepdims=True)
            e = jnp.exp2((s - top) * factor)
            total = jnp.sum(e, axis=1, keepdims=True)
            o = mm(e.astype(BF), v[...]) * (1.0 / total)
            lse2 = top * factor + jnp.log2(total)
            row = jnp.transpose(jnp.broadcast_to(lse2, (group, 128)))
            lse_ref[pl.ds(h, 1), at] = row[0:1, :]
            acc = jnp.where(masks[h], o, acc)
            s = ahead
        low = acc.astype(BF)
        mixed[at, :] = low
        part[at, :] = mm(low, w[3], NT).astype(BF)
        return carry

    lax.fori_loop(0, 2, attend, 0)
    stores.append(start(mixed, mixed_out, sem.at[8]))
    stores += stop_rows(part, parts, sem, 9)
    wait(stores)


def norm_stats(v):
    mean = jnp.mean(v, axis=-1, keepdims=True)
    centred = v - mean
    spread = jnp.mean(centred * centred, axis=-1, keepdims=True)
    r = lax.rsqrt(spread + NORM_EPS)
    return centred * r, r


def norm_body(h_ref, gain_ref, o_ref):
    xhat, _ = norm_stats(h_ref[...].astype(F32))
    o_ref[...] = (xhat * gain_ref[...]).astype(BF)


def pack_body(qkv, out, inner, down, first, second):
    first[0:3] = qkv[...]
    first[3] = out[...].T
    second[0:2] = inner[...]
    second[2] = down[...]


def middle_rows(h_ref, gain, a, b, c, mid_ref, norm_ref):
    total = h_ref[...].astype(F32) + (a[...].astype(F32) + b[...].astype(F32) + c[...].astype(F32))
    mid_ref[...] = total
    xhat, _ = norm_stats(total)
    norm_ref[...] = (xhat * gain[...]).astype(BF)


INV_SQRT2 = 1.0 / math.sqrt(2.0)
INV_SQRT2PI = 1.0 / math.sqrt(2.0 * math.pi)


def feed_rows(n, c, w, grad, out, hid, gug, count, rows):
    def one_block(i, carry):
        at = pl.ds(pl.multiple_of(i * rows, rows), rows)
        gate = mm(n[at, :], w[0], NT)
        up = mm(n[at, :], w[1], NT)
        back = mm(c[at, :], w[2], NT)
        cdf = 0.5 * (1.0 + lax.erf(gate * INV_SQRT2))
        pdf = jnp.exp(-0.5 * gate * gate) * INV_SQRT2PI
        act = gate * cdf
        hidden = (act * up).astype(BF)
        g0 = (back * up * (cdf + gate * pdf)).astype(BF)
        g1 = (back * act).astype(BF)
        grad[at, :] = (mm(g0, w[0]) + mm(g1, w[1])).astype(BF)
        out[at, :] = mm(hidden, w[2]).astype(BF)
        hid[:, at] = hidden.T
        gug[0, :, at] = g0.T
        gug[1, :, at] = g1.T
        return carry

    lax.fori_loop(0, count, one_block, 0, unroll=True)


def load_mlp(pieces, offs, size, w, sem):
    return [
        start_pieces([x.at[j] for x in pieces], offs, size, w.at[j], sem.at[j], 1) for j in range(3)
    ]


def feed_far(n_pieces, size, refs):
    offs, n_in, c_in, pieces = refs[0], refs[1:3], refs[3:5], refs[5 : 5 + n_pieces]
    refs = refs[5 + n_pieces :]
    grads, outs, (hid, gug) = refs[0:2], refs[2:4], refs[4:6]
    n, c, grad, out, w, sem_w, sem = refs[6:]
    loads = start_rows(n_in, n, sem, 0) + start_rows(c_in, c, sem, 2)
    for group in load_mlp(pieces, offs, size, w, sem_w):
        wait(group)
    wait(loads)
    feed_rows(n, c, w, grad, out, hid, gug, 2, n_in[0].shape[0])
    wait(stop_rows(grad, grads, sem, 0) + stop_rows(out, outs, sem, 2))


def pick_columns(ref, first, second, size):
    a = ref[:, pl.ds(pl.multiple_of(first * size, size), size)]
    b = ref[:, pl.ds(pl.multiple_of(second * size, size), size)]
    return jnp.concatenate([a, b], axis=1)


def mlp_grads(cols, first_block, n, c, hidden, grads, block_sums):
    group = hidden[0].shape[1]

    def one_block(k, carry):
        at = 2 * (first_block + k)
        rights = [pick_columns(x, cols[at], cols[at + 1], 128) for x in (n, c)]
        for j in range(3):
            left = hidden if j == 2 else [x.at[j] for x in grads]
            right = rights[1] if j == 2 else rights[0]
            total = mm(left[0][...], right[:group]) + mm(left[1][...], right[group:])
            block_sums[k, 0, j] = total[:, :128].astype(BF)
            block_sums[k, 1, j] = total[:, 128:].astype(BF)
        return carry

    lax.fori_loop(0, 2, one_block, 0)


def stop_blocks(block_sums, blocks, sem, at):
    return [start(block_sums.at[i // 2, i % 2], x, sem.at[at + i]) for i, x in enumerate(blocks)]


def start_rows(sources, target, sem, at):
    rows = sources[0].shape[0]
    return [start(x, target.at[pl.ds(i * rows, rows)], sem.at[at + i]) for i, x in enumerate(sources)]


def feed_near(n_pieces, size, refs):
    offs, cols, n_in, c_in, hid_far, gug_far = refs[0], refs[1], refs[2:6], refs[6:10], refs[10], refs[11]
    pieces = refs[12 : 12 + n_pieces]
    refs = refs[12 + n_pieces :]
    grads, outs, (hid, gug), blocks = refs[0:2], refs[2:4], refs[4:6], refs[6:10]
    n, c, hf, gf, grad, out, block_sums, w, sem_w, sem = refs[10:]
    loads = start_rows(n_in, n, sem, 0)
    groups = load_mlp(pieces, offs, size, w, sem_w)
    loads += start_rows(c_in, c, sem, 4)
    late = [start(hid_far, hf, sem.at[8]), start(gug_far, gf, sem.at[9])]
    for group in groups:
        wait(group)
    wait(loads)
    feed_rows(n, c, w, grad, out, hid, gug, 2, n_in[0].shape[0])
    wait(late)
    stores = stop_rows(grad, grads, sem, 0) + stop_rows(out, outs, sem, 2)
    mlp_grads(cols, 0, n, c, (hid, hf), (gug, gf), block_sums)
    wait(stores + stop_blocks(block_sums, blocks, sem, 4))


def feed_late(refs):
    cols, n_in, c_in = refs[0], refs[1:5], refs[5:9]
    sources, blocks = refs[9:13], refs[13:17]
    n, c, hn, hf, gn, gf, block_sums, sem = refs[17:]
    loads = start_rows(n_in, n, sem, 0)
    loads += [start(x, y, sem.at[8 + i]) for i, (x, y) in enumerate(zip(sources, (hn, hf, gn, gf)))]
    loads += start_rows(c_in, c, sem, 4)
    wait(loads)
    mlp_grads(cols, 2, n, c, (hn, hf), (gn, gf), block_sums)
    wait(stop_blocks(block_sums, blocks, sem, 0))


def norm_back(v, g):
    xhat, r = norm_stats(v)
    mean_g = jnp.mean(g, axis=-1, keepdims=True)
    mean_gx = jnp.mean(g * xhat, axis=-1, keepdims=True)
    return r * (g - mean_g - xhat * mean_gx), xhat


def middle_back(mid, cot, gain, sa, sb, sc, mg_ref, low_ref, gain_ref):
    got = sa[...].astype(F32) + sb[...].astype(F32) + sc[...].astype(F32)
    back, xhat = norm_back(mid[...], gain[...] * got)
    sums = jnp.sum(got * xhat, axis=0, keepdims=True)
    for i in range(8):
        gain_ref[pl.ds(i, 1), :] = sums[:, 128 * i : 128 * i + 128]
    mg = cot[...].astype(F32) + back
    mg_ref[...] = mg
    low_ref[...] = mg.astype(BF)


def attend_backward(n_pieces, piece_rows, scale, refs):
    cols, mine, offs, gain, gain_two = refs[:5]
    refs = refs[5:]
    grads_in, mixed_in, q_in, k_in, v_in, lse_in, table, norms = (
        refs[0:4], refs[4], refs[5], refs[6], refs[7], refs[8], refs[9], refs[10:14]
    )
    pieces = refs[14 : 14 + n_pieces]
    refs = refs[14 + n_pieces :]
    outs, parts, gain_ref = refs[0:8], refs[8:12], refs[12]
    pg, do, o, q, k, v, lse, tab, n, a, dot_rows, dq, w, block_sums, sent, sem_w, sem = refs[13:]
    rows = grads_in[0].shape[0]
    length, width = q.shape
    heads = width // HD
    weights = start_pieces(pieces, offs, piece_rows, w, sem_w, 1)
    grads = start_rows(grads_in, a, sem, 0)
    pairs = ((mixed_in, o), (q_in, q), (k_in, k), (v_in, v), (lse_in, lse))
    near = [start(x, y, sem.at[4 + i]) for i, (x, y) in enumerate(pairs)]
    late = [start(table, tab, sem.at[12])]
    late += start_rows(norms, n, sem, 13)
    wait(weights)
    wait(grads)
    wait(near)
    lane = lax.broadcasted_iota(jnp.int32, (8, width), 1) >> 6
    head = lax.broadcasted_iota(jnp.int32, (8, width), 0)
    ones = jnp.where(lane == head, 1.0, 0.0).astype(BF)

    def output_grads(i, carry):
        at = pl.ds(pl.multiple_of(i * rows, rows), rows)
        d = mm(a[at, :], w[3]).astype(BF)
        do[at, :] = d
        t = d.astype(F32) * o[at, :].astype(F32)
        hi = t.astype(BF)
        lo = (t - hi.astype(F32)).astype(BF)
        dot_rows[:, at] = mm(ones, hi, NT) + mm(ones, lo, NT)
        return carry

    lax.fori_loop(0, 4, output_grads, 0, unroll=2)
    dq[...] = jnp.zeros_like(dq)
    factor = scale * LOG2E
    nil = jnp.zeros((), BF)

    def one_block(i, carry):
        at = pl.ds(pl.multiple_of(i * rows, rows), rows)
        dk_acc = jnp.zeros((rows, width), F32)
        dv_acc = jnp.zeros((rows, width), F32)
        dq_acc = None
        for h in range(heads):
            mask = head_mask((length, width), h)
            qm = jnp.where(mask, q[...], nil)
            dom = jnp.where(mask, do[...], nil)
            km = jnp.where(head_mask((rows, width), h), k[at, :], nil)
            s = mm(k[at, :], qm, NT)
            dp = mm(v[at, :], dom, NT)
            p = jnp.exp2(s * factor - lse[pl.ds(h, 1), :])
            ds = (p * (dp - dot_rows[pl.ds(h, 1), :])).astype(BF)
            dv_acc = dv_acc + mm(p.astype(BF), dom)
            dk_acc = dk_acc + mm(ds, qm)
            part = mm(ds, km, TN)
            dq_acc = part if dq_acc is None else dq_acc + part
        dq[...] += dq_acc
        cos, sin = angles_at(tab, mine[0] ^ i, rows)
        for g in range(width // 128):
            col = slice(g * 128, g * 128 + 128)
            to = slice(width + g * 128, width + g * 128 + 128)
            pg[at, to] = turn(dk_acc[:, col] * scale, cos, -sin).astype(BF)
        pg[at, 2 * width :] = dv_acc.astype(BF)
        return carry

    wait(late[:1])
    lax.fori_loop(0, 4, one_block, 0)

    def query_grads(i, carry):
        at = pl.ds(pl.multiple_of(i * rows, rows), rows)
        cos, sin = angles_at(tab, mine[0] ^ i, rows)
        for g in range(width // 128):
            col = slice(g * 128, g * 128 + 128)
            pg[at, col] = turn(dq[at, col] * scale, cos, -sin).astype(BF)
        return carry

    lax.fori_loop(0, 4, query_grads, 0)
    wait(late[1:])

    def weight_grads(block, carry):
        first, second = cols[2 * block], cols[2 * block + 1]
        total = mm(pick_columns(n, first, second, 128), pg[...], TN)
        last = mm(pick_columns(a, first, second, 128), o[...], TN)
        for j in range(4):
            part = last if j == 3 else total[:, j * width : (j + 1) * width]
            part = part.astype(BF)
            block_sums[block, 0, j] = part[:128]
            block_sums[block, 1, j] = part[128:]
        return carry

    lax.fori_loop(0, 4, weight_grads, 0, unroll=True)
    stores = stop_blocks(block_sums, outs, sem, 0)

    def row_grads(i, sums):
        at = pl.ds(pl.multiple_of(i * rows, rows), rows)
        total = sum(mm(pg[at, j * width : (j + 1) * width], w[j], NT) for j in range(3))
        sent[at, :] = total.astype(BF)
        return sums + jnp.sum(total * n[at, :].astype(F32), axis=0, keepdims=True)

    sums = lax.fori_loop(0, 4, row_grads, jnp.zeros((1, n.shape[1]), F32), unroll=2)
    sums = sums / gain[...]
    both = [sums[:, 128 * i : 128 * i + 128] for i in range(8)] + [gain_two[...]]
    gain_ref[...] = write_gains(sent, length, jnp.concatenate(both, axis=0))
    ends = [rows] * 3 + [rows + 16]
    for i in range(4):
        stores.append(start(sent.at[pl.ds(i * rows, ends[i])], parts[i], sem.at[8 + i]))
    wait(stores)


def write_gains(ref, rows, gains):
    high = gains.astype(BF)
    low = (gains - high.astype(F32)).astype(BF)
    tail = pl.ds(rows, 16)
    ref[tail, :] = jnp.zeros((16, ref.shape[1]), BF)
    ref[tail, 0:128] = high
    ref[tail, 128:256] = low
    return high.astype(F32) + low.astype(F32)


def read_gains(ref, rows):
    tail = pl.ds(rows, 16)
    return ref[tail, 0:128].astype(F32) + ref[tail, 128:256].astype(F32)


def add_far(part, got, gains, o_ref, gains_ref):
    rows = part.shape[0]
    o_ref[pl.ds(0, rows), :] = (part[...].astype(F32) + got[pl.ds(0, rows), :].astype(F32)).astype(BF)
    gains_ref[...] = write_gains(o_ref, rows, gains[...] + read_gains(got, rows))


def input_back(h, mg, gain, sa, sb, sc, o_ref):
    got = sa[...].astype(F32) + sb[...].astype(F32) + sc[pl.ds(0, sa.shape[0]), :].astype(F32)
    back, _ = norm_back(h[...].astype(F32), gain[...] * got)
    o_ref[...] = mg[...] + back


def body(function, *static):
    return lambda *refs: function(*static, refs)


def angle_table(length):
    exponents = np.arange(0, HD, 2).astype(np.float32) / np.float32(HD)
    inverse = np.float32(ROPE_BASE) ** (-exponents)
    angles = np.arange(length).astype(np.float32)[:, None] * inverse[None, :]
    cos, sin = np.cos(angles), np.sin(angles)
    half = length // 2
    return np.concatenate([cos[:half], sin[:half], cos[half:], sin[half:]], axis=1).astype(np.float32)


def shards(sizes, *args):
    hidden_in, attn_gain, qkv_weight, out_weight, mlp_gain, in_weight, down_weight, cotangent = args
    dp, tp = sizes
    rows, model = hidden_in.shape
    length = rows * tp
    piece_rows = qkv_weight.shape[1]
    width = qkv_weight.shape[2]
    units = in_weight.shape[2]
    scale = HD ** (-0.5)
    direct = dp == 8
    mine_one = lax.axis_index("tensor").astype(jnp.int32).reshape(1)
    place = lax.axis_index("dp")
    gain_one, gain_two = attn_gain.reshape(1, model), mlp_gain.reshape(1, model)

    def tensor(value, k, label):
        return swap(value, "tensor", tp, k, f"{label}_t{k}")

    def depth(value, k, label):
        return swap(value, "dp", dp, k, f"{label}_d{k}")

    def gather(shard, axis, label):
        if direct:
            far = depth(shard, 4, label)
            along = [shard, depth(shard, 2, label), far, depth(far, 2, label + "far")]
            across = [depth(v, 1, f"{label}{i}") for i, v in enumerate(along[:3])]
            across.append(depth(gate(along[3:], across[1:2])[0], 1, label + "3"))
            return [v for pair in zip(along, across) for v in pair]
        return [lax.all_gather(shard, "dp", axis=axis, tiled=True)]

    def only_direct(values):
        return values if direct else []

    if direct:
        offs = place ^ jnp.arange(8, dtype=jnp.int32)
        n_pieces, piece = 8, piece_rows
        z, y = place // 2, place % 2
        order = [1, 3, 2, 0]
        cols = jnp.stack([c for b in order for c in ((z ^ b) * 2 + (1 - y), (z ^ b) * 2 + y)])
    else:
        offs = jnp.zeros((1,), jnp.int32)
        n_pieces, piece = 1, model
        cols = jnp.arange(8, dtype=jnp.int32)
    cols = cols.astype(jnp.int32)
    sems = lambda *s: pltpu.SemaphoreType.DMA(s)
    add = lambda a, b: (a.astype(F32) + b.astype(F32)).astype(BF)

    def spread(own, label):
        far = tensor(own, 2, label)
        return [own, tensor(own, 1, label), far, tensor(far, 1, label + "far")]

    def exchange(blocks, label):
        return [blocks[0]] + [tensor(blocks[k], k, label) for k in (1, 2, 3)]

    def reduce(blocks, axis, label):
        whole = jnp.concatenate(blocks, axis=axis)
        return lax.psum_scatter(whole, "dp", scatter_dimension=axis, tiled=True).astype(F32)

    def sum_of(*values):
        return sum(v.astype(F32) for v in values)

    near = lambda *xs: [(x, vmem()) for x in xs]
    away = lambda xs: [(x, hbm()) for x in xs]
    scalar = lambda *xs: [(x, smem()) for x in xs]
    vm = lambda shape, dtype=BF: (shape, dtype, vmem())
    hb = lambda shape, dtype=BF: (shape, dtype, hbm())
    buf = lambda *shape, dtype=BF: pltpu.VMEM(shape, dtype)

    shard, mlp_shard = call(
        pack_body,
        near(qkv_weight, out_weight, in_weight.transpose(0, 2, 1), down_weight),
        [vm((4, piece_rows, width)), vm((3, units, piece_rows))],
        name="pack",
    )
    qkvo = gather(shard, 1, "qkvo")
    (normed,) = call(norm_body, near(hidden_in, gain_one), [vm((rows, model))], name="norm")
    if direct:
        (normed,) = gate([normed], [qkvo[1], qkvo[2], qkvo[4]])
    normed_attn = spread(normed, "norm")
    table = jnp.asarray(angle_table(length))
    if direct:
        (mlp_along,) = gate([mlp_shard], [qkvo[6]])
        (mlp_across,) = gate([mlp_shard], [qkvo[5], qkvo[7]])
        z2, z1 = [depth(mlp_along, 2 * k, "mlp") for k in (2, 1)]
        (cotangent_there,) = gate([cotangent], [normed_attn[2]])
    else:
        cotangent_there = cotangent
    cot = spread(cotangent_there, "cot")
    if direct:
        before = []
    else:
        mlp, before = gather(mlp_shard, 2, "mlp"), []
    *parts, mixed, q, k, v, lse = call(
        body(attend_forward, n_pieces, piece, scale),
        scalar(offs, mine_one)
        + away(gate(normed_attn, [z1]) if direct else normed_attn)
        + away([table] + qkvo),
        [hb((rows, model))] * 4 + [hb((length, width))] * 4 + [vm((8, length), F32)],
        [buf(4, rows, model), buf(length // 2, 128, dtype=F32), buf(4, model, width)]
        + [buf(length, width)] * 4
        + [buf(length, model), sems(n_pieces), sems(13)],
        name="attend_forward",
    )
    if direct:
        y0, y1 = depth(mlp_across, 1, "mlp0"), depth(gate([z1], [qkvo[5], qkvo[7]])[0], 1, "mlp1")
        *parts, lse = gate(parts + [lse], [z2, y0, y1, cot[2]])
    attn_far = add(parts[2], tensor(parts[3], 1, "afar"))
    attn_near = tensor(parts[1], 1, "anear")
    attn_got = tensor(attn_far, 2, "afar")
    if direct:
        z3 = depth(gate([z2], [lse])[0], 2, "mlpfar")
        y2, y3 = [depth(gate([x], [lse])[0], 1, f"mlp{i}") for i, x in ((2, z2), (3, z3))]
        before = [y2, z3]
        mlp = [mlp_shard, y0, z1, y1, z2, y2, z3, y3]
    middle, normed_two = call(
        middle_rows,
        near(hidden_in, gain_two, *gate([parts[0]], before), attn_near, attn_got),
        [vm((rows, model), F32), vm((rows, model))],
        name="middle_rows",
    )

    normed_far = tensor(normed_two, 2, "norm2")
    (normed_relay,) = gate([normed_far], only_direct(mlp[5:]))
    normed_mlp = [normed_two, tensor(normed_two, 1, "norm2"), normed_far, tensor(normed_relay, 1, "norm2far")]
    far_back, far_send, far_out, far_out_send, far_hidden, far_grad = call(
        body(feed_far, n_pieces, piece),
        scalar(offs) + away(normed_mlp[2:] + cot[2:] + mlp),
        [hb((rows, model))] * 4 + [vm((units, 2 * rows)), vm((2, units, 2 * rows))],
        [buf(2 * rows, model)] * 4 + [buf(3, units, model), sems(3, n_pieces), sems(4)],
        name="feed_far",
    )
    far_sum = add(far_back, tensor(far_send, 1, "far"))
    from_far = tensor(far_sum, 2, "far")
    near_back, near_send, near_out, near_out_send, near_hidden, near_grad, *grads = call(
        body(feed_near, n_pieces, piece),
        scalar(offs, cols)
        + away(gate(normed_mlp, [far_sum]) + cot + [far_hidden, far_grad] + mlp),
        [hb((rows, model))] * 4
        + [vm((units, 2 * rows)), vm((2, units, 2 * rows))]
        + [hb((3, units, 128))] * 4,
        [buf(length, model)] * 2
        + [buf(units, 2 * rows), buf(2, units, 2 * rows)]
        + [buf(2 * rows, model)] * 2
        + [buf(2, 2, 3, units, 128), buf(3, units, model), sems(3, n_pieces), sems(10)],
        name="feed_near",
    )
    near_got = tensor(near_send, 1, "near")
    out_sum = add(far_out, tensor(far_out_send, 1, "lofar"))
    out_near = tensor(near_out_send, 1, "lonear")

    middle_grad, low_grad, gain_two_part = call(
        middle_back,
        near(middle, cotangent, gain_two, near_back, near_got, from_far),
        [vm((rows, model), F32), vm((rows, model)), vm((8, 128), F32)],
        name="middle_back",
    )
    attn_out_grad = spread(low_grad, "aog")
    if direct:
        (grads[0],) = gate(grads[:1], [from_far])
        got = [depth(grads[0], 1, "gmlp0")]
        sums = [add(grads[1], got[0])]
        (grads[2],) = gate(grads[2:3], sums)
        before = [low_grad, sums[0], out_sum, out_near]
    else:
        before = [low_grad]
    grads += call(
        body(feed_late),
        scalar(cols)
        + away(gate(normed_mlp, before) + cot + [near_hidden, far_hidden, near_grad, far_grad]),
        [hb((3, units, 128))] * 4,
        [buf(length, model)] * 2
        + [buf(units, 2 * rows)] * 2
        + [buf(2, units, 2 * rows)] * 2
        + [buf(2, 2, 3, units, 128), sems(12)],
        name="feed_late",
    )
    early = [grads[7]]
    if direct:
        grads[4], grads[6] = gate([grads[4], grads[6]], [attn_out_grad[2]])
        got += [depth(grads[2 * i], 1, f"gmlp{i}") for i in (1, 2, 3)]
        sums.append(add(grads[3], got[1]))
        back = [depth(sums[i], 2, f"gmlpz{i}") for i in range(2)]
        early.append(sums[1])

    *attn, b0, b1, b2, b3, gains = call(
        body(attend_backward, n_pieces, piece, scale),
        scalar(cols, mine_one, offs)
        + near(gain_one, gain_two_part)
        + away(gate(attn_out_grad, early) + [mixed, q, k, v, lse, table] + normed_attn + qkvo),
        [hb((4, 128, width))] * 8
        + [hb((rows, model))] * 3
        + [hb((rows + 16, model)), vm((16, 128), F32)],
        [buf(length, 3 * width)]
        + [buf(length, width)] * 5
        + [buf(8, length, dtype=F32), buf(length // 2, 128, dtype=F32), buf(length, model), buf(length, model)]
        + [buf(8, length, dtype=F32), buf(length, width, dtype=F32)]
        + [buf(4, model, width), buf(4, 2, 4, 128, width), buf(length + 16, model)]
        + [sems(n_pieces), sems(17)],
        name="attend_backward",
    )
    if direct:
        late = sum_of(gate([grads[5]], [b0])[0], got[2], back[1]).astype(BF)
        last = depth(late, 4, "gmlp")
        *attn, b3 = gate(attn + [b3], [late, back[0], got[3]])
        gqkv = [depth(attn[2 * i], 1, f"gqkv{i}") for i in range(3)]
        qkv_sums = [add(attn[2 * i + 1], gqkv[i]) for i in range(2)]
        qkv_back = [depth(qkv_sums[i], 2, f"gqkvz{i}") for i in range(2)]
    sent_far, gains = call(
        add_far,
        near(b2, tensor(b3, 1, "nfar"), gains),
        [vm((rows + 16, model)), vm((16, 128), F32)],
        name="add_far",
    )
    got_far = tensor(sent_far, 2, "nfar")
    (b1,) = gate([b1], [sent_far])
    near_sum = tensor(b1, 1, "nnear")
    gains = gains + (got_far[rows:, 0:128].astype(F32) + got_far[rows:, 128:256].astype(F32))
    if direct:
        gains = gains + depth(gains, 1, "gain")
        (b0,) = gate([b0], [last, gains])
    (input_grad,) = call(
        input_back,
        near(hidden_in, middle_grad, gain_one, b0, near_sum, got_far),
        [vm((rows, model), F32)],
        name="input_back",
    )
    out_far = tensor(gate([out_sum], [got_far])[0], 2, "lofar")
    out_near = near_out.astype(F32) + out_near.astype(F32)
    layer_out = (middle + (out_near + out_far.astype(F32))).astype(BF)

    if direct:
        (attn[6],) = gate(attn[6:7], [got_far])
        gains = gains + depth(gains, 2, "gain")
        gains = gains + depth(gains, 4, "gain")
        gqkv.append(depth(attn[6], 1, "gqkv3"))
        qkv_late = sum_of(attn[5], gqkv[2], qkv_back[1]).astype(BF)
        qkv_last = depth(qkv_late, 4, "gqkv")
        ends = [attn[7], gqkv[3], qkv_back[0], gate([qkv_last], [out_far, gains])[0]]
        qkv_shard = sum_of(*[x[0:3] for x in ends])
        out_shard = sum_of(*[x[3] for x in ends]).T
    else:
        gains = lax.psum(gains, "dp")
        attn_total = reduce(attn, 1, "gqkv")
        qkv_shard, out_shard = attn_total[0:3], attn_total[3].T
    gains = gains.reshape(2, model)

    if direct:
        ends = [grads[7], got[3], back[0], gate([last], [input_grad])[0]]
        in_shard = sum_of(*[x[0:2] for x in ends]).transpose(0, 2, 1)
        down_shard = sum_of(*[x[2] for x in ends])
    else:
        mlp_total = reduce(grads, 2, "gmlp")
        in_shard, down_shard = mlp_total[0:2].transpose(0, 2, 1), mlp_total[2]

    return (layer_out, input_grad, gains[0], qkv_shard, out_shard, gains[1], in_shard, down_shard)


def solution(mesh):
    sizes = (mesh.shape["dp"], mesh.shape["tensor"])
    return jax.shard_map(
        functools.partial(shards, sizes),
        mesh=mesh,
        in_specs=(
            P(("dp", "tensor"), None),
            P(),
            P(None, "dp", "tensor"),
            P("tensor", "dp"),
            P(),
            P(None, "dp", "tensor"),
            P("tensor", "dp"),
            P(("dp", "tensor"), None),
        ),
        out_specs=(
            P(("dp", "tensor"), None),
            P(("dp", "tensor"), None),
            P(),
            P(None, "dp", "tensor"),
            P("tensor", "dp"),
            P(),
            P(None, "dp", "tensor"),
            P("tensor", "dp"),
        ),
        check_vma=False,
    )
```

```python
import functools
import math

import jax
import jax.numpy as jnp
import numpy as np
from jax import lax
from jax.experimental import pallas as pl
from jax.experimental.pallas import tpu as pltpu
from jax.sharding import PartitionSpec as P

HD = 64
NORM_EPS = 1e-05
ROPE_BASE = 160000.0
BF = jnp.bfloat16
F32 = jnp.float32
LOG2E = math.log2(math.e)
COST = 1000
VMEM_MIB = 32

NN = (((1,), (0,)), ((), ()))
NT = (((1,), (1,)), ((), ()))
TN = (((0,), (0,)), ((), ()))


def mm(a, b, dims=NN):
    return lax.dot_general(a, b, dims, preferred_element_type=F32)


def vmem():
    return pl.BlockSpec(memory_space=pltpu.VMEM)


def smem():
    return pl.BlockSpec(memory_space=pltpu.SMEM)


def hbm():
    return pl.BlockSpec(memory_space=pltpu.HBM)


def call(body, ins, outs, scratch=(), name=None):
    return pl.pallas_call(
        body,
        out_shape=[jax.ShapeDtypeStruct(o[0], o[1]) for o in outs],
        in_specs=[i[1] for i in ins],
        out_specs=[o[2] for o in outs],
        scratch_shapes=list(scratch),
        compiler_params=pltpu.CompilerParams(vmem_limit_bytes=VMEM_MIB * 1024 * 1024),
        cost_estimate=pl.CostEstimate(flops=COST, transcendentals=0, bytes_accessed=COST),
        name=name,
    )(*[i[0] for i in ins])


def swap(value, axis, size, distance, label):
    with jax.named_scope(label):
        return lax.ppermute(value, axis, [(i, i ^ distance) for i in range(size)])


def gate(values, others):
    return list(lax.optimization_barrier((tuple(values), tuple(others)))[0])


def start(source, target, sem):
    copy = pltpu.make_async_copy(source, target, sem)
    copy.start()
    return copy


def start_pieces(pieces, offs, size, target, sem, axis):
    copies = []
    for i, piece in enumerate(pieces):
        where = pl.ds(pl.multiple_of(offs[i] * size, size), size)
        copies.append(start(piece, target.at[(slice(None),) * axis + (where,)], sem.at[i]))
    return copies


def stop_rows(source, targets, sem, at):
    rows = targets[0].shape[0]
    return [
        start(source.at[pl.ds(i * rows, rows)], x, sem.at[at + i]) for i, x in enumerate(targets)
    ]


def wait(copies):
    for c in copies:
        c.wait()


def angles_at(table, block, rows):
    both = table[pl.ds(pl.multiple_of((block & 1) * rows, rows), rows), :]
    here = jnp.where(block < 2, both, pltpu.roll(both, 64, 1))
    a, b, c = [pltpu.roll(here, shift, 1) for shift in (32, 64, 96)]
    lane = lax.broadcasted_iota(jnp.int32, both.shape, 1)
    even = (lane & 63) < 32
    cos = jnp.where(lane < 64, jnp.where(even, here, a), jnp.where(even, b, c))
    sin = jnp.where(lane < 64, jnp.where(even, -c, here), jnp.where(even, -a, b))
    return cos, sin


def turn(u, cos, sin):
    lane = lax.broadcasted_iota(jnp.int32, u.shape, 1)
    low = (lane & 63) < 32
    turned = jnp.where(low, pltpu.roll(u, 96, 1), pltpu.roll(u, 32, 1))
    return u * cos + turned * sin


def head_mask(shape, head):
    lane = lax.broadcasted_iota(jnp.int32, shape, 1)
    return (lane >> 6) == head


def attend_forward(n_pieces, piece_rows, scale, refs):
    offs, mine = refs[:2]
    norms, table = refs[2:6], refs[6]
    pieces = refs[7 : 7 + n_pieces]
    refs = refs[7 + n_pieces :]
    parts, (mixed_out, q_out, k_out, v_out, lse_ref) = refs[0:4], refs[4:9]
    n, tab, w, q, k, v, mixed, part, sem_w, sem = refs[9:]
    rows, width = n.shape[1], w.shape[2]
    loads = start_pieces(pieces, offs, piece_rows, w, sem_w, 1)
    norm_loads = [start(norms[i], n.at[i], sem.at[i]) for i in range(4)]
    table_load = start(table, tab, sem.at[4])
    wait(loads)
    table_load.wait()
    wait(norm_loads)

    def project(i, carry):
        at = pl.ds(pl.multiple_of(i * rows, rows), rows)
        cos, sin = angles_at(tab, mine[0] ^ i, rows)
        for j, ref in ((0, q), (1, k)):
            u = mm(n[i], w[j])
            for g in range(width // 128):
                col = slice(g * 128, g * 128 + 128)
                ref[at, col] = turn(u[:, col], cos, sin).astype(BF)
        v[at, :] = mm(n[i], w[2]).astype(BF)
        return carry

    lax.fori_loop(0, 4, project, 0)
    stores = [start(x, y, sem.at[5 + i]) for i, (x, y) in enumerate(((q, q_out), (k, k_out), (v, v_out)))]
    factor = scale * LOG2E
    heads = width // HD
    group = 2 * rows

    def attend(half, carry):
        at = pl.ds(pl.multiple_of(half * group, group), group)
        masks = [head_mask((group, width), h) for h in range(heads)]

        def scores(h):
            return mm(jnp.where(masks[h], q[at, :], jnp.zeros((), BF)), k[...], NT)

        acc = jnp.zeros((group, width), F32)
        s = scores(0)
        for h in range(heads):
            ahead = scores(h + 1) if h + 1 < heads else None
            top = jnp.max(s, axis=1, keepdims=True)
            e = jnp.exp2((s - top) * factor)
            total = jnp.sum(e, axis=1, keepdims=True)
            o = mm(e.astype(BF), v[...]) * (1.0 / total)
            lse2 = top * factor + jnp.log2(total)
            row = jnp.transpose(jnp.broadcast_to(lse2, (group, 128)))
            lse_ref[pl.ds(h, 1), at] = row[0:1, :]
            acc = jnp.where(masks[h], o, acc)
            s = ahead
        low = acc.astype(BF)
        mixed[at, :] = low
        part[at, :] = mm(low, w[3], NT).astype(BF)
        return carry

    lax.fori_loop(0, 2, attend, 0)
    stores.append(start(mixed, mixed_out, sem.at[8]))
    stores += stop_rows(part, parts, sem, 9)
    wait(stores)


def norm_stats(v):
    mean = jnp.mean(v, axis=-1, keepdims=True)
    centred = v - mean
    spread = jnp.mean(centred * centred, axis=-1, keepdims=True)
    r = lax.rsqrt(spread + NORM_EPS)
    return centred * r, r


def norm_body(h_ref, gain_ref, o_ref):
    xhat, _ = norm_stats(h_ref[...].astype(F32))
    o_ref[...] = (xhat * gain_ref[...]).astype(BF)


def pack_body(qkv, out, inner, down, first, second):
    first[0:3] = qkv[...]
    first[3] = out[...].T
    second[0:2] = inner[...]
    second[2] = down[...]


def middle_rows(h_ref, gain, a, b, c, mid_ref, norm_ref):
    total = h_ref[...].astype(F32) + (a[...].astype(F32) + b[...].astype(F32) + c[...].astype(F32))
    mid_ref[...] = total
    xhat, _ = norm_stats(total)
    norm_ref[...] = (xhat * gain[...]).astype(BF)


INV_SQRT2 = 1.0 / math.sqrt(2.0)
INV_SQRT2PI = 1.0 / math.sqrt(2.0 * math.pi)


def feed_rows(n, c, w, grad, out, hid, gug, count, rows):
    def one_block(i, carry):
        at = pl.ds(pl.multiple_of(i * rows, rows), rows)
        gate = mm(n[at, :], w[0], NT)
        up = mm(n[at, :], w[1], NT)
        back = mm(c[at, :], w[2], NT)
        cdf = 0.5 * (1.0 + lax.erf(gate * INV_SQRT2))
        pdf = jnp.exp(-0.5 * gate * gate) * INV_SQRT2PI
        act = gate * cdf
        hidden = (act * up).astype(BF)
        g0 = (back * up * (cdf + gate * pdf)).astype(BF)
        g1 = (back * act).astype(BF)
        grad[at, :] = (mm(g0, w[0]) + mm(g1, w[1])).astype(BF)
        out[at, :] = mm(hidden, w[2]).astype(BF)
        hid[:, at] = hidden.T
        gug[0, :, at] = g0.T
        gug[1, :, at] = g1.T
        return carry

    lax.fori_loop(0, count, one_block, 0)


def load_mlp(pieces, offs, size, w, sem):
    return [
        start_pieces([x.at[j] for x in pieces], offs, size, w.at[j], sem.at[j], 1) for j in range(3)
    ]


def feed_far(n_pieces, size, refs):
    offs, n_in, c_in, pieces = refs[0], refs[1:3], refs[3:5], refs[5 : 5 + n_pieces]
    refs = refs[5 + n_pieces :]
    grads, outs, (hid, gug) = refs[0:2], refs[2:4], refs[4:6]
    n, c, grad, out, w, sem_w, sem = refs[6:]
    loads = start_rows(n_in, n, sem, 0) + start_rows(c_in, c, sem, 2)
    for group in load_mlp(pieces, offs, size, w, sem_w):
        wait(group)
    wait(loads)
    feed_rows(n, c, w, grad, out, hid, gug, 2, n_in[0].shape[0])
    wait(stop_rows(grad, grads, sem, 0) + stop_rows(out, outs, sem, 2))


def pick_columns(ref, first, second, size):
    a = ref[:, pl.ds(pl.multiple_of(first * size, size), size)]
    b = ref[:, pl.ds(pl.multiple_of(second * size, size), size)]
    return jnp.concatenate([a, b], axis=1)


def mlp_grads(cols, first_block, n, c, hidden, grads, block_sums):
    group = hidden[0].shape[1]

    def one_block(k, carry):
        at = 2 * (first_block + k)
        rights = [pick_columns(x, cols[at], cols[at + 1], 128) for x in (n, c)]
        for j in range(3):
            left = hidden if j == 2 else [x.at[j] for x in grads]
            right = rights[1] if j == 2 else rights[0]
            total = mm(left[0][...], right[:group]) + mm(left[1][...], right[group:])
            block_sums[k, 0, j] = total[:, :128].astype(BF)
            block_sums[k, 1, j] = total[:, 128:].astype(BF)
        return carry

    lax.fori_loop(0, 2, one_block, 0)


def stop_blocks(block_sums, blocks, sem, at):
    return [start(block_sums.at[i // 2, i % 2], x, sem.at[at + i]) for i, x in enumerate(blocks)]


def start_rows(sources, target, sem, at):
    rows = sources[0].shape[0]
    return [start(x, target.at[pl.ds(i * rows, rows)], sem.at[at + i]) for i, x in enumerate(sources)]


def feed_near(n_pieces, size, refs):
    offs, cols, n_in, c_in, hid_far, gug_far = refs[0], refs[1], refs[2:6], refs[6:10], refs[10], refs[11]
    pieces = refs[12 : 12 + n_pieces]
    refs = refs[12 + n_pieces :]
    grads, outs, (hid, gug), blocks = refs[0:2], refs[2:4], refs[4:6], refs[6:10]
    n, c, hf, gf, grad, out, block_sums, w, sem_w, sem = refs[10:]
    loads = start_rows(n_in, n, sem, 0)
    groups = load_mlp(pieces, offs, size, w, sem_w)
    loads += start_rows(c_in, c, sem, 4)
    late = [start(hid_far, hf, sem.at[8]), start(gug_far, gf, sem.at[9])]
    for group in groups:
        wait(group)
    wait(loads)
    feed_rows(n, c, w, grad, out, hid, gug, 2, n_in[0].shape[0])
    wait(late)
    stores = stop_rows(grad, grads, sem, 0) + stop_rows(out, outs, sem, 2)
    mlp_grads(cols, 0, n, c, (hid, hf), (gug, gf), block_sums)
    wait(stores + stop_blocks(block_sums, blocks, sem, 4))


def feed_late(refs):
    cols, n_in, c_in = refs[0], refs[1:5], refs[5:9]
    sources, blocks = refs[9:13], refs[13:17]
    n, c, hn, hf, gn, gf, block_sums, sem = refs[17:]
    loads = start_rows(n_in, n, sem, 0)
    loads += [start(x, y, sem.at[8 + i]) for i, (x, y) in enumerate(zip(sources, (hn, hf, gn, gf)))]
    loads += start_rows(c_in, c, sem, 4)
    wait(loads)
    mlp_grads(cols, 2, n, c, (hn, hf), (gn, gf), block_sums)
    wait(stop_blocks(block_sums, blocks, sem, 0))


def norm_back(v, g):
    xhat, r = norm_stats(v)
    mean_g = jnp.mean(g, axis=-1, keepdims=True)
    mean_gx = jnp.mean(g * xhat, axis=-1, keepdims=True)
    return r * (g - mean_g - xhat * mean_gx), xhat


def middle_back(mid, cot, gain, sa, sb, sc, mg_ref, low_ref, gain_ref):
    got = sa[...].astype(F32) + sb[...].astype(F32) + sc[...].astype(F32)
    back, xhat = norm_back(mid[...], gain[...] * got)
    sums = jnp.sum(got * xhat, axis=0, keepdims=True)
    for i in range(8):
        gain_ref[pl.ds(i, 1), :] = sums[:, 128 * i : 128 * i + 128]
    mg = cot[...].astype(F32) + back
    mg_ref[...] = mg
    low_ref[...] = mg.astype(BF)


def attend_backward(n_pieces, piece_rows, scale, refs):
    cols, mine, offs, gain, gain_two = refs[:5]
    refs = refs[5:]
    grads_in, mixed_in, q_in, k_in, v_in, lse_in, table, norms = (
        refs[0:4], refs[4], refs[5], refs[6], refs[7], refs[8], refs[9], refs[10:14]
    )
    pieces = refs[14 : 14 + n_pieces]
    refs = refs[14 + n_pieces :]
    outs, parts, gain_ref = refs[0:8], refs[8:12], refs[12]
    pg, do, o, q, k, v, lse, tab, n, a, dot_rows, dq, w, block_sums, sent, sem_w, sem = refs[13:]
    rows = grads_in[0].shape[0]
    length, width = q.shape
    heads = width // HD
    weights = start_pieces(pieces, offs, piece_rows, w, sem_w, 1)
    grads = start_rows(grads_in, a, sem, 0)
    pairs = ((mixed_in, o), (q_in, q), (k_in, k), (v_in, v), (lse_in, lse))
    near = [start(x, y, sem.at[4 + i]) for i, (x, y) in enumerate(pairs)]
    late = [start(table, tab, sem.at[12])]
    late += start_rows(norms, n, sem, 13)
    wait(weights)
    wait(grads)
    wait(near)
    lane = lax.broadcasted_iota(jnp.int32, (8, width), 1) >> 6
    head = lax.broadcasted_iota(jnp.int32, (8, width), 0)
    ones = jnp.where(lane == head, 1.0, 0.0).astype(BF)

    def output_grads(i, carry):
        at = pl.ds(pl.multiple_of(i * rows, rows), rows)
        d = mm(a[at, :], w[3]).astype(BF)
        do[at, :] = d
        t = d.astype(F32) * o[at, :].astype(F32)
        hi = t.astype(BF)
        lo = (t - hi.astype(F32)).astype(BF)
        dot_rows[:, at] = mm(ones, hi, NT) + mm(ones, lo, NT)
        return carry

    lax.fori_loop(0, 4, output_grads, 0, unroll=2)
    dq[...] = jnp.zeros_like(dq)
    factor = scale * LOG2E
    nil = jnp.zeros((), BF)

    def one_block(i, carry):
        at = pl.ds(pl.multiple_of(i * rows, rows), rows)
        dk_acc = jnp.zeros((rows, width), F32)
        dv_acc = jnp.zeros((rows, width), F32)
        dq_acc = None
        for h in range(heads):
            mask = head_mask((length, width), h)
            qm = jnp.where(mask, q[...], nil)
            dom = jnp.where(mask, do[...], nil)
            km = jnp.where(head_mask((rows, width), h), k[at, :], nil)
            s = mm(k[at, :], qm, NT)
            dp = mm(v[at, :], dom, NT)
            p = jnp.exp2(s * factor - lse[pl.ds(h, 1), :])
            ds = (p * (dp - dot_rows[pl.ds(h, 1), :])).astype(BF)
            dv_acc = dv_acc + mm(p.astype(BF), dom)
            dk_acc = dk_acc + mm(ds, qm)
            part = mm(ds, km, TN)
            dq_acc = part if dq_acc is None else dq_acc + part
        dq[...] += dq_acc
        cos, sin = angles_at(tab, mine[0] ^ i, rows)
        for g in range(width // 128):
            col = slice(g * 128, g * 128 + 128)
            to = slice(width + g * 128, width + g * 128 + 128)
            pg[at, to] = turn(dk_acc[:, col] * scale, cos, -sin).astype(BF)
        pg[at, 2 * width :] = dv_acc.astype(BF)
        return carry

    wait(late[:1])
    lax.fori_loop(0, 4, one_block, 0)

    def query_grads(i, carry):
        at = pl.ds(pl.multiple_of(i * rows, rows), rows)
        cos, sin = angles_at(tab, mine[0] ^ i, rows)
        for g in range(width // 128):
            col = slice(g * 128, g * 128 + 128)
            pg[at, col] = turn(dq[at, col] * scale, cos, -sin).astype(BF)
        return carry

    lax.fori_loop(0, 4, query_grads, 0)
    wait(late[1:])

    def weight_grads(block, carry):
        first, second = cols[2 * block], cols[2 * block + 1]
        total = mm(pick_columns(n, first, second, 128), pg[...], TN)
        last = mm(pick_columns(a, first, second, 128), o[...], TN)
        for j in range(4):
            part = last if j == 3 else total[:, j * width : (j + 1) * width]
            part = part.astype(BF)
            block_sums[block, 0, j] = part[:128]
            block_sums[block, 1, j] = part[128:]
        return carry

    lax.fori_loop(0, 4, weight_grads, 0, unroll=True)
    stores = stop_blocks(block_sums, outs, sem, 0)

    def row_grads(i, sums):
        at = pl.ds(pl.multiple_of(i * rows, rows), rows)
        total = sum(mm(pg[at, j * width : (j + 1) * width], w[j], NT) for j in range(3))
        sent[at, :] = total.astype(BF)
        return sums + jnp.sum(total * n[at, :].astype(F32), axis=0, keepdims=True)

    sums = lax.fori_loop(0, 4, row_grads, jnp.zeros((1, n.shape[1]), F32), unroll=2)
    sums = sums / gain[...]
    both = [sums[:, 128 * i : 128 * i + 128] for i in range(8)] + [gain_two[...]]
    gain_ref[...] = write_gains(sent, length, jnp.concatenate(both, axis=0))
    ends = [rows] * 3 + [rows + 16]
    for i in range(4):
        stores.append(start(sent.at[pl.ds(i * rows, ends[i])], parts[i], sem.at[8 + i]))
    wait(stores)


def write_gains(ref, rows, gains):
    high = gains.astype(BF)
    low = (gains - high.astype(F32)).astype(BF)
    tail = pl.ds(rows, 16)
    ref[tail, :] = jnp.zeros((16, ref.shape[1]), BF)
    ref[tail, 0:128] = high
    ref[tail, 128:256] = low
    return high.astype(F32) + low.astype(F32)


def read_gains(ref, rows):
    tail = pl.ds(rows, 16)
    return ref[tail, 0:128].astype(F32) + ref[tail, 128:256].astype(F32)


def add_far(part, got, gains, o_ref, gains_ref):
    rows = part.shape[0]
    o_ref[pl.ds(0, rows), :] = (part[...].astype(F32) + got[pl.ds(0, rows), :].astype(F32)).astype(BF)
    gains_ref[...] = write_gains(o_ref, rows, gains[...] + read_gains(got, rows))


def input_back(h, mg, gain, sa, sb, sc, o_ref):
    got = sa[...].astype(F32) + sb[...].astype(F32) + sc[pl.ds(0, sa.shape[0]), :].astype(F32)
    back, _ = norm_back(h[...].astype(F32), gain[...] * got)
    o_ref[...] = mg[...] + back


def body(function, *static):
    return lambda *refs: function(*static, refs)


def angle_table(length):
    exponents = np.arange(0, HD, 2).astype(np.float32) / np.float32(HD)
    inverse = np.float32(ROPE_BASE) ** (-exponents)
    angles = np.arange(length).astype(np.float32)[:, None] * inverse[None, :]
    cos, sin = np.cos(angles), np.sin(angles)
    half = length // 2
    return np.concatenate([cos[:half], sin[:half], cos[half:], sin[half:]], axis=1).astype(np.float32)


def shards(sizes, *args):
    hidden_in, attn_gain, qkv_weight, out_weight, mlp_gain, in_weight, down_weight, cotangent = args
    dp, tp = sizes
    rows, model = hidden_in.shape
    length = rows * tp
    piece_rows = qkv_weight.shape[1]
    width = qkv_weight.shape[2]
    units = in_weight.shape[2]
    scale = HD ** (-0.5)
    direct = dp == 8
    mine_one = lax.axis_index("tensor").astype(jnp.int32).reshape(1)
    place = lax.axis_index("dp")
    gain_one, gain_two = attn_gain.reshape(1, model), mlp_gain.reshape(1, model)

    def tensor(value, k, label):
        return swap(value, "tensor", tp, k, f"{label}_t{k}")

    def depth(value, k, label):
        return swap(value, "dp", dp, k, f"{label}_d{k}")

    def gather(shard, axis, label):
        if direct:
            far = depth(shard, 4, label)
            along = [shard, depth(shard, 2, label), far, depth(far, 2, label + "far")]
            across = [depth(v, 1, f"{label}{i}") for i, v in enumerate(along[:3])]
            across.append(depth(gate(along[3:], across[1:2])[0], 1, label + "3"))
            return [v for pair in zip(along, across) for v in pair]
        return [lax.all_gather(shard, "dp", axis=axis, tiled=True)]

    def only_direct(values):
        return values if direct else []

    if direct:
        offs = place ^ jnp.arange(8, dtype=jnp.int32)
        n_pieces, piece = 8, piece_rows
        z, y = place // 2, place % 2
        order = [1, 3, 2, 0]
        cols = jnp.stack([c for b in order for c in ((z ^ b) * 2 + (1 - y), (z ^ b) * 2 + y)])
    else:
        offs = jnp.zeros((1,), jnp.int32)
        n_pieces, piece = 1, model
        cols = jnp.arange(8, dtype=jnp.int32)
    cols = cols.astype(jnp.int32)
    sems = lambda *s: pltpu.SemaphoreType.DMA(s)
    add = lambda a, b: (a.astype(F32) + b.astype(F32)).astype(BF)

    def spread(own, label):
        far = tensor(own, 2, label)
        return [own, tensor(own, 1, label), far, tensor(far, 1, label + "far")]

    def exchange(blocks, label):
        return [blocks[0]] + [tensor(blocks[k], k, label) for k in (1, 2, 3)]

    def reduce(blocks, axis, label):
        whole = jnp.concatenate(blocks, axis=axis)
        return lax.psum_scatter(whole, "dp", scatter_dimension=axis, tiled=True).astype(F32)

    def sum_of(*values):
        return sum(v.astype(F32) for v in values)

    near = lambda *xs: [(x, vmem()) for x in xs]
    away = lambda xs: [(x, hbm()) for x in xs]
    scalar = lambda *xs: [(x, smem()) for x in xs]
    vm = lambda shape, dtype=BF: (shape, dtype, vmem())
    hb = lambda shape, dtype=BF: (shape, dtype, hbm())
    buf = lambda *shape, dtype=BF: pltpu.VMEM(shape, dtype)

    shard, mlp_shard = call(
        pack_body,
        near(qkv_weight, out_weight, in_weight.transpose(0, 2, 1), down_weight),
        [vm((4, piece_rows, width)), vm((3, units, piece_rows))],
        name="pack",
    )
    qkvo = gather(shard, 1, "qkvo")
    (normed,) = call(norm_body, near(hidden_in, gain_one), [vm((rows, model))], name="norm")
    if direct:
        (normed,) = gate([normed], [qkvo[1], qkvo[2], qkvo[4]])
    normed_attn = spread(normed, "norm")
    table = jnp.asarray(angle_table(length))
    if direct:
        (mlp_along,) = gate([mlp_shard], [qkvo[6]])
        (mlp_across,) = gate([mlp_shard], [qkvo[5], qkvo[7]])
        z2, z1 = [depth(mlp_along, 2 * k, "mlp") for k in (2, 1)]
        (cotangent_there,) = gate([cotangent], [normed_attn[2]])
    else:
        cotangent_there = cotangent
    cot = spread(cotangent_there, "cot")
    if direct:
        before = []
    else:
        mlp, before = gather(mlp_shard, 2, "mlp"), []
    *parts, mixed, q, k, v, lse = call(
        body(attend_forward, n_pieces, piece, scale),
        scalar(offs, mine_one)
        + away(gate(normed_attn, [z1]) if direct else normed_attn)
        + away([table] + qkvo),
        [hb((rows, model))] * 4 + [hb((length, width))] * 4 + [vm((8, length), F32)],
        [buf(4, rows, model), buf(length // 2, 128, dtype=F32), buf(4, model, width)]
        + [buf(length, width)] * 4
        + [buf(length, model), sems(n_pieces), sems(13)],
        name="attend_forward",
    )
    if direct:
        y0, y1 = depth(mlp_across, 1, "mlp0"), depth(gate([z1], [qkvo[5], qkvo[7]])[0], 1, "mlp1")
        *parts, lse = gate(parts + [lse], [z2, y0, y1, cot[2]])
    attn_far = add(parts[2], tensor(parts[3], 1, "afar"))
    attn_near = tensor(parts[1], 1, "anear")
    attn_got = tensor(attn_far, 2, "afar")
    if direct:
        z3 = depth(gate([z2], [lse])[0], 2, "mlpfar")
        y2, y3 = [depth(gate([x], [lse])[0], 1, f"mlp{i}") for i, x in ((2, z2), (3, z3))]
        before = [y2, z3]
        mlp = [mlp_shard, y0, z1, y1, z2, y2, z3, y3]
    middle, normed_two = call(
        middle_rows,
        near(hidden_in, gain_two, *gate([parts[0]], before), attn_near, attn_got),
        [vm((rows, model), F32), vm((rows, model))],
        name="middle_rows",
    )

    normed_far = tensor(normed_two, 2, "norm2")
    (normed_relay,) = gate([normed_far], only_direct(mlp[5:]))
    normed_mlp = [normed_two, tensor(normed_two, 1, "norm2"), normed_far, tensor(normed_relay, 1, "norm2far")]
    far_back, far_send, far_out, far_out_send, far_hidden, far_grad = call(
        body(feed_far, n_pieces, piece),
        scalar(offs) + away(normed_mlp[2:] + cot[2:] + mlp),
        [hb((rows, model))] * 4 + [vm((units, 2 * rows)), vm((2, units, 2 * rows))],
        [buf(2 * rows, model)] * 4 + [buf(3, units, model), sems(3, n_pieces), sems(4)],
        name="feed_far",
    )
    far_sum = add(far_back, tensor(far_send, 1, "far"))
    from_far = tensor(far_sum, 2, "far")
    near_back, near_send, near_out, near_out_send, near_hidden, near_grad, *grads = call(
        body(feed_near, n_pieces, piece),
        scalar(offs, cols)
        + away(gate(normed_mlp, [far_sum]) + cot + [far_hidden, far_grad] + mlp),
        [hb((rows, model))] * 4
        + [vm((units, 2 * rows)), vm((2, units, 2 * rows))]
        + [hb((3, units, 128))] * 4,
        [buf(length, model)] * 2
        + [buf(units, 2 * rows), buf(2, units, 2 * rows)]
        + [buf(2 * rows, model)] * 2
        + [buf(2, 2, 3, units, 128), buf(3, units, model), sems(3, n_pieces), sems(10)],
        name="feed_near",
    )
    near_got = tensor(near_send, 1, "near")
    out_sum = add(far_out, tensor(far_out_send, 1, "lofar"))
    out_near = tensor(near_out_send, 1, "lonear")

    middle_grad, low_grad, gain_two_part = call(
        middle_back,
        near(middle, cotangent, gain_two, near_back, near_got, from_far),
        [vm((rows, model), F32), vm((rows, model)), vm((8, 128), F32)],
        name="middle_back",
    )
    attn_out_grad = spread(low_grad, "aog")
    if direct:
        (grads[0],) = gate(grads[:1], [from_far])
        got = [depth(grads[0], 1, "gmlp0")]
        sums = [add(grads[1], got[0])]
        (grads[2],) = gate(grads[2:3], sums)
        before = [low_grad, sums[0], out_sum, out_near]
    else:
        before = [low_grad]
    grads += call(
        body(feed_late),
        scalar(cols)
        + away(gate(normed_mlp, before) + cot + [near_hidden, far_hidden, near_grad, far_grad]),
        [hb((3, units, 128))] * 4,
        [buf(length, model)] * 2
        + [buf(units, 2 * rows)] * 2
        + [buf(2, units, 2 * rows)] * 2
        + [buf(2, 2, 3, units, 128), sems(12)],
        name="feed_late",
    )
    early = [grads[7]]
    if direct:
        grads[4], grads[6] = gate([grads[4], grads[6]], [attn_out_grad[2]])
        got += [depth(grads[2 * i], 1, f"gmlp{i}") for i in (1, 2, 3)]
        sums.append(add(grads[3], got[1]))
        back = [depth(sums[i], 2, f"gmlpz{i}") for i in range(2)]
        early.append(sums[1])

    *attn, b0, b1, b2, b3, gains = call(
        body(attend_backward, n_pieces, piece, scale),
        scalar(cols, mine_one, offs)
        + near(gain_one, gain_two_part)
        + away(gate(attn_out_grad, early) + [mixed, q, k, v, lse, table] + normed_attn + qkvo),
        [hb((4, 128, width))] * 8
        + [hb((rows, model))] * 3
        + [hb((rows + 16, model)), vm((16, 128), F32)],
        [buf(length, 3 * width)]
        + [buf(length, width)] * 5
        + [buf(8, length, dtype=F32), buf(length // 2, 128, dtype=F32), buf(length, model), buf(length, model)]
        + [buf(8, length, dtype=F32), buf(length, width, dtype=F32)]
        + [buf(4, model, width), buf(4, 2, 4, 128, width), buf(length + 16, model)]
        + [sems(n_pieces), sems(17)],
        name="attend_backward",
    )
    if direct:
        late = sum_of(gate([grads[5]], [b0])[0], got[2], back[1]).astype(BF)
        last = depth(late, 4, "gmlp")
        *attn, b3 = gate(attn + [b3], [late, back[0], got[3]])
        gqkv = [depth(attn[2 * i], 1, f"gqkv{i}") for i in range(3)]
        qkv_sums = [add(attn[2 * i + 1], gqkv[i]) for i in range(2)]
        qkv_back = [depth(qkv_sums[i], 2, f"gqkvz{i}") for i in range(2)]
    sent_far, gains = call(
        add_far,
        near(b2, tensor(b3, 1, "nfar"), gains),
        [vm((rows + 16, model)), vm((16, 128), F32)],
        name="add_far",
    )
    got_far = tensor(sent_far, 2, "nfar")
    (b1,) = gate([b1], [sent_far])
    near_sum = tensor(b1, 1, "nnear")
    gains = gains + (got_far[rows:, 0:128].astype(F32) + got_far[rows:, 128:256].astype(F32))
    if direct:
        gains = gains + depth(gains, 1, "gain")
        (b0,) = gate([b0], [last, gains])
    (input_grad,) = call(
        input_back,
        near(hidden_in, middle_grad, gain_one, b0, near_sum, got_far),
        [vm((rows, model), F32)],
        name="input_back",
    )
    out_far = tensor(gate([out_sum], [got_far])[0], 2, "lofar")
    out_near = near_out.astype(F32) + out_near.astype(F32)
    layer_out = (middle + (out_near + out_far.astype(F32))).astype(BF)

    if direct:
        (attn[6],) = gate(attn[6:7], [got_far])
        gains = gains + depth(gains, 2, "gain")
        gains = gains + depth(gains, 4, "gain")
        gqkv.append(depth(attn[6], 1, "gqkv3"))
        qkv_late = sum_of(attn[5], gqkv[2], qkv_back[1]).astype(BF)
        qkv_last = depth(qkv_late, 4, "gqkv")
        ends = [attn[7], gqkv[3], qkv_back[0], gate([qkv_last], [out_far, gains])[0]]
        qkv_shard = sum_of(*[x[0:3] for x in ends])
        out_shard = sum_of(*[x[3] for x in ends]).T
    else:
        gains = lax.psum(gains, "dp")
        attn_total = reduce(attn, 1, "gqkv")
        qkv_shard, out_shard = attn_total[0:3], attn_total[3].T
    gains = gains.reshape(2, model)

    if direct:
        ends = [grads[7], got[3], back[0], gate([last], [input_grad])[0]]
        in_shard = sum_of(*[x[0:2] for x in ends]).transpose(0, 2, 1)
        down_shard = sum_of(*[x[2] for x in ends])
    else:
        mlp_total = reduce(grads, 2, "gmlp")
        in_shard, down_shard = mlp_total[0:2].transpose(0, 2, 1), mlp_total[2]

    return (layer_out, input_grad, gains[0], qkv_shard, out_shard, gains[1], in_shard, down_shard)


def solution(mesh):
    sizes = (mesh.shape["dp"], mesh.shape["tensor"])
    return jax.shard_map(
        functools.partial(shards, sizes),
        mesh=mesh,
        in_specs=(
            P(("dp", "tensor"), None),
            P(),
            P(None, "dp", "tensor"),
            P("tensor", "dp"),
            P(),
            P(None, "dp", "tensor"),
            P("tensor", "dp"),
            P(("dp", "tensor"), None),
        ),
        out_specs=(
            P(("dp", "tensor"), None),
            P(("dp", "tensor"), None),
            P(),
            P(None, "dp", "tensor"),
            P("tensor", "dp"),
            P(),
            P(None, "dp", "tensor"),
            P("tensor", "dp"),
        ),
        check_vma=False,
    )
```

```python
import functools
import math

import jax
import jax.numpy as jnp
import numpy as np
from jax import lax
from jax.experimental import pallas as pl
from jax.experimental.pallas import tpu as pltpu
from jax.sharding import PartitionSpec as P

HD = 64
NORM_EPS = 1e-05
ROPE_BASE = 160000.0
BF = jnp.bfloat16
F32 = jnp.float32
LOG2E = math.log2(math.e)
COST = 1000
VMEM_MIB = 32

NN = (((1,), (0,)), ((), ()))
NT = (((1,), (1,)), ((), ()))
TN = (((0,), (0,)), ((), ()))


def mm(a, b, dims=NN):
    return lax.dot_general(a, b, dims, preferred_element_type=F32)


def vmem():
    return pl.BlockSpec(memory_space=pltpu.VMEM)


def smem():
    return pl.BlockSpec(memory_space=pltpu.SMEM)


def hbm():
    return pl.BlockSpec(memory_space=pl.ANY)


def call(body, ins, outs, scratch=(), name=None):
    return pl.pallas_call(
        body,
        out_shape=[jax.ShapeDtypeStruct(o[0], o[1]) for o in outs],
        in_specs=[i[1] for i in ins],
        out_specs=[o[2] for o in outs],
        scratch_shapes=list(scratch),
        compiler_params=pltpu.CompilerParams(vmem_limit_bytes=VMEM_MIB * 1024 * 1024),
        cost_estimate=pl.CostEstimate(flops=COST, transcendentals=0, bytes_accessed=COST),
        name=name,
    )(*[i[0] for i in ins])


def swap(value, axis, size, distance, label):
    with jax.named_scope(label):
        return lax.ppermute(value, axis, [(i, i ^ distance) for i in range(size)])


def gate(values, others):
    return list(lax.optimization_barrier((tuple(values), tuple(others)))[0])


def start(source, target, sem):
    copy = pltpu.make_async_copy(source, target, sem)
    copy.start()
    return copy


def start_pieces(pieces, offs, size, target, sem, axis):
    copies = []
    for i, piece in enumerate(pieces):
        where = pl.ds(pl.multiple_of(offs[i] * size, size), size)
        copies.append(start(piece, target.at[(slice(None),) * axis + (where,)], sem.at[i]))
    return copies


def stop_rows(source, targets, sem, at):
    rows = targets[0].shape[0]
    return [
        start(source.at[pl.ds(i * rows, rows)], x, sem.at[at + i]) for i, x in enumerate(targets)
    ]


def wait(copies):
    for c in copies:
        c.wait()


def angles_at(table, block, rows):
    both = table[pl.ds(pl.multiple_of((block & 1) * rows, rows), rows), :]
    here = jnp.where(block < 2, both, pltpu.roll(both, 64, 1))
    a, b, c = [pltpu.roll(here, shift, 1) for shift in (32, 64, 96)]
    lane = lax.broadcasted_iota(jnp.int32, both.shape, 1)
    even = (lane & 63) < 32
    cos = jnp.where(lane < 64, jnp.where(even, here, a), jnp.where(even, b, c))
    sin = jnp.where(lane < 64, jnp.where(even, -c, here), jnp.where(even, -a, b))
    return cos, sin


def turn(u, cos, sin):
    lane = lax.broadcasted_iota(jnp.int32, u.shape, 1)
    low = (lane & 63) < 32
    turned = jnp.where(low, pltpu.roll(u, 96, 1), pltpu.roll(u, 32, 1))
    return u * cos + turned * sin


def head_mask(shape, head):
    lane = lax.broadcasted_iota(jnp.int32, shape, 1)
    return (lane >> 6) == head


def attend_forward(n_pieces, piece_rows, scale, refs):
    offs, mine = refs[:2]
    norms, table = refs[2:6], refs[6]
    pieces = refs[7 : 7 + n_pieces]
    refs = refs[7 + n_pieces :]
    parts, (mixed_out, q_out, k_out, v_out, lse_ref) = refs[0:4], refs[4:9]
    n, tab, w, q, k, v, mixed, part, sem_w, sem = refs[9:]
    rows, width = n.shape[1], w.shape[2]
    loads = start_pieces(pieces, offs, piece_rows, w, sem_w, 1)
    norm_loads = [start(norms[i], n.at[i], sem.at[i]) for i in range(4)]
    table_load = start(table, tab, sem.at[4])
    wait(loads)
    table_load.wait()
    wait(norm_loads)

    def project(i, carry):
        at = pl.ds(pl.multiple_of(i * rows, rows), rows)
        cos, sin = angles_at(tab, mine[0] ^ i, rows)
        for j, ref in ((0, q), (1, k)):
            u = mm(n[i], w[j])
            for g in range(width // 128):
                col = slice(g * 128, g * 128 + 128)
                ref[at, col] = turn(u[:, col], cos, sin).astype(BF)
        v[at, :] = mm(n[i], w[2]).astype(BF)
        return carry

    lax.fori_loop(0, 4, project, 0)
    stores = [start(x, y, sem.at[5 + i]) for i, (x, y) in enumerate(((q, q_out), (k, k_out), (v, v_out)))]
    factor = scale * LOG2E
    heads = width // HD
    group = 2 * rows

    def attend(half, carry):
        at = pl.ds(pl.multiple_of(half * group, group), group)
        masks = [head_mask((group, width), h) for h in range(heads)]

        def scores(h):
            return mm(jnp.where(masks[h], q[at, :], jnp.zeros((), BF)), k[...], NT)

        acc = jnp.zeros((group, width), F32)
        s = scores(0)
        for h in range(heads):
            ahead = scores(h + 1) if h + 1 < heads else None
            top = jnp.max(s, axis=1, keepdims=True)
            e = jnp.exp2((s - top) * factor)
            total = jnp.sum(e, axis=1, keepdims=True)
            o = mm(e.astype(BF), v[...]) * (1.0 / total)
            lse2 = top * factor + jnp.log2(total)
            row = jnp.transpose(jnp.broadcast_to(lse2, (group, 128)))
            lse_ref[pl.ds(h, 1), at] = row[0:1, :]
            acc = jnp.where(masks[h], o, acc)
            s = ahead
        low = acc.astype(BF)
        mixed[at, :] = low
        part[at, :] = mm(low, w[3], NT).astype(BF)
        return carry

    lax.fori_loop(0, 2, attend, 0)
    stores.append(start(mixed, mixed_out, sem.at[8]))
    stores += stop_rows(part, parts, sem, 9)
    wait(stores)


def norm_stats(v):
    mean = jnp.mean(v, axis=-1, keepdims=True)
    centred = v - mean
    spread = jnp.mean(centred * centred, axis=-1, keepdims=True)
    r = lax.rsqrt(spread + NORM_EPS)
    return centred * r, r


def norm_body(h_ref, gain_ref, o_ref):
    xhat, _ = norm_stats(h_ref[...].astype(F32))
    o_ref[...] = (xhat * gain_ref[...]).astype(BF)


def pack_body(qkv, out, inner, down, first, second):
    first[0:3] = qkv[...]
    first[3] = out[...].T
    second[0:2] = inner[...]
    second[2] = down[...]


def middle_rows(h_ref, gain, a, b, c, mid_ref, norm_ref):
    total = h_ref[...].astype(F32) + (a[...].astype(F32) + b[...].astype(F32) + c[...].astype(F32))
    mid_ref[...] = total
    xhat, _ = norm_stats(total)
    norm_ref[...] = (xhat * gain[...]).astype(BF)


INV_SQRT2 = 1.0 / math.sqrt(2.0)
INV_SQRT2PI = 1.0 / math.sqrt(2.0 * math.pi)


def feed_rows(n, c, w, grad, out, hid, gug, count, rows):
    def one_block(i, carry):
        at = pl.ds(pl.multiple_of(i * rows, rows), rows)
        gate = mm(n[at, :], w[0], NT)
        up = mm(n[at, :], w[1], NT)
        back = mm(c[at, :], w[2], NT)
        cdf = 0.5 * (1.0 + lax.erf(gate * INV_SQRT2))
        pdf = jnp.exp(-0.5 * gate * gate) * INV_SQRT2PI
        act = gate * cdf
        hidden = (act * up).astype(BF)
        g0 = (back * up * (cdf + gate * pdf)).astype(BF)
        g1 = (back * act).astype(BF)
        grad[at, :] = (mm(g0, w[0]) + mm(g1, w[1])).astype(BF)
        out[at, :] = mm(hidden, w[2]).astype(BF)
        hid[:, at] = hidden.T
        gug[0, :, at] = g0.T
        gug[1, :, at] = g1.T
        return carry

    lax.fori_loop(0, count, one_block, 0)


def load_mlp(pieces, offs, size, w, sem):
    return [
        start_pieces([x.at[j] for x in pieces], offs, size, w.at[j], sem.at[j], 1) for j in range(3)
    ]


def feed_far(n_pieces, size, refs):
    offs, n_in, c_in, pieces = refs[0], refs[1:3], refs[3:5], refs[5 : 5 + n_pieces]
    refs = refs[5 + n_pieces :]
    grads, outs, (hid, gug) = refs[0:2], refs[2:4], refs[4:6]
    n, c, grad, out, w, sem_w, sem = refs[6:]
    loads = start_rows(n_in, n, sem, 0) + start_rows(c_in, c, sem, 2)
    for group in load_mlp(pieces, offs, size, w, sem_w):
        wait(group)
    wait(loads)
    feed_rows(n, c, w, grad, out, hid, gug, 2, n_in[0].shape[0])
    wait(stop_rows(grad, grads, sem, 0) + stop_rows(out, outs, sem, 2))


def pick_columns(ref, first, second, size):
    a = ref[:, pl.ds(pl.multiple_of(first * size, size), size)]
    b = ref[:, pl.ds(pl.multiple_of(second * size, size), size)]
    return jnp.concatenate([a, b], axis=1)


def mlp_grads(cols, first_block, n, c, hidden, grads, block_sums):
    group = hidden[0].shape[1]

    def one_block(k, carry):
        at = 2 * (first_block + k)
        rights = [pick_columns(x, cols[at], cols[at + 1], 128) for x in (n, c)]
        for j in range(3):
            left = hidden if j == 2 else [x.at[j] for x in grads]
            right = rights[1] if j == 2 else rights[0]
            total = mm(left[0][...], right[:group]) + mm(left[1][...], right[group:])
            block_sums[k, 0, j] = total[:, :128].astype(BF)
            block_sums[k, 1, j] = total[:, 128:].astype(BF)
        return carry

    lax.fori_loop(0, 2, one_block, 0)


def stop_blocks(block_sums, blocks, sem, at):
    return [start(block_sums.at[i // 2, i % 2], x, sem.at[at + i]) for i, x in enumerate(blocks)]


def start_rows(sources, target, sem, at):
    rows = sources[0].shape[0]
    return [start(x, target.at[pl.ds(i * rows, rows)], sem.at[at + i]) for i, x in enumerate(sources)]


def feed_near(n_pieces, size, refs):
    offs, cols, n_in, c_in, hid_far, gug_far = refs[0], refs[1], refs[2:6], refs[6:10], refs[10], refs[11]
    pieces = refs[12 : 12 + n_pieces]
    refs = refs[12 + n_pieces :]
    grads, outs, (hid, gug), blocks = refs[0:2], refs[2:4], refs[4:6], refs[6:10]
    n, c, hf, gf, grad, out, block_sums, w, sem_w, sem = refs[10:]
    loads = start_rows(n_in, n, sem, 0)
    groups = load_mlp(pieces, offs, size, w, sem_w)
    loads += start_rows(c_in, c, sem, 4)
    late = [start(hid_far, hf, sem.at[8]), start(gug_far, gf, sem.at[9])]
    for group in groups:
        wait(group)
    wait(loads)
    feed_rows(n, c, w, grad, out, hid, gug, 2, n_in[0].shape[0])
    wait(late)
    stores = stop_rows(grad, grads, sem, 0) + stop_rows(out, outs, sem, 2)
    mlp_grads(cols, 0, n, c, (hid, hf), (gug, gf), block_sums)
    wait(stores + stop_blocks(block_sums, blocks, sem, 4))


def feed_late(refs):
    cols, n_in, c_in = refs[0], refs[1:5], refs[5:9]
    sources, blocks = refs[9:13], refs[13:17]
    n, c, hn, hf, gn, gf, block_sums, sem = refs[17:]
    loads = start_rows(n_in, n, sem, 0)
    loads += [start(x, y, sem.at[8 + i]) for i, (x, y) in enumerate(zip(sources, (hn, hf, gn, gf)))]
    loads += start_rows(c_in, c, sem, 4)
    wait(loads)
    mlp_grads(cols, 2, n, c, (hn, hf), (gn, gf), block_sums)
    wait(stop_blocks(block_sums, blocks, sem, 0))


def norm_back(v, g):
    xhat, r = norm_stats(v)
    mean_g = jnp.mean(g, axis=-1, keepdims=True)
    mean_gx = jnp.mean(g * xhat, axis=-1, keepdims=True)
    return r * (g - mean_g - xhat * mean_gx), xhat


def middle_back(mid, cot, gain, sa, sb, sc, mg_ref, low_ref, gain_ref):
    got = sa[...].astype(F32) + sb[...].astype(F32) + sc[...].astype(F32)
    back, xhat = norm_back(mid[...], gain[...] * got)
    sums = jnp.sum(got * xhat, axis=0, keepdims=True)
    for i in range(8):
        gain_ref[pl.ds(i, 1), :] = sums[:, 128 * i : 128 * i + 128]
    mg = cot[...].astype(F32) + back
    mg_ref[...] = mg
    low_ref[...] = mg.astype(BF)


def attend_backward(n_pieces, piece_rows, scale, refs):
    cols, mine, offs, gain, gain_two = refs[:5]
    refs = refs[5:]
    grads_in, mixed_in, q_in, k_in, v_in, lse_in, table, norms = (
        refs[0:4], refs[4], refs[5], refs[6], refs[7], refs[8], refs[9], refs[10:14]
    )
    pieces = refs[14 : 14 + n_pieces]
    refs = refs[14 + n_pieces :]
    outs, parts, gain_ref = refs[0:8], refs[8:12], refs[12]
    pg, do, o, q, k, v, lse, tab, n, a, dot_rows, dq, w, block_sums, sent, sem_w, sem = refs[13:]
    rows = grads_in[0].shape[0]
    length, width = q.shape
    heads = width // HD
    weights = start_pieces(pieces, offs, piece_rows, w, sem_w, 1)
    grads = start_rows(grads_in, a, sem, 0)
    pairs = ((mixed_in, o), (q_in, q), (k_in, k), (v_in, v), (lse_in, lse))
    near = [start(x, y, sem.at[4 + i]) for i, (x, y) in enumerate(pairs)]
    late = [start(table, tab, sem.at[12])]
    late += start_rows(norms, n, sem, 13)
    wait(weights)
    wait(grads)
    wait(near)
    lane = lax.broadcasted_iota(jnp.int32, (8, width), 1) >> 6
    head = lax.broadcasted_iota(jnp.int32, (8, width), 0)
    ones = jnp.where(lane == head, 1.0, 0.0).astype(BF)

    def output_grads(i, carry):
        at = pl.ds(pl.multiple_of(i * rows, rows), rows)
        d = mm(a[at, :], w[3]).astype(BF)
        do[at, :] = d
        t = d.astype(F32) * o[at, :].astype(F32)
        hi = t.astype(BF)
        lo = (t - hi.astype(F32)).astype(BF)
        dot_rows[:, at] = mm(ones, hi, NT) + mm(ones, lo, NT)
        return carry

    lax.fori_loop(0, 4, output_grads, 0, unroll=2)
    dq[...] = jnp.zeros_like(dq)
    factor = scale * LOG2E
    nil = jnp.zeros((), BF)

    def one_block(i, carry):
        at = pl.ds(pl.multiple_of(i * rows, rows), rows)
        dk_acc = jnp.zeros((rows, width), F32)
        dv_acc = jnp.zeros((rows, width), F32)
        dq_acc = None
        for h in range(heads):
            mask = head_mask((length, width), h)
            qm = jnp.where(mask, q[...], nil)
            dom = jnp.where(mask, do[...], nil)
            km = jnp.where(head_mask((rows, width), h), k[at, :], nil)
            s = mm(k[at, :], qm, NT)
            dp = mm(v[at, :], dom, NT)
            p = jnp.exp2(s * factor - lse[pl.ds(h, 1), :])
            ds = (p * (dp - dot_rows[pl.ds(h, 1), :])).astype(BF)
            dv_acc = dv_acc + mm(p.astype(BF), dom)
            dk_acc = dk_acc + mm(ds, qm)
            part = mm(ds, km, TN)
            dq_acc = part if dq_acc is None else dq_acc + part
        dq[...] += dq_acc
        cos, sin = angles_at(tab, mine[0] ^ i, rows)
        for g in range(width // 128):
            col = slice(g * 128, g * 128 + 128)
            to = slice(width + g * 128, width + g * 128 + 128)
            pg[at, to] = turn(dk_acc[:, col] * scale, cos, -sin).astype(BF)
        pg[at, 2 * width :] = dv_acc.astype(BF)
        return carry

    wait(late[:1])
    lax.fori_loop(0, 4, one_block, 0)

    def query_grads(i, carry):
        at = pl.ds(pl.multiple_of(i * rows, rows), rows)
        cos, sin = angles_at(tab, mine[0] ^ i, rows)
        for g in range(width // 128):
            col = slice(g * 128, g * 128 + 128)
            pg[at, col] = turn(dq[at, col] * scale, cos, -sin).astype(BF)
        return carry

    lax.fori_loop(0, 4, query_grads, 0)
    wait(late[1:])

    def weight_grads(block, carry):
        first, second = cols[2 * block], cols[2 * block + 1]
        total = mm(pick_columns(n, first, second, 128), pg[...], TN)
        last = mm(pick_columns(a, first, second, 128), o[...], TN)
        for j in range(4):
            part = last if j == 3 else total[:, j * width : (j + 1) * width]
            part = part.astype(BF)
            block_sums[block, 0, j] = part[:128]
            block_sums[block, 1, j] = part[128:]
        return carry

    lax.fori_loop(0, 4, weight_grads, 0, unroll=True)
    stores = stop_blocks(block_sums, outs, sem, 0)

    def row_grads(i, sums):
        at = pl.ds(pl.multiple_of(i * rows, rows), rows)
        total = sum(mm(pg[at, j * width : (j + 1) * width], w[j], NT) for j in range(3))
        sent[at, :] = total.astype(BF)
        return sums + jnp.sum(total * n[at, :].astype(F32), axis=0, keepdims=True)

    sums = lax.fori_loop(0, 4, row_grads, jnp.zeros((1, n.shape[1]), F32), unroll=2)
    sums = sums / gain[...]
    both = [sums[:, 128 * i : 128 * i + 128] for i in range(8)] + [gain_two[...]]
    gain_ref[...] = write_gains(sent, length, jnp.concatenate(both, axis=0))
    ends = [rows] * 3 + [rows + 16]
    for i in range(4):
        stores.append(start(sent.at[pl.ds(i * rows, ends[i])], parts[i], sem.at[8 + i]))
    wait(stores)


def write_gains(ref, rows, gains):
    high = gains.astype(BF)
    low = (gains - high.astype(F32)).astype(BF)
    tail = pl.ds(rows, 16)
    ref[tail, :] = jnp.zeros((16, ref.shape[1]), BF)
    ref[tail, 0:128] = high
    ref[tail, 128:256] = low
    return high.astype(F32) + low.astype(F32)


def read_gains(ref, rows):
    tail = pl.ds(rows, 16)
    return ref[tail, 0:128].astype(F32) + ref[tail, 128:256].astype(F32)


def add_far(part, got, gains, o_ref, gains_ref):
    rows = part.shape[0]
    o_ref[pl.ds(0, rows), :] = (part[...].astype(F32) + got[pl.ds(0, rows), :].astype(F32)).astype(BF)
    gains_ref[...] = write_gains(o_ref, rows, gains[...] + read_gains(got, rows))


def input_back(h, mg, gain, sa, sb, sc, o_ref):
    got = sa[...].astype(F32) + sb[...].astype(F32) + sc[pl.ds(0, sa.shape[0]), :].astype(F32)
    back, _ = norm_back(h[...].astype(F32), gain[...] * got)
    o_ref[...] = mg[...] + back


def body(function, *static):
    return lambda *refs: function(*static, refs)


def angle_table(length):
    exponents = np.arange(0, HD, 2).astype(np.float32) / np.float32(HD)
    inverse = np.float32(ROPE_BASE) ** (-exponents)
    angles = np.arange(length).astype(np.float32)[:, None] * inverse[None, :]
    cos, sin = np.cos(angles), np.sin(angles)
    half = length // 2
    return np.concatenate([cos[:half], sin[:half], cos[half:], sin[half:]], axis=1).astype(np.float32)


def shards(sizes, *args):
    hidden_in, attn_gain, qkv_weight, out_weight, mlp_gain, in_weight, down_weight, cotangent = args
    dp, tp = sizes
    rows, model = hidden_in.shape
    length = rows * tp
    piece_rows = qkv_weight.shape[1]
    width = qkv_weight.shape[2]
    units = in_weight.shape[2]
    scale = HD ** (-0.5)
    direct = dp == 8
    mine_one = lax.axis_index("tensor").astype(jnp.int32).reshape(1)
    place = lax.axis_index("dp")
    gain_one, gain_two = attn_gain.reshape(1, model), mlp_gain.reshape(1, model)

    def tensor(value, k, label):
        return swap(value, "tensor", tp, k, f"{label}_t{k}")

    def depth(value, k, label):
        return swap(value, "dp", dp, k, f"{label}_d{k}")

    def gather(shard, axis, label):
        if direct:
            far = depth(shard, 4, label)
            along = [shard, depth(shard, 2, label), far, depth(far, 2, label + "far")]
            across = [depth(v, 1, f"{label}{i}") for i, v in enumerate(along[:3])]
            across.append(depth(gate(along[3:], across[1:2])[0], 1, label + "3"))
            return [v for pair in zip(along, across) for v in pair]
        return [lax.all_gather(shard, "dp", axis=axis, tiled=True)]

    def only_direct(values):
        return values if direct else []

    if direct:
        offs = place ^ jnp.arange(8, dtype=jnp.int32)
        n_pieces, piece = 8, piece_rows
        z, y = place // 2, place % 2
        order = [1, 3, 2, 0]
        cols = jnp.stack([c for b in order for c in ((z ^ b) * 2 + (1 - y), (z ^ b) * 2 + y)])
    else:
        offs = jnp.zeros((1,), jnp.int32)
        n_pieces, piece = 1, model
        cols = jnp.arange(8, dtype=jnp.int32)
    cols = cols.astype(jnp.int32)
    sems = lambda *s: pltpu.SemaphoreType.DMA(s)
    add = lambda a, b: (a.astype(F32) + b.astype(F32)).astype(BF)

    def spread(own, label):
        far = tensor(own, 2, label)
        return [own, tensor(own, 1, label), far, tensor(far, 1, label + "far")]

    def exchange(blocks, label):
        return [blocks[0]] + [tensor(blocks[k], k, label) for k in (1, 2, 3)]

    def reduce(blocks, axis, label):
        whole = jnp.concatenate(blocks, axis=axis)
        return lax.psum_scatter(whole, "dp", scatter_dimension=axis, tiled=True).astype(F32)

    def sum_of(*values):
        return sum(v.astype(F32) for v in values)

    near = lambda *xs: [(x, vmem()) for x in xs]
    away = lambda xs: [(x, hbm()) for x in xs]
    scalar = lambda *xs: [(x, smem()) for x in xs]
    vm = lambda shape, dtype=BF: (shape, dtype, vmem())
    hb = lambda shape, dtype=BF: (shape, dtype, hbm())
    buf = lambda *shape, dtype=BF: pltpu.VMEM(shape, dtype)

    shard, mlp_shard = call(
        pack_body,
        near(qkv_weight, out_weight, in_weight.transpose(0, 2, 1), down_weight),
        [vm((4, piece_rows, width)), vm((3, units, piece_rows))],
        name="pack",
    )
    qkvo = gather(shard, 1, "qkvo")
    (normed,) = call(norm_body, near(hidden_in, gain_one), [vm((rows, model))], name="norm")
    if direct:
        (normed,) = gate([normed], [qkvo[1], qkvo[2], qkvo[4]])
    normed_attn = spread(normed, "norm")
    table = jnp.asarray(angle_table(length))
    if direct:
        (mlp_along,) = gate([mlp_shard], [qkvo[6]])
        (mlp_across,) = gate([mlp_shard], [qkvo[5], qkvo[7]])
        z2, z1 = [depth(mlp_along, 2 * k, "mlp") for k in (2, 1)]
        (cotangent_there,) = gate([cotangent], [normed_attn[2]])
    else:
        cotangent_there = cotangent
    cot = spread(cotangent_there, "cot")
    if direct:
        before = []
    else:
        mlp, before = gather(mlp_shard, 2, "mlp"), []
    *parts, mixed, q, k, v, lse = call(
        body(attend_forward, n_pieces, piece, scale),
        scalar(offs, mine_one)
        + away(gate(normed_attn, [z1]) if direct else normed_attn)
        + away([table] + qkvo),
        [hb((rows, model))] * 4 + [hb((length, width))] * 4 + [vm((8, length), F32)],
        [buf(4, rows, model), buf(length // 2, 128, dtype=F32), buf(4, model, width)]
        + [buf(length, width)] * 4
        + [buf(length, model), sems(n_pieces), sems(13)],
        name="attend_forward",
    )
    if direct:
        y0, y1 = depth(mlp_across, 1, "mlp0"), depth(gate([z1], [qkvo[5], qkvo[7]])[0], 1, "mlp1")
        *parts, lse = gate(parts + [lse], [z2, y0, y1, cot[2]])
    attn_far = add(parts[2], tensor(parts[3], 1, "afar"))
    attn_near = tensor(parts[1], 1, "anear")
    attn_got = tensor(attn_far, 2, "afar")
    if direct:
        z3 = depth(gate([z2], [lse])[0], 2, "mlpfar")
        y2, y3 = [depth(gate([x], [lse])[0], 1, f"mlp{i}") for i, x in ((2, z2), (3, z3))]
        before = [y2, z3]
        mlp = [mlp_shard, y0, z1, y1, z2, y2, z3, y3]
    middle, normed_two = call(
        middle_rows,
        near(hidden_in, gain_two, *gate([parts[0]], before), attn_near, attn_got),
        [vm((rows, model), F32), vm((rows, model))],
        name="middle_rows",
    )

    normed_far = tensor(normed_two, 2, "norm2")
    (normed_relay,) = gate([normed_far], only_direct(mlp[5:]))
    normed_mlp = [normed_two, tensor(normed_two, 1, "norm2"), normed_far, tensor(normed_relay, 1, "norm2far")]
    far_back, far_send, far_out, far_out_send, far_hidden, far_grad = call(
        body(feed_far, n_pieces, piece),
        scalar(offs) + away(normed_mlp[2:] + cot[2:] + mlp),
        [hb((rows, model))] * 4 + [vm((units, 2 * rows)), vm((2, units, 2 * rows))],
        [buf(2 * rows, model)] * 4 + [buf(3, units, model), sems(3, n_pieces), sems(4)],
        name="feed_far",
    )
    far_sum = add(far_back, tensor(far_send, 1, "far"))
    from_far = tensor(far_sum, 2, "far")
    near_back, near_send, near_out, near_out_send, near_hidden, near_grad, *grads = call(
        body(feed_near, n_pieces, piece),
        scalar(offs, cols)
        + away(gate(normed_mlp, [far_sum]) + cot + [far_hidden, far_grad] + mlp),
        [hb((rows, model))] * 4
        + [vm((units, 2 * rows)), vm((2, units, 2 * rows))]
        + [hb((3, units, 128))] * 4,
        [buf(length, model)] * 2
        + [buf(units, 2 * rows), buf(2, units, 2 * rows)]
        + [buf(2 * rows, model)] * 2
        + [buf(2, 2, 3, units, 128), buf(3, units, model), sems(3, n_pieces), sems(10)],
        name="feed_near",
    )
    near_got = tensor(near_send, 1, "near")
    out_sum = add(far_out, tensor(far_out_send, 1, "lofar"))
    out_near = tensor(near_out_send, 1, "lonear")

    middle_grad, low_grad, gain_two_part = call(
        middle_back,
        near(middle, cotangent, gain_two, near_back, near_got, from_far),
        [vm((rows, model), F32), vm((rows, model)), vm((8, 128), F32)],
        name="middle_back",
    )
    attn_out_grad = spread(low_grad, "aog")
    if direct:
        (grads[0],) = gate(grads[:1], [from_far])
        got = [depth(grads[0], 1, "gmlp0")]
        sums = [add(grads[1], got[0])]
        (grads[2],) = gate(grads[2:3], sums)
        before = [low_grad, sums[0], out_sum, out_near]
    else:
        before = [low_grad]
    grads += call(
        body(feed_late),
        scalar(cols)
        + away(gate(normed_mlp, before) + cot + [near_hidden, far_hidden, near_grad, far_grad]),
        [hb((3, units, 128))] * 4,
        [buf(length, model)] * 2
        + [buf(units, 2 * rows)] * 2
        + [buf(2, units, 2 * rows)] * 2
        + [buf(2, 2, 3, units, 128), sems(12)],
        name="feed_late",
    )
    early = [grads[7]]
    if direct:
        grads[4], grads[6] = gate([grads[4], grads[6]], [attn_out_grad[2]])
        got += [depth(grads[2 * i], 1, f"gmlp{i}") for i in (1, 2, 3)]
        sums.append(add(grads[3], got[1]))
        back = [depth(sums[i], 2, f"gmlpz{i}") for i in range(2)]
        early.append(sums[1])

    *attn, b0, b1, b2, b3, gains = call(
        body(attend_backward, n_pieces, piece, scale),
        scalar(cols, mine_one, offs)
        + near(gain_one, gain_two_part)
        + away(gate(attn_out_grad, early) + [mixed, q, k, v, lse, table] + normed_attn + qkvo),
        [hb((4, 128, width))] * 8
        + [hb((rows, model))] * 3
        + [hb((rows + 16, model)), vm((16, 128), F32)],
        [buf(length, 3 * width)]
        + [buf(length, width)] * 5
        + [buf(8, length, dtype=F32), buf(length // 2, 128, dtype=F32), buf(length, model), buf(length, model)]
        + [buf(8, length, dtype=F32), buf(length, width, dtype=F32)]
        + [buf(4, model, width), buf(4, 2, 4, 128, width), buf(length + 16, model)]
        + [sems(n_pieces), sems(17)],
        name="attend_backward",
    )
    if direct:
        late = sum_of(gate([grads[5]], [b0])[0], got[2], back[1]).astype(BF)
        last = depth(late, 4, "gmlp")
        *attn, b3 = gate(attn + [b3], [late, back[0], got[3]])
        gqkv = [depth(attn[2 * i], 1, f"gqkv{i}") for i in range(3)]
        qkv_sums = [add(attn[2 * i + 1], gqkv[i]) for i in range(2)]
        qkv_back = [depth(qkv_sums[i], 2, f"gqkvz{i}") for i in range(2)]
    sent_far, gains = call(
        add_far,
        near(b2, tensor(b3, 1, "nfar"), gains),
        [vm((rows + 16, model)), vm((16, 128), F32)],
        name="add_far",
    )
    got_far = tensor(sent_far, 2, "nfar")
    (b1,) = gate([b1], [sent_far])
    near_sum = tensor(b1, 1, "nnear")
    gains = gains + (got_far[rows:, 0:128].astype(F32) + got_far[rows:, 128:256].astype(F32))
    if direct:
        gains = gains + depth(gains, 1, "gain")
        (b0,) = gate([b0], [last, gains])
    (input_grad,) = call(
        input_back,
        near(hidden_in, middle_grad, gain_one, b0, near_sum, got_far),
        [vm((rows, model), F32)],
        name="input_back",
    )
    out_far = tensor(gate([out_sum], [got_far])[0], 2, "lofar")
    out_near = near_out.astype(F32) + out_near.astype(F32)
    layer_out = (middle + (out_near + out_far.astype(F32))).astype(BF)

    if direct:
        (attn[6],) = gate(attn[6:7], [got_far])
        gains = gains + depth(gains, 2, "gain")
        gains = gains + depth(gains, 4, "gain")
        gqkv.append(depth(attn[6], 1, "gqkv3"))
        qkv_late = sum_of(attn[5], gqkv[2], qkv_back[1]).astype(BF)
        qkv_last = depth(qkv_late, 4, "gqkv")
        ends = [attn[7], gqkv[3], qkv_back[0], gate([qkv_last], [out_far, gains])[0]]
        qkv_shard = sum_of(*[x[0:3] for x in ends])
        out_shard = sum_of(*[x[3] for x in ends]).T
    else:
        gains = lax.psum(gains, "dp")
        attn_total = reduce(attn, 1, "gqkv")
        qkv_shard, out_shard = attn_total[0:3], attn_total[3].T
    gains = gains.reshape(2, model)

    if direct:
        ends = [grads[7], got[3], back[0], gate([last], [input_grad])[0]]
        in_shard = sum_of(*[x[0:2] for x in ends]).transpose(0, 2, 1)
        down_shard = sum_of(*[x[2] for x in ends])
    else:
        mlp_total = reduce(grads, 2, "gmlp")
        in_shard, down_shard = mlp_total[0:2].transpose(0, 2, 1), mlp_total[2]

    return (layer_out, input_grad, gains[0], qkv_shard, out_shard, gains[1], in_shard, down_shard)


def solution(mesh):
    sizes = (mesh.shape["dp"], mesh.shape["tensor"])
    return jax.shard_map(
        functools.partial(shards, sizes),
        mesh=mesh,
        in_specs=(
            P(("dp", "tensor"), None),
            P(),
            P(None, "dp", "tensor"),
            P("tensor", "dp"),
            P(),
            P(None, "dp", "tensor"),
            P("tensor", "dp"),
            P(("dp", "tensor"), None),
        ),
        out_specs=(
            P(("dp", "tensor"), None),
            P(("dp", "tensor"), None),
            P(),
            P(None, "dp", "tensor"),
            P("tensor", "dp"),
            P(),
            P(None, "dp", "tensor"),
            P("tensor", "dp"),
        ),
        check_vma=False,
    )
```
